32 devices in a mesh: seq: 2 (over x), fsdp: 16 (over z, y, core).
Axes of the slice: x: 2, y: 2, z: 4, core: 2. Of those that a mesh axis runs over, the one named last changes fastest.
Arguments:
- tokens: bfloat16 [16, 1024, 768], P('fsdp', 'seq'), may hold values from -8 to 8
- cotangent: bfloat16 [16, 1024, 768], P('fsdp', 'seq'), may hold values from -6 to 6
- routes: int32 [16, 1024, 2], P('fsdp', 'seq'), may hold values from 0 to 3, all different within a row; in each aligned block of 512 rows (0 to 511, 512 to 1023, ..., all dimensions but the last counted through in order) at most 384 rows name the same one
- gain_one: bfloat16 [768], P(('seq', 'fsdp')), may hold values from 0.25 to 1.75
- w_qkv: bfloat16 [768, 2304], P(('seq', 'fsdp')), may hold values from -0.21875 to 0.21875
- w_attn_out: bfloat16 [768, 768], P(('seq', 'fsdp')), may hold values from -1.75 to 1.75
- gain_two: bfloat16 [768], P(('seq', 'fsdp')), may hold values from 0.25 to 1.75
- router: bfloat16 [768, 4], P(('seq', 'fsdp')), may hold values from -0.1875 to 0.1875
- w_ffn_in: bfloat16 [768, 5, 4096], P(('seq', 'fsdp')), may hold values from -0.21875 to 0.21875
- w_ffn_out: bfloat16 [2048, 5, 768], P(('seq', 'fsdp')), may hold values from -0.125 to 0.125
Outputs:
- output: bfloat16 [16, 1024, 768], P('fsdp', 'seq')
- d_tokens: bfloat16 [16, 1024, 768], P('fsdp', 'seq')
- d_gain_one: float32 [768], P(('seq', 'fsdp'))
- d_w_qkv: float32 [768, 2304], P(('seq', 'fsdp'))
- d_w_attn_out: float32 [768, 768], P(('seq', 'fsdp'))
- d_gain_two: float32 [768], P(('seq', 'fsdp'))
- d_router: float32 [768, 4], P(('seq', 'fsdp'))
- d_w_ffn_in: float32 [768, 5, 4096], P(('seq', 'fsdp'))
- d_w_ffn_out: float32 [2048, 5, 768], P(('seq', 'fsdp'))
- stats: float32 [5], replicated
The draws below stay inside these ranges and needn't reach their ends.
Inputs may be any that keep to these rules, and one draw needn't show every extreme that they name: `routes`: each row names 2 different experts; the 512 rows of one device name no expert more than 384 times, and in some devices' rows one expert exactly 384 times.
All inputs are finite; a program needn't handle non-finite values.
Results may differ from the reference program's by a relative error of at most 0.014.
Values may be sent and summed in bfloat16 or wider, within the bound.
No kernel may reach another device: no remote copies, remote signals or barrier semaphores. Data moves between devices by JAX's collectives and lax.ppermute only.
A program may use at most 512 MiB of HBM per device.

```python
import math
import jax
import jax.numpy as jnp
import numpy as np
from jax import lax

D = 768
HEADS = 12
HEAD_DIM = 64
FF = 2048
EXPERTS = 4
TOP = 2
BLOCK = 256
SEQ_LEN = 1024
TOK_DEV = 512
CAP = 384
SEQS = 16
TOKENS = 16384
N_SEQ = 2


def draw_tokens(key, part):
    first_key, second_key = jax.random.split(jax.random.fold_in(key, 17), 2)
    seq_place = jnp.arange(SEQS, dtype=jnp.float32) / max(SEQS - 1, 1)
    tok_place = jnp.arange(SEQ_LEN, dtype=jnp.float32) / max(SEQ_LEN - 1, 1)
    rough = jnp.exp(0.3 * jax.random.normal(second_key, (SEQS, SEQ_LEN, 1), jnp.float32))
    scale = 0.6 * (3.0 ** seq_place)[:, None, None] * (1.5 ** tok_place)[None, :, None] * rough
    values = jax.random.normal(first_key, (SEQS, SEQ_LEN, D), jnp.float32) * scale
    return jnp.clip(values, -8.0, 8.0).astype(jnp.bfloat16)


def block_levels(own_key, shape, shards, least, top_value):
    loudness, own = 1.0, jax.random.fold_in(own_key, 6)
    for dim, parts in shards:
        steps = jnp.exp(jax.random.uniform(jax.random.fold_in(own, dim), (parts,), jnp.float32, least / len(shards), top_value / len(shards)))
        loudness = loudness * jnp.repeat(steps, shape[dim] // parts).reshape([-1 if axis == dim else 1 for axis in range(len(shape))])
    return loudness


def deal_out(rng, own, number, rows, count, top, reach, slope):
    sequence = jax.random.permutation(rng, count)
    crowded, usual = load_shares(count, rows * top, reach, slope, True), load_shares(count, rows * top, reach, slope, False)
    places = jnp.arange(count)

    def named(tallies, offset_by):
        used = int((tallies > 0).sum())
        fixed = max(1, used // 4)
        shifted = fixed + (places - fixed + offset_by * (used - fixed)) % max(1, count - fixed)
        return jnp.zeros((count,), jnp.int32).at[sequence[jnp.where(places < fixed, places, shifted)]].set(jnp.asarray(tallies, jnp.int32))

    tallies = jnp.where(number % 4 == 0, named(crowded, number // 4), named(usual, number - number // 4 - 1))
    mixed = jax.random.permutation(jax.random.fold_in(own, 3), count)
    giver, receiver = mixed[0:count // 2 * 2:2], mixed[1:count // 2 * 2:2]
    margin = jnp.minimum(tallies[giver] - 1, reach - tallies[receiver]) // 2
    margin = jnp.where((giver == sequence[0]) | (receiver == sequence[0]) | (tallies[receiver] == 0), 0, jnp.maximum(margin, 0))
    shifted = jax.random.randint(jax.random.fold_in(own, 4), (count // 2,), 0, 1 << 20) % (margin + 1)
    tallies = tallies.at[giver].add(-shifted).at[receiver].add(shifted)
    labels = jnp.searchsorted(jnp.cumsum(tallies), jnp.arange(rows * top), side="right").astype(jnp.int32)
    listing = labels.reshape(top, rows).T
    listing = listing[jax.random.permutation(jax.random.fold_in(own, 1), rows)]
    offset_by = jax.random.randint(jax.random.fold_in(own, 2), (rows, 1), 0, top)
    return jnp.take_along_axis(listing, (jnp.arange(top)[None, :] + offset_by) % top, axis=1)


def load_shares(count, total, limit, lean, full):
    portions = [(1 << 20) // math.isqrt(rank ** lean) + 1 for rank in range(1, count + 1)]
    largest = limit if full else min(limit, max(-(-total // count), total * portions[0] // sum(portions)))
    least = 1 if total - largest >= count - 1 else 0
    given, surplus = [largest] + [least] * (count - 1), total - largest - least * (count - 1)
    while surplus > 0:
        free = [i for i in range(1, count) if given[i] < largest] or [i for i in range(1, count) if given[i] < limit]
        whole, left = sum([portions[i] for i in free]), surplus
        for i in free:
            more = min(limit - given[i], max(1, left * portions[i] // whole), surplus)
            given[i] = given[i] + more
            surplus = surplus - more
    return np.array(given)


def bell_draw(key, extent, deviation, most, cuts=(), kind=jnp.bfloat16):
    level = block_levels(key, extent, cuts, -0.22, 0.18) if cuts else 1.0
    array = jax.random.normal(key, extent, jnp.float32) * deviation * level
    return jnp.minimum(jnp.maximum(array, -most), most).astype(kind)


def setup_inputs(seed: int = 0) -> dict:
    seeds = jax.random.split(jax.random.key(seed), 11)
    tokens = draw_tokens(jax.random.fold_in(seeds[10], 71), 0)
    cotangent = bell_draw(seeds[1], (SEQS, SEQ_LEN, D), 1.0, 6.0, ((0, 16), (1, 2)))
    routes_keys = jax.random.split(jax.random.fold_in(seeds[2], 1), SEQS * SEQ_LEN // TOK_DEV)
    routes_turns = jax.random.permutation(jax.random.fold_in(seeds[2], 3), SEQS * SEQ_LEN // TOK_DEV)
    routes = jax.vmap(lambda own, number: deal_out(jax.random.fold_in(seeds[2], 2), own, number, TOK_DEV, EXPERTS, TOP, CAP, 1))(routes_keys, routes_turns).reshape((SEQS, SEQ_LEN, TOP))
    gain_one = jnp.clip(1.0 + 0.15 * jax.random.normal(seeds[3], (D,), jnp.float32), 0.25, 1.75).astype(jnp.bfloat16)
    w_qkv = bell_draw(seeds[4], (D, 3 * D), D ** -0.5, 0.21875, ((0, 32),))
    w_attn_out = bell_draw(seeds[5], (D, D), (D // 64) ** -0.5, 1.75, ((0, 32),))
    gain_two = jnp.clip(1.0 + 0.15 * jax.random.normal(seeds[6], (D,), jnp.float32), 0.25, 1.75).astype(jnp.bfloat16)
    router = bell_draw(seeds[7], (D, EXPERTS), (D * 3 // 2) ** -0.5, 0.1875, ((0, 32),))
    w_ffn_in = bell_draw(seeds[8], (D, EXPERTS + 1, 2 * FF), D ** -0.5, 0.21875, ((0, 32),))
    w_ffn_out = bell_draw(seeds[9], (FF, EXPERTS + 1, D), FF ** -0.5, 0.125, ((0, 32),))
    return {"tokens": tokens, "cotangent": cotangent, "routes": routes, "gain_one": gain_one, "w_qkv": w_qkv, "w_attn_out": w_attn_out, "gain_two": gain_two, "router": router, "w_ffn_in": w_ffn_in, "w_ffn_out": w_ffn_out}


epsilon = 1e-05
HIGHEST = lax.Precision.HIGHEST

@jax.custom_vjp
def low(v):
    return lax.optimization_barrier(v.astype(jnp.bfloat16)).astype(jnp.float32)

@jax.custom_vjp
def low_back(v):
    return v

def low_keep(v):
    return (low(v), None)

def low_pass(kept, grad):
    return (grad,)

def back_keep(v):
    return (v, None)

def back_low(kept, grad):
    return (low(grad),)
low.defvjp(low_keep, low_pass)
low_back.defvjp(back_keep, back_low)

def normalize(rows_in):
    return rows_in * lax.rsqrt(lax.optimization_barrier(jnp.mean(rows_in * rows_in, axis=-1, keepdims=True)) + epsilon)

def swiglu(values):
    return jax.nn.silu(values[..., :FF]) * values[..., FF:]

def rope_tables(positions):
    halfdim = HEAD_DIM // 2
    inverse = 10000.0 ** (-2.0 * jnp.arange(halfdim, dtype=jnp.float32) / HEAD_DIM)
    angles = positions.astype(jnp.float32)[:, None] * inverse[None, :]
    return (jnp.cos(angles), jnp.sin(angles))

def rotate(values, cosine, sine):
    halfdim = HEAD_DIM // 2
    first_half = values[..., :halfdim]
    second_half = values[..., halfdim:]
    cos_wide = cosine[:, None, :]
    sin_wide = sine[:, None, :]
    return jnp.concatenate([first_half * cos_wide - second_half * sin_wide, second_half * cos_wide + first_half * sin_wide], axis=-1)

def attend_sequence(triple):
    query_rows, key_rows, value_rows = triple
    scores = low_back(jnp.einsum('qhd,khd->hqk', query_rows, key_rows, precision=HIGHEST))
    block_of = jnp.arange(SEQ_LEN) // BLOCK
    allowed = block_of[None, :] <= block_of[:, None]
    scores = jnp.where(allowed[None, :, :], scores, -1e+30)
    probs_full = jax.nn.softmax(scores, axis=-1)
    return jnp.einsum('hqk,khd->qhd', low(probs_full), value_rows, precision=HIGHEST)

def mixture(normed_rows, route, router, w_ffn_in, w_ffn_out):
    logits = jnp.dot(normed_rows, router, precision=HIGHEST)
    chosen = jnp.take_along_axis(logits, route, axis=1)
    gate_vals = jax.nn.softmax(chosen, axis=1)
    flat_routes = route.reshape(-1).astype(jnp.int32)
    onehot = (flat_routes[:, None] == jnp.arange(EXPERTS, dtype=jnp.int32)[None, :]).astype(jnp.int32)
    before = jnp.cumsum(onehot, axis=0) - onehot
    slot_index = lax.optimization_barrier(jnp.sum(before * onehot, axis=1)).astype(jnp.int32)
    buffer_index = (flat_routes * CAP + slot_index).astype(jnp.int32)
    spread_rows = jnp.repeat(normed_rows, TOP, axis=0)
    buffered = jnp.zeros((EXPERTS * CAP, D), normed_rows.dtype).at[buffer_index].add(spread_rows)
    buffered = buffered.reshape(EXPERTS, CAP, D)
    shared_pre = low_back(jnp.dot(normed_rows, w_ffn_in[:, EXPERTS, :], precision=HIGHEST))
    shared_hid = low(swiglu(shared_pre))
    shared_out = low_back(jnp.dot(shared_hid, w_ffn_out[:, EXPERTS, :], precision=HIGHEST))
    expert_pre = low_back(jnp.einsum('ecd,def->ecf', buffered, w_ffn_in[:, :EXPERTS, :], precision=HIGHEST))
    expert_hid = low(swiglu(expert_pre))
    expert_out = low_back(jnp.einsum('ecf,fed->ecd', expert_hid, w_ffn_out[:, :EXPERTS, :], precision=HIGHEST))
    picked = expert_out.reshape(EXPERTS * CAP, D)[buffer_index].reshape(TOK_DEV, TOP, D)
    return shared_out + lax.optimization_barrier(jnp.sum(gate_vals[:, :, None] * picked, axis=1))

def layer(tokens, gain_one, w_qkv, w_attn_out, gain_two, router, w_ffn_in, w_ffn_out, routes):
    rows_in = tokens.reshape(TOKENS, D)
    normed_one = low(normalize(rows_in) * gain_one)
    joined = low_back(jnp.dot(normed_one, w_qkv, precision=HIGHEST))
    joined = joined.reshape(SEQS, SEQ_LEN, 3, HEADS, HEAD_DIM)
    cosine, sine = rope_tables(jnp.arange(SEQ_LEN))
    query_rows = low(rotate(joined[:, :, 0], cosine, sine) * 0.125)
    key_rows = low(rotate(joined[:, :, 1], cosine, sine))
    value_rows = low(joined[:, :, 2])
    attended = lax.map(jax.checkpoint(attend_sequence), (query_rows, key_rows, value_rows))
    mixed_heads = low(low_back(attended.reshape(TOKENS, D)))
    attn_out = low_back(jnp.dot(mixed_heads, w_attn_out, precision=HIGHEST))
    middle = rows_in + attn_out
    normed_two = low(normalize(middle) * gain_two)
    device_rows = normed_two.reshape(SEQS * N_SEQ, TOK_DEV, D)
    device_routes = routes.reshape(SEQS * N_SEQ, TOK_DEV, TOP)
    checked = jax.checkpoint(mixture)

    def one_device(pair):
        return checked(pair[0], pair[1], router, w_ffn_in, w_ffn_out)
    ffn_out = lax.map(one_device, (device_rows, device_routes)).reshape(TOKENS, D)
    output = middle + ffn_out
    stats = jnp.stack([jnp.sqrt(jnp.mean(rows_in * rows_in)), jnp.sqrt(jnp.mean(attn_out * attn_out)), jnp.sqrt(jnp.mean(middle * middle)), jnp.sqrt(jnp.mean(ffn_out * ffn_out)), jnp.sqrt(jnp.mean(output * output))])
    return (output, stats)

def reference(tokens, cotangent, routes, gain_one, w_qkv, w_attn_out, gain_two, router, w_ffn_in, w_ffn_out):
    primals = (tokens.astype(jnp.float32), gain_one.astype(jnp.float32), w_qkv.astype(jnp.float32), w_attn_out.astype(jnp.float32), gain_two.astype(jnp.float32), router.astype(jnp.float32), w_ffn_in.astype(jnp.float32), w_ffn_out.astype(jnp.float32))

    def forward(tok_in, gain_a, weight_a, weight_b, gain_b, router_in, weight_c, weight_d):
        return layer(tok_in, gain_a, weight_a, weight_b, gain_b, router_in, weight_c, weight_d, routes)
    output, pull_back, stats = jax.vjp(forward, *primals, has_aux=True)
    grads = pull_back(cotangent.astype(jnp.float32).reshape(TOKENS, D))
    return (output.reshape(SEQS, SEQ_LEN, D).astype(jnp.bfloat16), grads[0].reshape(SEQS, SEQ_LEN, D).astype(jnp.bfloat16), grads[1], grads[2], grads[3], grads[4], grads[5], grads[6], grads[7], stats)
```

```python
import jax
import jax.numpy as jnp
from jax import lax
from jax.experimental import pallas as pl
from jax.experimental.pallas import tpu as pltpu
from jax.sharding import Mesh, PartitionSpec as P

D = 768
HEAD_DIM = 64
FF = 2048
EXPERTS = 4
BRANCHES = EXPERTS + 1
TOP = 2
BLOCK = 256
LANES = 128

epsilon = 1e-05
f32 = jnp.float32
bf16 = jnp.bfloat16
ALL = ("x", "z", "y", "c")
PLANE = ("x", "y", "c")


def swap(v, axis, bit=0):
    n = lax.axis_size(axis)
    return lax.ppermute(v, axis, [(i, i ^ (1 << bit)) for i in range(n)])


def own_bit(axis, bit=0):
    return (lax.axis_index(axis) >> bit) & 1


def all_bits():
    names = []
    for axis in ALL:
        width = lax.axis_size(axis).bit_length() - 1
        names += [(axis, bit) for bit in reversed(range(width))]
    return names


def gather_bits(v, order):
    for axis, bit in order:
        other = swap(v, axis, bit)
        low = own_bit(axis, bit) == 0
        v = jnp.where(low, jnp.stack([v, other]), jnp.stack([other, v]))
    held = list(reversed(order))
    wanted = [name for name in all_bits() if name in held]
    lead = [held.index(name) for name in wanted]
    return v.transpose(lead + list(range(len(lead), v.ndim)))


def reduce_bits(v, names, order):
    names = list(names)
    for axis, bit in order:
        at = names.index((axis, bit))
        mine = own_bit(axis, bit)
        kept = lax.dynamic_index_in_dim(v, mine, at, keepdims=False)
        sent = lax.dynamic_index_in_dim(v, 1 - mine, at, keepdims=False).astype(bf16)
        v = kept.astype(f32) + swap(sent, axis, bit).astype(f32)
        names.pop(at)
    return v


def split_order(first, second):
    z = [name for name in all_bits() if name[0] == "z"]
    return z[::-1] + [(first, 0), (second, 0), ("c", 0)]


def gather_rows(v):
    rows, columns = v.shape
    half = (columns // 2 + LANES - 1) // LANES * LANES
    parts = [
        gather_bits(v[:, :half], split_order("x", "y")),
        gather_bits(v[:, half:], split_order("y", "x")),
    ]
    return jnp.concatenate([part.reshape(-1, part.shape[-1]) for part in parts], axis=1)


def scatter_rows(v, rows):
    columns = v.shape[1]
    half = (columns // 2 + LANES - 1) // LANES * LANES
    names = all_bits()
    parts = []
    for piece, order in (
        (v[:, :half], split_order("x", "y")),
        (v[:, half:], split_order("y", "x")),
    ):
        piece = piece.reshape((2,) * len(names) + (rows, piece.shape[1]))
        parts.append(reduce_bits(piece, names, order[::-1]))
    return jnp.concatenate(parts, axis=1)


def plane_blocks(v):
    rows = v.shape[0] // 2
    across_x = swap(v, "x")
    across_y = swap(v, "y")
    corner = jnp.concatenate([swap(across_x[:rows], "y"), swap(across_y[rows:], "x")])
    return [jnp.concatenate([block, swap(block, "c")]) for block in (v, across_x, across_y, corner)]


def plane_sums(own, across_x, across_y, corner):
    def on_chip(block):
        rows = block.shape[0] // 2
        return block[:rows] + swap(block[rows:].astype(bf16), "c").astype(f32)

    own, across_x, across_y, corner = [on_chip(b) for b in (own, across_x, across_y, corner)]
    rows = own.shape[0] // 2
    top = swap(corner[:rows].astype(bf16), "x").astype(f32)
    low = swap(corner[rows:].astype(bf16), "y").astype(f32)
    for_y = jnp.concatenate([across_y[:rows] + top, across_y[rows:]])
    for_x = jnp.concatenate([across_x[:rows], across_x[rows:] + low])
    return own + swap(for_x.astype(bf16), "x").astype(f32) + swap(for_y.astype(bf16), "y").astype(f32)


def sum_all(v):
    for axis, bit in reversed(all_bits()):
        v = v + swap(v, axis, bit)
    return v


def contract(a, b, dims):
    return lax.dot_general(a, b, (dims, ((), ())), preferred_element_type=f32)


def ffn_body(x_ref, g_ref, r_ref, win_ref, wout_ref, rt_ref, *refs):
    out_ref, gx_ref, h_ref, p_ref, xs_ref, gs_ref = refs[-6:]
    units = wout_ref.shape[1]
    x, g = x_ref[...], g_ref[...]
    router = rt_ref[...]
    logits = contract(x, router, ((1,), (0,)))
    lane = lax.broadcasted_iota(jnp.int32, logits.shape, 1)
    first, second = lane == r_ref[:, 0:1], lane == r_ref[:, 1:2]
    one = jnp.sum(jnp.where(first, logits, 0.0), axis=1, keepdims=True)
    two = jnp.sum(jnp.where(second, logits, 0.0), axis=1, keepdims=True)
    top = jnp.maximum(one, two)
    one, two = jnp.exp(one - top), jnp.exp(two - top)
    total = one + two
    gates = jnp.where(first, one / total, 0.0) + jnp.where(second, two / total, 0.0)
    grad_gates = jnp.zeros_like(logits)
    for e in range(BRANCHES):
        pre = contract(x, win_ref[:, e * 2 * units : (e + 1) * 2 * units], ((1,), (0,)))
        a, b = pre[:, :units], pre[:, units:]
        s = 1.0 / (1.0 + jnp.exp(-a))
        silu = a * s
        hidden = (silu * b).astype(bf16)
        back = contract(g, wout_ref[e], ((1,), (1,)))
        if e < EXPERTS:
            gate = gates[:, e : e + 1]
            hidden = hidden.astype(f32)
            own = jnp.sum(hidden * back, axis=1, keepdims=True)
            grad_gates = jnp.where(lane == e, own, grad_gates)
            hidden = (gate * hidden).astype(bf16)
            back = gate * back
        h_ref[:, e * units : (e + 1) * units] = hidden
        at = e * 2 * units
        p_ref[:, at : at + units] = (back * b * (s * (1.0 + a * (1.0 - s)))).astype(bf16)
        p_ref[:, at + units : at + 2 * units] = (back * silu).astype(bf16)
    inner = jnp.sum(gates * grad_gates, axis=1, keepdims=True)
    p_ref[:, BRANCHES * 2 * units :] = (gates * (grad_gates - inner)).astype(bf16)
    wide = BRANCHES * units
    out_ref[...] = contract(h_ref[...], wout_ref[...].reshape(wide, D), ((1,), (0,)))
    gx_ref[...] = contract(p_ref[:, : 2 * wide], win_ref[...], ((1,), (1,))) + contract(
        p_ref[:, 2 * wide :], router, ((1,), (1,))
    )
    xs_ref[...] = x
    gs_ref[...] = g


def ffn_call(part, parts, x, g, route, w_in, w_out, router, held):
    rows = x.shape[0]
    tile = min(512, rows)
    steps = rows // tile
    units = w_out.shape[1]
    wide = BRANCHES * units
    all_rows = parts * rows
    here = lambda i: (i, 0)
    there = lambda i: (part * steps + i, 0)
    whole = lambda shape: pl.BlockSpec(shape, lambda i: (0,) * len(shape))
    kept = [
        jax.ShapeDtypeStruct((all_rows, wide), bf16),
        jax.ShapeDtypeStruct((all_rows, 2 * wide + LANES), bf16),
        jax.ShapeDtypeStruct((all_rows, D), bf16),
        jax.ShapeDtypeStruct((all_rows, D), bf16),
    ]
    flops = 2 * rows * D * wide * 6
    outs = pl.pallas_call(
        ffn_body,
        grid=(steps,),
        in_specs=[
            pl.BlockSpec((tile, D), here),
            pl.BlockSpec((tile, D), here),
            pl.BlockSpec((tile, TOP), here),
            whole(w_in.shape),
            whole(w_out.shape),
            whole(router.shape),
        ]
        + [pl.BlockSpec(memory_space=pl.ANY)] * len(held),
        out_specs=[pl.BlockSpec((tile, D), here)] * 2
        + [pl.BlockSpec((tile, k.shape[1]), there) for k in kept],
        out_shape=[jax.ShapeDtypeStruct((rows, D), f32)] * 2 + kept,
        input_output_aliases={6 + i: 2 + i for i in range(len(held))},
        compiler_params=pltpu.CompilerParams(vmem_limit_bytes=56 * 2**20),
        cost_estimate=pl.CostEstimate(
            flops=flops,
            transcendentals=rows * wide,
            bytes_accessed=2 * (w_in.size + w_out.size) + rows * (4 * D + 2 * D * 4 + 6 * wide),
        ),
        name="ffn",
    )(x, g, route, w_in, w_out, router, *held)
    return outs[0], outs[1], outs[2:]


def normalize(rows_in):
    return rows_in * lax.rsqrt(jnp.mean(rows_in * rows_in, axis=-1, keepdims=True) + epsilon)


def rope_tables(positions):
    halfdim = HEAD_DIM // 2
    inverse = 10000.0 ** (-2.0 * jnp.arange(halfdim, dtype=f32) / HEAD_DIM)
    angles = positions.astype(f32)[:, None] * inverse[None, :]
    return (jnp.cos(angles), jnp.sin(angles))


def rotate(values, cosine, sine):
    halfdim = HEAD_DIM // 2
    first_half = values[..., :halfdim]
    second_half = values[..., halfdim:]
    cos_wide = cosine[:, None, :]
    sin_wide = sine[:, None, :]
    return jnp.concatenate(
        [
            first_half * cos_wide - second_half * sin_wide,
            second_half * cos_wide + first_half * sin_wide,
        ],
        axis=-1,
    )


def dot(a, b):
    return jnp.dot(a, b, preferred_element_type=f32)


def on_device(
    tokens, cotangent, routes, gain_one, w_qkv, w_attn_out, gain_two, router, w_ffn_in, w_ffn_out
):
    rows_dev = tokens.shape[1]
    heads = D // HEAD_DIM
    group_size = lax.axis_size(ALL)
    depth = lax.axis_size("z")
    own_rows = w_qkv.shape[0]
    units_own = w_ffn_out.shape[0]
    units = depth * units_own
    low_tokens = tokens.reshape(rows_dev, D)
    low_grad = cotangent.reshape(rows_dev, D)
    rows_in = low_tokens.astype(f32)
    grad_out = low_grad.astype(f32)

    small = jnp.concatenate([gain_one[:, None], gain_two[:, None], router], axis=1)
    small = jnp.pad(small, ((0, 0), (0, LANES - small.shape[1])))
    qkv_full = gather_rows(jnp.concatenate([w_qkv, small], axis=1))
    w_qkv_full = qkv_full[:, : 3 * D]
    gain_one_full = qkv_full[:, 3 * D].astype(f32)
    gain_two_full = qkv_full[:, 3 * D + 1].astype(f32)
    router_full = jnp.pad(
        qkv_full[:, 3 * D + 2 : 3 * D + 2 + EXPERTS], ((0, 0), (0, LANES - EXPERTS))
    )
    w_out_full = gather_rows(w_attn_out)
    before = lax.ppermute(low_tokens, "x", [(i, i + 1) for i in range(lax.axis_size("x") - 1)])

    cut = w_ffn_in.reshape(own_rows, BRANCHES, 2, 2, depth, 2, 2, units_own)
    cut = cut.transpose(3, 5, 6, 0, 1, 2, 4, 7).reshape(8, own_rows, BRANCHES * 2 * units)
    cut = lax.all_to_all(cut, PLANE, split_axis=0, concat_axis=0, tiled=True)
    w_in_mine = lax.all_gather(
        cut.reshape(2, 4 * own_rows, BRANCHES * 2 * units), "z", axis=1, tiled=True
    ).reshape(D, BRANCHES * 2 * units)
    w_out_mine = lax.all_gather(w_ffn_out.transpose(1, 0, 2), "z", axis=1, tiled=True)

    grad_blocks = plane_blocks(low_grad)
    route = routes.reshape(rows_dev, TOP)
    route_blocks = plane_blocks(route)

    hat_one = normalize(jnp.concatenate([before, low_tokens]).astype(f32))
    normed_one = (hat_one * gain_one_full).astype(bf16)
    query_raw = dot(normed_one[rows_dev:], w_qkv_full[:, :D])
    other_raw = dot(normed_one, w_qkv_full[:, D:])
    seq_index = lax.axis_index("x")
    positions = seq_index * rows_dev + jnp.arange(rows_dev, dtype=jnp.int32)
    key_pos = jnp.concatenate([positions - rows_dev, positions])
    cos_q, sin_q = rope_tables(positions)
    cos_k, sin_k = rope_tables(key_pos)

    def rope_query(raw):
        return rotate(raw, cos_q, sin_q) * 0.125

    def rope_key(raw):
        return rotate(raw, cos_k, sin_k)

    query_pre, query_back = jax.vjp(rope_query, query_raw.reshape(rows_dev, heads, HEAD_DIM))
    key_pre, key_back = jax.vjp(rope_key, other_raw[:, :D].reshape(2 * rows_dev, heads, HEAD_DIM))
    query_rows, key_rows = query_pre.astype(bf16), key_pre.astype(bf16)
    value_rows = other_raw[:, D:].astype(bf16).reshape(2 * rows_dev, heads, HEAD_DIM)
    usable = jnp.logical_or(jnp.arange(2 * rows_dev) >= rows_dev, seq_index > 0)
    allowed = jnp.logical_and(
        (key_pos // BLOCK)[None, :] <= (positions // BLOCK)[:, None], usable[None, :]
    )
    scores = jnp.einsum("qhd,khd->hqk", query_rows, key_rows, preferred_element_type=f32)
    scores = jnp.where(allowed[None], scores, -1e30)
    row_max = jnp.max(scores, axis=-1, keepdims=True)
    log_total = row_max + jnp.log(jnp.sum(jnp.exp(scores - row_max), axis=-1, keepdims=True))
    probs = jnp.exp(scores - log_total)
    probs_low = probs.astype(bf16)
    mixed = jnp.einsum("hqk,khd->qhd", probs_low, value_rows, preferred_element_type=f32)
    mixed = mixed.reshape(rows_dev, D).astype(bf16)
    attn_out = dot(mixed, w_out_full)
    middle = rows_in + attn_out
    hat_two = normalize(middle)
    normed_two = (hat_two * gain_two_full).astype(bf16)

    blocks = plane_blocks(normed_two)
    held = ()
    outs, grads = [None] * 4, [None] * 4
    for part, which in enumerate((0, 1, 3, 2)):
        outs[which], grads[which], held = ffn_call(
            part, 4, blocks[which], grad_blocks[which], route_blocks[which],
            w_in_mine, w_out_mine, router_full, held,
        )
    hidden_all, pre_all, x_all, g_all = held
    grad_rows = plane_sums(*grads)
    ffn_out = plane_sums(*outs)
    output = middle + ffn_out
    d_in = contract(x_all, pre_all, ((0,), (0,)))
    d_router_part = d_in[:, BRANCHES * 2 * units : BRANCHES * 2 * units + EXPERTS]
    d_in = d_in[:, : BRANCHES * 2 * units].astype(bf16).reshape(2, D // 2, BRANCHES * 2 * units)
    d_in = lax.psum_scatter(d_in, "z", scatter_dimension=1, tiled=True)
    d_in = d_in.reshape(8, own_rows, BRANCHES * 2 * units)
    d_in = lax.all_to_all(d_in, PLANE, split_axis=0, concat_axis=0, tiled=True)
    d_in = d_in.reshape(2, 2, 2, own_rows, BRANCHES, 2, depth, units_own).astype(f32)
    d_w_ffn_in = d_in.transpose(3, 4, 5, 0, 6, 1, 2, 7).reshape(own_rows, BRANCHES, 2 * FF)
    d_hid = contract(hidden_all, g_all, ((0,), (0,))).astype(bf16).reshape(BRANCHES, units, D)
    d_w_ffn_out = lax.psum_scatter(d_hid, "z", scatter_dimension=1, tiled=True)
    d_w_ffn_out = d_w_ffn_out.transpose(1, 0, 2).astype(f32)

    d_gain_two_part = jnp.sum(grad_rows * hat_two, axis=0)
    _, norm_two_back = jax.vjp(normalize, middle)
    grad_middle = grad_out + norm_two_back(grad_rows * gain_two_full)[0]
    grad_attn = grad_middle.astype(bf16)
    d_w_attn_out = scatter_rows(contract(mixed, grad_attn, ((0,), (0,))), own_rows)

    grad_mixed = contract(grad_attn, w_out_full, ((1,), (1,))).astype(bf16)
    grad_mixed = grad_mixed.reshape(rows_dev, heads, HEAD_DIM)
    grad_probs = jnp.einsum("qhd,khd->hqk", grad_mixed, value_rows, preferred_element_type=f32)
    inner = jnp.sum(probs * grad_probs, axis=-1, keepdims=True)
    grad_scores = (probs * (grad_probs - inner)).astype(bf16)
    grad_query = jnp.einsum("hqk,khd->qhd", grad_scores, key_rows, preferred_element_type=f32)
    grad_keys = jnp.einsum("hqk,qhd->khd", grad_scores, query_rows, preferred_element_type=f32)
    grad_values = jnp.einsum("hqk,qhd->khd", probs_low, grad_mixed, preferred_element_type=f32)
    grad_q = query_back(grad_query)[0].reshape(rows_dev, D).astype(bf16)
    grad_kv = jnp.concatenate(
        [key_back(grad_keys)[0].reshape(2 * rows_dev, D), grad_values.reshape(2 * rows_dev, D)],
        axis=1,
    ).astype(bf16)
    grad_one = contract(grad_kv, w_qkv_full[:, D:], ((1,), (1,)))
    grad_one_prev, grad_one_own = grad_one[:rows_dev], grad_one[rows_dev:]
    back = lax.ppermute(
        grad_one_prev.astype(bf16), "x", [(i + 1, i) for i in range(lax.axis_size("x") - 1)]
    )
    grad_one_own = grad_one_own + contract(grad_q, w_qkv_full[:, :D], ((1,), (1,)))
    d_gain_one_part = jnp.sum(grad_one_own * hat_one[rows_dev:], axis=0) + jnp.sum(
        grad_one_prev * hat_one[:rows_dev], axis=0
    )
    d_qkv = jnp.concatenate(
        [
            contract(normed_one[rows_dev:], grad_q, ((0,), (0,))),
            contract(normed_one, grad_kv, ((0,), (0,))),
            jnp.pad(
                jnp.concatenate(
                    [d_gain_one_part[:, None], d_gain_two_part[:, None], d_router_part], axis=1
                ),
                ((0, 0), (0, LANES - 2 - EXPERTS)),
            ),
        ],
        axis=1,
    )
    d_qkv = scatter_rows(d_qkv, own_rows)
    grad_one_own = grad_one_own + back.astype(f32)
    _, norm_one_back = jax.vjp(normalize, rows_in)
    grad_tokens = grad_middle + norm_one_back(grad_one_own * gain_one_full)[0]
    partial_sums = jnp.stack(
        [jnp.sum(v * v) for v in (rows_in, attn_out, middle, ffn_out, output)]
    )
    stats = jnp.sqrt(sum_all(partial_sums) / (rows_dev * group_size * D))
    return (
        output.reshape(tokens.shape).astype(bf16),
        grad_tokens.reshape(tokens.shape).astype(bf16),
        d_qkv[:, 3 * D],
        d_qkv[:, : 3 * D],
        d_w_attn_out,
        d_qkv[:, 3 * D + 1],
        d_qkv[:, 3 * D + 2 : 3 * D + 2 + EXPERTS],
        d_w_ffn_in,
        d_w_ffn_out,
        stats,
    )


def solution(mesh):
    seq, fsdp = mesh.shape["seq"], mesh.shape["fsdp"]
    inner = Mesh(mesh.devices.reshape(seq, fsdp // 4, 2, 2), ALL)
    data = P(("z", "y", "c"), "x", None)
    in_specs = (data, data, data) + tuple(P(ALL, *(None,) * k) for k in (0, 1, 1, 0, 1, 2, 2))
    out_specs = (
        (data, data) + tuple(P(ALL, *(None,) * k) for k in (0, 1, 1, 0, 1, 2, 2)) + (P(),)
    )
    return jax.shard_map(
        on_device, mesh=inner, in_specs=in_specs, out_specs=out_specs, check_vma=False
    )
```

```python
import functools

import jax
import jax.numpy as jnp
from jax import lax
from jax.experimental import pallas as pl
from jax.experimental.pallas import tpu as pltpu
from jax.sharding import Mesh, PartitionSpec as P

D = 768
HEAD_DIM = 64
FF = 2048
EXPERTS = 4
BRANCHES = EXPERTS + 1
TOP = 2
BLOCK = 256
LANES = 128
GROUP = 256
GROUPS = D // GROUP

epsilon = 1e-05
f32 = jnp.float32
bf16 = jnp.bfloat16
ALL = ("x", "z", "y", "c")
PLANE = ("x", "y", "c")


def swap(v, axis, bit=0):
    n = lax.axis_size(axis)
    return lax.ppermute(v, axis, [(i, i ^ (1 << bit)) for i in range(n)])


def own_bit(axis, bit=0):
    return (lax.axis_index(axis) >> bit) & 1


def all_bits():
    names = []
    for axis in ALL:
        width = lax.axis_size(axis).bit_length() - 1
        names += [(axis, bit) for bit in reversed(range(width))]
    return names


def gather_bit(v, name):
    other = swap(v, *name)
    low = own_bit(*name) == 0
    return jnp.where(low, jnp.stack([v, other]), jnp.stack([other, v]))


def in_order(v, order):
    held = list(reversed(order))
    lead = [held.index(name) for name in all_bits()]
    v = v.transpose(lead + list(range(len(lead), v.ndim)))
    return v.reshape(-1, v.shape[-1])


def gather_rows(v, half):
    z = [name for name in all_bits() if name[0] == "z"][::-1]
    for name in z:
        v = gather_bit(v, name)
    parts = []
    for part, first, second in ((v[..., :half], "x", "y"), (v[..., half:], "y", "x")):
        order = z + [(first, 0), (second, 0), ("c", 0)]
        for name in order[len(z) :]:
            part = gather_bit(part, name)
        parts.append(in_order(part, order))
    return parts


def scatter_rows(v, rows, first, second):
    names = all_bits()
    order = [("c", 0), (first, 0), (second, 0)] + [name for name in names if name[0] == "z"]
    v = v.reshape((2,) * len(names) + (rows, v.shape[1]))
    for name in order:
        at = names.index(name)
        mine = own_bit(*name)
        kept = lax.dynamic_index_in_dim(v, mine, at, keepdims=False)
        sent = lax.dynamic_index_in_dim(v, 1 - mine, at, keepdims=False).astype(bf16)
        v = kept.astype(f32) + swap(sent, *name).astype(f32)
        names.pop(at)
    return v


def plane_blocks(v):
    rows = v.shape[0] // 2
    across_x = swap(v, "x")
    across_y = swap(v, "y")
    corner = jnp.concatenate([swap(across_x[:rows], "y"), swap(across_y[rows:], "x")])
    return [(block, swap(block, "c")) for block in (v, across_x, across_y, corner)]


def plane_sums(own, across_x, across_y, corner):
    def on_chip(pair):
        return pair[0] + swap(pair[1], "c").astype(f32)

    corner = on_chip(corner)
    rows = corner.shape[0] // 2
    top = swap(corner[:rows].astype(bf16), "x").astype(f32)
    low = swap(corner[rows:].astype(bf16), "y").astype(f32)
    across_x, across_y = on_chip(across_x), on_chip(across_y)
    for_y = jnp.concatenate([across_y[:rows] + top, across_y[rows:]]).astype(bf16)
    for_x = jnp.concatenate([across_x[:rows], across_x[rows:] + low]).astype(bf16)
    return on_chip(own) + swap(for_x, "x").astype(f32) + swap(for_y, "y").astype(f32)


def sum_all(v):
    for name in reversed(all_bits()):
        v = v + swap(v, *name)
    return v


def contract(a, b, dims):
    return lax.dot_general(a, b, (dims, ((), ())), preferred_element_type=f32)


def whole(shape):
    return pl.BlockSpec(shape, lambda *i: (0,) * len(shape))


def shapes(*pairs):
    return [jax.ShapeDtypeStruct(shape, kind) for shape, kind in pairs]


def params(mib):
    return pltpu.CompilerParams(vmem_limit_bytes=mib * 2**20)


def cost(flops, moved, exps=0):
    return pl.CostEstimate(flops=flops, transcendentals=exps, bytes_accessed=moved)


def sigmoid(a):
    return 0.5 * jnp.tanh(0.5 * a) + 0.5


def ffn_up_body(xa_ref, xb_ref, ga_ref, gb_ref, win_ref, rt_ref, *refs):
    pre_ref, h_ref, gate_ref, xs_ref, gs_ref = refs[-5:]
    units = h_ref.shape[1] // BRANCHES
    own = pl.program_id(0) == 0
    x = jnp.where(own, xa_ref[...], xb_ref[...])
    g = jnp.where(own, ga_ref[...], gb_ref[...])
    xs_ref[...] = x
    gs_ref[...] = g[:, :D]
    route = g[:, D:].astype(f32).astype(jnp.int32)
    logits = contract(x, rt_ref[...], ((1,), (0,)))
    lane = lax.broadcasted_iota(jnp.int32, logits.shape, 1)
    first, second = lane == route[:, 0:1], lane == route[:, 1:2]
    one = jnp.sum(jnp.where(first, logits, 0.0), axis=1, keepdims=True)
    two = jnp.sum(jnp.where(second, logits, 0.0), axis=1, keepdims=True)
    top = jnp.maximum(one, two)
    one, two = jnp.exp(one - top), jnp.exp(two - top)
    total = one + two
    gates = jnp.where(first, one / total, 0.0) + jnp.where(second, two / total, 0.0)
    gate_ref[...] = gates
    for e in range(BRANCHES):
        at = e * 2 * units
        pre = contract(x, win_ref[:, at : at + 2 * units], ((1,), (0,)))
        pre_ref[:, at : at + 2 * units] = pre
        a, b = pre[:, :units], pre[:, units:]
        hidden = (a * sigmoid(a) * b).astype(bf16)
        if e < EXPERTS:
            hidden = (gates[:, e : e + 1] * hidden.astype(f32)).astype(bf16)
        h_ref[:, e * units : (e + 1) * units] = hidden


def ffn_down_body(
    ga_ref, gb_ref, pre_ref, h_ref, gate_ref, win_ref, wout_ref, rt_ref, *refs
):
    gxa_ref, gxb_ref, outa_ref, outb_ref, p_ref = refs[-5:]
    units = wout_ref.shape[1]
    wide = BRANCHES * units
    own = pl.program_id(0) == 0
    g = jnp.where(own, ga_ref[...], gb_ref[...])
    gates = gate_ref[...]
    lane = lax.broadcasted_iota(jnp.int32, gates.shape, 1)
    grad_gates = jnp.zeros_like(gates)
    for e in range(BRANCHES):
        at = e * 2 * units
        a = pre_ref[:, at : at + units]
        b = pre_ref[:, at + units : at + 2 * units]
        back = contract(g, wout_ref[e], ((1,), (1,)))
        s = sigmoid(a)
        silu = a * s
        if e < EXPERTS:
            hidden = (silu * b).astype(bf16).astype(f32)
            this = jnp.sum(hidden * back, axis=1, keepdims=True)
            grad_gates = jnp.where(lane == e, this, grad_gates)
            back = gates[:, e : e + 1] * back
        p_ref[:, at : at + units] = (back * b * (s + silu * (1.0 - s))).astype(bf16)
        p_ref[:, at + units : at + 2 * units] = (back * silu).astype(bf16)
    inner = jnp.sum(gates * grad_gates, axis=1, keepdims=True)
    p_ref[:, 2 * wide :] = (gates * (grad_gates - inner)).astype(bf16)
    out = contract(h_ref[...], wout_ref[...].reshape(wide, D), ((1,), (0,)))
    gx = contract(p_ref[:, : 2 * wide], win_ref[...], ((1,), (1,))) + contract(
        p_ref[:, 2 * wide :], rt_ref[...], ((1,), (1,))
    )

    @pl.when(own)
    def _():
        gxa_ref[...] = gx
        outa_ref[...] = out

    @pl.when(jnp.logical_not(own))
    def _():
        gxb_ref[...] = gx.astype(bf16)
        outb_ref[...] = out.astype(bf16)


def ffn_up(part, parts, x, g, w_in, router, held):
    rows = x[0].shape[0]
    wide = w_in.shape[1]
    total = parts * 2 * rows
    kept = shapes(
        ((total, wide), f32),
        ((total, wide // 2), bf16),
        ((total, LANES), f32),
        ((total, D), bf16),
        ((total, D), bf16),
    )
    row_spec = lambda width: pl.BlockSpec((rows, width), lambda i: (2 * part + i, 0))
    return pl.pallas_call(
        ffn_up_body,
        grid=(2,),
        in_specs=[whole(v.shape) for v in (*x, *g, w_in, router)]
        + [pl.BlockSpec(memory_space=pl.ANY)] * len(held),
        out_specs=[row_spec(k.shape[1]) for k in kept],
        out_shape=kept,
        input_output_aliases={6 + i: i for i in range(len(held))},
        compiler_params=params(56),
        cost_estimate=cost(
            4 * rows * D * wide, 2 * w_in.size + rows * (8 * D + 10 * wide), rows * wide
        ),
        name="ffn_up",
    )(*x, *g, w_in, router, *held)


def ffn_down(part, parts, g, pre, hidden, gates, w_in, w_out, router, held):
    rows = g[0].shape[0]
    wide = w_in.shape[1]
    total = parts * 2 * rows
    row_spec = lambda width: pl.BlockSpec((rows, width), lambda i: (2 * part + i, 0))
    outs = pl.pallas_call(
        ffn_down_body,
        grid=(2,),
        in_specs=[whole((rows, D)), whole((rows, D))]
        + [row_spec(v.shape[1]) for v in (pre, hidden, gates)]
        + [whole(v.shape) for v in (w_in, w_out, router)]
        + [pl.BlockSpec(memory_space=pl.ANY)] * len(held),
        out_specs=[whole((rows, D))] * 4 + [row_spec(wide + LANES)],
        out_shape=shapes(
            ((rows, D), f32),
            ((rows, D), bf16),
            ((rows, D), f32),
            ((rows, D), bf16),
            ((total, wide + LANES), bf16),
        ),
        input_output_aliases={8 + i: 4 + i for i in range(len(held))},
        compiler_params=params(58),
        cost_estimate=cost(8 * rows * D * wide, 3 * w_in.size + rows * (20 * D + 14 * wide)),
        name="ffn_down",
    )(*g, pre, hidden, gates, w_in, w_out, router, *held)
    return outs[0:2], outs[2:4], outs[4:]


def half_turn(v):
    lane = lax.broadcasted_iota(jnp.int32, v.shape, 1)
    low = lane % HEAD_DIM < HEAD_DIM // 2
    return jnp.where(low, pltpu.roll(v, 128 - HEAD_DIM // 2, 1), pltpu.roll(v, HEAD_DIM // 2, 1))


def rope(v, cosine, sine):
    parts = [v[:, at : at + LANES] for at in range(0, v.shape[1], LANES)]
    return jnp.concatenate([p * cosine + half_turn(p) * sine for p in parts], axis=1)


def one_head(v, j):
    lane = lax.broadcasted_iota(jnp.int32, v.shape, 1)
    return jnp.where(lane // HEAD_DIM == j, v, jnp.zeros_like(v))


def normal(rows_in):
    return rows_in * lax.rsqrt(jnp.mean(rows_in * rows_in, axis=-1, keepdims=True) + epsilon)


def row_of(column):
    return jnp.broadcast_to(column, (column.shape[0], LANES)).T[:8]


def attend_body(
    seq_ref, prev_ref, tok_ref, gains_ref, wq_ref, wk_ref, wv_ref, wo_ref, cos_ref, sin_ref,
    normed_ref, q_ref, k_ref, v_ref, mixed_ref, lse_ref, middle_ref, two_ref, sums_ref, acc_ref,
):
    step = pl.program_id(0)
    rows = tok_ref.shape[0]

    @pl.when(step == 0)
    def _():
        for at, ref in ((0, prev_ref), (rows, tok_ref)):
            hat = normal(ref[...].astype(f32))
            normed_ref[at : at + rows] = (hat * gains_ref[0:1]).astype(bf16)

    x = normed_ref[...]
    cosine, sine = cos_ref[...], sin_ref[...]
    own_cos, own_sin = cosine[rows:], sine[rows:]
    q = contract(x[rows:], wq_ref[...], ((1,), (0,)))
    q_ref[...] = (rope(q, own_cos, own_sin) * 0.125).astype(bf16)
    k_ref[...] = rope(contract(x, wk_ref[...], ((1,), (0,))), cosine, sine).astype(bf16)
    v_ref[...] = contract(x, wv_ref[...], ((1,), (0,))).astype(bf16)
    skip = jnp.where(seq_ref[0] > 0, 0.0, 1e30)
    for at in range(0, GROUP, LANES):
        cols = slice(at, at + LANES)
        for top in range(0, rows, BLOCK):
            mixed = jnp.zeros((BLOCK, LANES), f32)
            ends = rows + top + BLOCK
            for j in range(LANES // HEAD_DIM):
                query = one_head(q_ref[top : top + BLOCK, cols], j)
                far = contract(query, k_ref[:rows, cols], ((1,), (1,)))
                near = contract(query, k_ref[rows:ends, cols], ((1,), (1,)))
                peak = jnp.maximum(
                    jnp.max(far, axis=1, keepdims=True) - skip, jnp.max(near, axis=1, keepdims=True)
                )
                far, near = jnp.exp(far - (peak + skip)), jnp.exp(near - peak)
                total = jnp.sum(far, axis=1, keepdims=True) + jnp.sum(near, axis=1, keepdims=True)
                both = contract(far.astype(bf16), one_head(v_ref[:rows, cols], j), ((1,), (0,)))
                both += contract(near.astype(bf16), one_head(v_ref[rows:ends, cols], j), ((1,), (0,)))
                mixed += both / total
                head = (at // HEAD_DIM + j) * 8
                lse_ref[head : head + 8, top : top + BLOCK] = row_of(peak + jnp.log(total))
            mixed_ref[top : top + BLOCK, cols] = mixed.astype(bf16)
    piece = contract(mixed_ref[...], wo_ref[...], ((1,), (0,)))

    @pl.when(step == 0)
    def _():
        acc_ref[...] = piece

    @pl.when(step > 0)
    def _():
        acc_ref[...] += piece

    @pl.when(step == GROUPS - 1)
    def _():
        attn = acc_ref[...]
        tok = tok_ref[...].astype(f32)
        middle = tok + attn
        middle_ref[...] = middle
        two_ref[...] = (normal(middle) * gains_ref[1:2]).astype(bf16)
        for i, v in enumerate((tok, attn, middle)):
            sums_ref[i : i + 1] = jnp.sum(v * v, axis=0, keepdims=True)


def attend(seq, prev, tok, gains, w_qk, w_vo, cosine, sine):
    rows = tok.shape[0]
    heads = D // HEAD_DIM
    across = lambda n: pl.BlockSpec((n, GROUP), lambda i: (0, i))
    weight = lambda first: pl.BlockSpec((D, GROUP), lambda i: (0, first + i))
    return pl.pallas_call(
        attend_body,
        grid=(GROUPS,),
        in_specs=[
            pl.BlockSpec(memory_space=pltpu.SMEM),
            whole(prev.shape),
            whole(tok.shape),
            whole(gains.shape),
            weight(0),
            weight(GROUPS),
            weight(0),
            pl.BlockSpec((GROUP, D), lambda i: (i, 1)),
            whole(cosine.shape),
            whole(sine.shape),
        ],
        out_specs=[
            whole((2 * rows, D)),
            across(rows),
            across(2 * rows),
            across(2 * rows),
            across(rows),
            pl.BlockSpec((8 * heads // GROUPS, rows), lambda i: (i, 0)),
            whole((rows, D)),
            whole((rows, D)),
            whole((8, D)),
        ],
        out_shape=shapes(
            ((2 * rows, D), bf16),
            ((rows, D), bf16),
            ((2 * rows, D), bf16),
            ((2 * rows, D), bf16),
            ((rows, D), bf16),
            ((8 * heads, rows), f32),
            ((rows, D), f32),
            ((rows, D), bf16),
            ((8, D), f32),
        ),
        scratch_shapes=[pltpu.VMEM((rows, D), f32)],
        compiler_params=params(56),
        cost_estimate=cost(
            2 * rows * D * D * 6 + 8 * rows * rows * D, 8 * D * D + 20 * rows * D, heads * 2 * rows * rows
        ),
        name="attend",
    )(seq, prev, tok, gains, w_qk, w_qk, w_vo, w_vo, cosine, sine)


def attend_back_body(
    seq_ref, grad_ref, wo_ref, wq_ref, wk_ref, wv_ref, q_ref, k_ref, v_ref, mixed_ref, lse_ref,
    normed_ref, cos_ref, sin_ref, *refs,
):
    one_ref, d_ref, gq_ref, gk_ref, gv_ref, dqt_ref, dk_ref, dv_ref = refs[-8:]
    rows = grad_ref.shape[0]
    cosine, sine = cos_ref[...], sin_ref[...]
    skip = jnp.where(seq_ref[0] > 0, 0.0, 1e30)
    grad_mixed = contract(grad_ref[...], wo_ref[...], ((1,), (1,))).astype(bf16)
    for at in range(0, GROUP, LANES):
        cols = slice(at, at + LANES)
        key, value = k_ref[:, cols], v_ref[:, cols]
        key_t = key.T
        products = grad_mixed[:, cols].astype(f32) * mixed_ref[:, cols].astype(f32)
        for j in range(LANES // HEAD_DIM):
            head = (at // HEAD_DIM + j) * 8
            keep = lax.broadcasted_iota(jnp.int32, key_t.shape, 0) // HEAD_DIM == j
            key_j = jnp.where(keep, key_t, jnp.zeros_like(key_t))
            for top in range(0, rows, BLOCK):
                block = slice(top, top + BLOCK)
                query = one_head(q_ref[block, cols], j)
                grad = one_head(grad_mixed[block, cols], j)
                delta = row_of(
                    jnp.sum(one_head(products[block], j), axis=1, keepdims=True)
                )[0:1]
                lse = lse_ref[head : head + 1, block]
                for begin, end, less in ((0, rows, lse + skip), (rows, rows + top + BLOCK, lse)):
                    probs = jnp.exp(contract(key[begin:end], query, ((1,), (1,))) - less)
                    back = contract(value[begin:end], grad, ((1,), (1,))) - delta
                    scores = (probs * back).astype(bf16)
                    grad_v = contract(probs.astype(bf16), grad, ((1,), (0,)))
                    grad_k = contract(scores, query, ((1,), (0,)))
                    grad_q = contract(key_j[:, begin:end], scores, ((1,), (0,)))
                    if j == 0 and top == 0 and begin == 0:
                        dv_ref[begin:end], dk_ref[begin:end] = grad_v, grad_k
                    elif j == 0 and top == 0:
                        dv_ref[begin:end], dk_ref[begin:end] = grad_v, grad_k
                        if end < 2 * rows:
                            rest = jnp.zeros((2 * rows - end, LANES), f32)
                            dv_ref[end:], dk_ref[end:] = rest, rest
                    else:
                        dv_ref[begin:end] += grad_v
                        dk_ref[begin:end] += grad_k
                    if j == 0 and begin == 0:
                        dqt_ref[:, block] = grad_q
                    else:
                        dqt_ref[:, block] += grad_q
        own_cos, own_sin = cosine[rows:], sine[rows:]
        gq_ref[:, cols] = (rope(dqt_ref[...].T, own_cos, -own_sin) * 0.125).astype(bf16)
        gk_ref[:, cols] = rope(dk_ref[...], cosine, -sine).astype(bf16)
        gv_ref[:, cols] = dv_ref[...].astype(bf16)
    gq, gk, gv = gq_ref[...], gk_ref[...], gv_ref[...]
    one = contract(gk, wk_ref[...], ((1,), (1,))) + contract(gv, wv_ref[...], ((1,), (1,)))
    if len(refs) > 8:
        one += refs[0][...]
    one_ref[:rows] = one[:rows]
    one_ref[rows:] = one[rows:] + contract(gq, wq_ref[...], ((1,), (1,)))
    normed = normed_ref[...]
    d_ref[:, :GROUP] = contract(normed[:, rows:], gq, ((1,), (0,)))
    d_ref[:, GROUP : 2 * GROUP] = contract(normed, gk, ((1,), (0,)))
    d_ref[:, 2 * GROUP :] = contract(normed, gv, ((1,), (0,)))


def attend_back(i, seq, grad, w_qk, w_vo, q, k, v, mixed, lse, normed_t, cosine, sine, held):
    rows = grad.shape[0]
    heads = D // HEAD_DIM // GROUPS
    across = lambda n: pl.BlockSpec((n, GROUP), lambda _: (0, i))
    weight = lambda first: pl.BlockSpec((D, GROUP), lambda _: (0, first + i))
    return pl.pallas_call(
        attend_back_body,
        grid=(1,),
        in_specs=[
            pl.BlockSpec(memory_space=pltpu.SMEM),
            whole(grad.shape),
            pl.BlockSpec((GROUP, D), lambda _: (i, 1)),
            weight(0),
            weight(GROUPS),
            weight(0),
            across(rows),
            across(2 * rows),
            across(2 * rows),
            across(rows),
            pl.BlockSpec((8 * heads, rows), lambda _: (i, 0)),
            whole(normed_t.shape),
            whole(cosine.shape),
            whole(sine.shape),
        ]
        + [whole((2 * rows, D))] * len(held),
        out_specs=[whole((2 * rows, D)), whole((D, 3 * GROUP))],
        out_shape=shapes(((2 * rows, D), f32), ((D, 3 * GROUP), f32)),
        scratch_shapes=[
            pltpu.VMEM((rows, GROUP), bf16),
            pltpu.VMEM((2 * rows, GROUP), bf16),
            pltpu.VMEM((2 * rows, GROUP), bf16),
            pltpu.VMEM((LANES, rows), f32),
            pltpu.VMEM((2 * rows, LANES), f32),
            pltpu.VMEM((2 * rows, LANES), f32),
        ],
        compiler_params=params(56),
        cost_estimate=cost(
            2 * rows * D * GROUP * 11 + 20 * rows * rows * GROUP, 40 * rows * D, heads * 2 * rows * rows
        ),
        name="attend_back",
    )(seq, grad, w_vo, w_qk, w_qk, w_vo, q, k, v, mixed, lse, normed_t, cosine, sine, *held)


def rope_tables(positions):
    halfdim = HEAD_DIM // 2
    inverse = 10000.0 ** (-2.0 * jnp.arange(halfdim, dtype=f32) / HEAD_DIM)
    angles = positions.astype(f32)[:, None] * inverse[None, :]
    cosine, sine = jnp.cos(angles), jnp.sin(angles)
    times = LANES // HEAD_DIM
    return (
        jnp.tile(jnp.concatenate([cosine, cosine], axis=1), (1, times)),
        jnp.tile(jnp.concatenate([-sine, sine], axis=1), (1, times)),
    )


def on_device(
    tokens, cotangent, routes, gain_one, w_qkv, w_attn_out, gain_two, router, w_ffn_in, w_ffn_out
):
    rows = tokens.shape[1]
    depth = lax.axis_size("z")
    own_rows = w_qkv.shape[0]
    units_own = w_ffn_out.shape[0]
    units = depth * units_own
    wide = BRANCHES * 2 * units
    low_tokens = tokens.reshape(rows, D)
    low_grad = cotangent.reshape(rows, D)

    cut = w_ffn_in.reshape(own_rows, BRANCHES, 2, 2, depth, 2, 2, units_own)
    cut = cut.transpose(3, 5, 6, 0, 1, 2, 4, 7).reshape(8, own_rows, wide)
    cut = lax.all_to_all(cut, PLANE, split_axis=0, concat_axis=0, tiled=True)
    w_in_mine = lax.all_gather(
        cut.reshape(2, 4 * own_rows, wide), "z", axis=1, tiled=True
    ).reshape(D, wide)
    w_out_mine = lax.all_gather(w_ffn_out.transpose(1, 0, 2), "z", axis=1, tiled=True)

    small = jnp.concatenate([gain_one[:, None], gain_two[:, None], router], axis=1)
    small = jnp.pad(small, ((0, 0), (0, LANES - small.shape[1])))
    w_qk, w_vo = gather_rows(jnp.concatenate([w_qkv, w_attn_out, small], axis=1), 2 * D)
    gains = w_vo[:, 2 * D : 2 * D + 2].astype(f32).T
    router_full = jnp.pad(
        w_vo[:, 2 * D + 2 : 2 * D + 2 + EXPERTS], ((0, 0), (0, LANES - EXPERTS))
    )
    before = lax.ppermute(low_tokens, "x", [(i, i + 1) for i in range(lax.axis_size("x") - 1)])

    route = jnp.pad(routes.reshape(rows, TOP), ((0, 0), (0, LANES - TOP))).astype(bf16)
    grad_blocks = plane_blocks(jnp.concatenate([low_grad, route], axis=1))

    seq_index = lax.axis_index("x")
    positions = (seq_index - 1) * rows + jnp.arange(2 * rows, dtype=jnp.int32)
    cosine, sine = rope_tables(positions)
    seq = seq_index.astype(jnp.int32).reshape(1)
    normed_one, q, k, v, mixed, lse, middle, normed_two, sums = attend(
        seq, before, low_tokens, gains, w_qk, w_vo, cosine, sine
    )

    blocks = plane_blocks(normed_two)
    held = ()
    for which in range(4):
        held = ffn_up(which, 4, blocks[which], grad_blocks[which], w_in_mine, router_full, held)
    pre_all, hidden_all, gates_all, x_all, g_all = held
    d_hid = contract(hidden_all, g_all, ((0,), (0,))).astype(bf16).reshape(BRANCHES, units, D)
    d_w_ffn_out = lax.psum_scatter(d_hid, "z", scatter_dimension=1, tiled=True)
    d_w_ffn_out = d_w_ffn_out.transpose(1, 0, 2).astype(f32)
    held = ()
    outs, grads = [None] * 4, [None] * 4
    for which in (3, 1, 2, 0):
        grads[which], outs[which], held = ffn_down(
            which, 4, grad_blocks[which], pre_all, hidden_all, gates_all,
            w_in_mine, w_out_mine, router_full, held,
        )
    grad_rows = plane_sums(*grads)
    d_in = contract(x_all, held[0], ((0,), (0,)))
    d_router_part = d_in[:, wide : wide + EXPERTS]
    d_in = d_in[:, :wide].astype(bf16).reshape(2, D // 2, wide)
    d_in = lax.psum_scatter(d_in, "z", scatter_dimension=1, tiled=True)
    d_in = d_in.reshape(8, own_rows, wide)
    d_in = lax.all_to_all(d_in, PLANE, split_axis=0, concat_axis=0, tiled=True)
    d_in = d_in.reshape(2, 2, 2, own_rows, BRANCHES, 2, depth, units_own).astype(f32)
    d_w_ffn_in = d_in.transpose(3, 4, 5, 0, 6, 1, 2, 7).reshape(own_rows, BRANCHES, 2 * FF)

    hat_two = normal(middle)
    d_gain_two_part = jnp.sum(grad_rows * hat_two, axis=0)
    _, norm_two_back = jax.vjp(normal, middle)
    grad_middle = low_grad.astype(f32) + norm_two_back(grad_rows * gains[1:2])[0]
    grad_attn = grad_middle.astype(bf16)
    d_attn_out = contract(mixed, grad_attn, ((0,), (0,)))
    outs, grad_rows = lax.optimization_barrier((outs, grad_rows))
    ffn_out = plane_sums(*outs)
    output = middle + ffn_out

    held, parts = (), []
    normed_t = normed_one.T
    for i in range(GROUPS):
        one, part = attend_back(
            i, seq, grad_attn, w_qk, w_vo, q, k, v, mixed, lse, normed_t, cosine, sine, held
        )
        held = (one,)
        parts.append(part)
    back = lax.ppermute(
        one[:rows].astype(bf16), "x", [(i + 1, i) for i in range(lax.axis_size("x") - 1)]
    )
    rows_in = low_tokens.astype(f32)
    hat_one = normal(rows_in)
    d_gain_one_part = jnp.sum(one[rows:] * hat_one, axis=0) + jnp.sum(
        one[:rows] * normal(before.astype(f32)), axis=0
    )
    tail = jnp.concatenate(
        [d_gain_one_part[:, None], d_gain_two_part[:, None], d_router_part], axis=1
    )
    tail = jnp.pad(tail, ((0, 0), (0, LANES - tail.shape[1])))
    first = scatter_rows(jnp.concatenate([parts[0], d_attn_out], axis=1), own_rows, "x", "y")
    second = scatter_rows(parts[1], own_rows, "y", "x")
    third = scatter_rows(jnp.concatenate([parts[2], tail], axis=1), own_rows, "x", "y")
    d_w_qkv = jnp.concatenate(
        [
            piece[:, at : at + GROUP]
            for at in range(0, 3 * GROUP, GROUP)
            for piece in (first, second, third)
        ],
        axis=1,
    )
    d_w_attn_out = first[:, 3 * GROUP :]
    tail = third[:, 3 * GROUP :]
    _, norm_one_back = jax.vjp(normal, rows_in)
    grad_one = (one[rows:] + back.astype(f32)) * gains[0:1]
    grad_tokens = grad_middle + norm_one_back(grad_one)[0]
    partial_sums = jnp.concatenate(
        [jnp.sum(sums[:3], axis=1), jnp.stack([jnp.sum(u * u) for u in (ffn_out, output)])]
    )
    stats = jnp.sqrt(sum_all(partial_sums) / (rows * lax.axis_size(ALL) * D))
    return (
        output.reshape(tokens.shape).astype(bf16),
        grad_tokens.reshape(tokens.shape).astype(bf16),
        tail[:, 0],
        d_w_qkv,
        d_w_attn_out,
        tail[:, 1],
        tail[:, 2 : 2 + EXPERTS],
        d_w_ffn_in,
        d_w_ffn_out,
        stats,
    )


def solution(mesh):
    seq, fsdp = mesh.shape["seq"], mesh.shape["fsdp"]
    inner = Mesh(mesh.devices.reshape(seq, fsdp // 4, 2, 2), ALL)
    data = P(("z", "y", "c"), "x", None)
    weights = tuple(P(ALL, *(None,) * k) for k in (0, 1, 1, 0, 1, 2, 2))
    return jax.shard_map(
        on_device,
        mesh=inner,
        in_specs=(data, data, data) + weights,
        out_specs=(data, data) + weights + (P(),),
        check_vma=False,
    )
```

```python
import functools
import itertools
import math

import jax
import jax.numpy as jnp
from jax import lax
from jax.experimental import pallas as pl
from jax.experimental.pallas import tpu as pltpu
from jax.sharding import Mesh, PartitionSpec as P

D = 768
HEAD_DIM = 64
FF = 2048
EXPERTS = 4
BRANCHES = EXPERTS + 1
TOP = 2
BLOCK = 256
LANES = 128
GROUP = 256
GROUPS = D // GROUP

epsilon = 1e-05
f32 = jnp.float32
bf16 = jnp.bfloat16
ALL = ("x", "z", "y", "c")
PLANE = ("x", "y", "c")


def shuffle(v, axes, by):
    sizes = [lax.axis_size(axis) for axis in axes]
    pairs = []
    for at in range(math.prod(sizes)):
        rest, to, scale = at, 0, 1
        for size, flip in reversed(list(zip(sizes, by))):
            to += (rest % size ^ flip) * scale
            rest, scale = rest // size, scale * size
        pairs.append((at, to))
    return lax.ppermute(v, axes, pairs)


def swap(v, axis):
    return shuffle(v, (axis,), (1,))


def own_bit(axis, bit=0):
    return (lax.axis_index(axis) >> bit) & 1


def after(v, *deps):
    return lax.optimization_barrier((v, deps))[0]


def ordered(low, mine, other):
    return jnp.where(low, jnp.stack([mine, other]), jnp.stack([other, mine]))


def gather_axes(v, bits):
    axes = tuple(dict.fromkeys(axis for axis, _ in bits))

    def part(flips):
        by = [0] * len(axes)
        for (axis, bit), flip in zip(bits, flips):
            by[axes.index(axis)] |= flip << bit
        return shuffle(v, axes, by) if any(flips) else v

    def level(flips):
        if len(flips) == len(bits):
            return part(flips)
        low = own_bit(*bits[len(flips)]) == 0
        return ordered(low, level(flips + (0,)), level(flips + (1,)))

    return level(())


def z_bits():
    return [("z", bit) for bit in reversed(range(lax.axis_size("z").bit_length() - 1))]


def z_stages():
    bits = z_bits()
    return [bits] if len(bits) <= 2 else [[name] for name in bits]


def all_bits():
    return [("x", 0)] + z_bits() + [("y", 0), ("c", 0)]


def gather_rows(v, deps, more):
    held = []
    for bits in z_stages()[::-1] + [[("x", 0), ("y", 0)], [("c", 0)]]:
        if ("x", 0) in bits:
            v = after(v, deps)
        if ("c", 0) in bits:
            v = after(v, more)
        v = gather_axes(v, bits)
        held = bits + held
    lead = [held.index(name) for name in all_bits()]
    v = v.transpose(lead + list(range(len(lead), v.ndim)))
    return v.reshape(-1, v.shape[-1])


class Scatter:
    def __init__(self, v, rows, extra=None):
        self.names = all_bits()
        self.v = v.reshape((2,) * len(self.names) + (rows, v.shape[1]))
        self.extra = extra
        self.stages = [[("c", 0)], [("x", 0), ("y", 0)]] + z_stages()

    def block(self, flips, bits):
        v = self.v
        at = {self.names.index(name): own_bit(*name) ^ flip for name, flip in zip(bits, flips)}
        starts = [at.get(i, 0) for i in range(v.ndim)]
        sizes = [1 if i in at else v.shape[i] for i in range(v.ndim)]
        piece = lax.dynamic_slice(v, starts, sizes)
        return piece.reshape([n for i, n in enumerate(v.shape) if i not in at])

    def send(self):
        bits = self.stages[0]
        axes = tuple(dict.fromkeys(axis for axis, _ in bits))
        width = self.v.shape[-1]
        if self.extra is not None:
            count = self.extra.shape[0]
            coded, rest = [], self.extra
            for _ in range(3):
                coded.append(lax.reduce_precision(rest, 8, 7))
                rest = rest - coded[-1]
            spread = jnp.pad(jnp.concatenate(coded).astype(bf16), (width - 3 * count, 0))
            lane = jnp.arange(width) >= width - 3 * count
        moves = []
        for flips in itertools.product((0, 1), repeat=len(bits)):
            if not any(flips):
                continue
            by = [0] * len(axes)
            for (axis, bit), flip in zip(bits, flips):
                by[axes.index(axis)] |= flip << bit
            sent = self.block(flips, bits).astype(bf16)
            if self.extra is not None:
                sent = jnp.where(lane, spread, sent)
            moves.append(shuffle(sent, axes, by))
        return moves

    def take(self, moves):
        bits, self.stages = self.stages[0], self.stages[1:]
        total = self.block((0,) * len(bits), bits).astype(f32)
        for got in moves:
            got = got.astype(f32)
            total += got
            if self.extra is not None:
                count = self.extra.shape[0]
                parts = got.reshape(-1, got.shape[-1])[0, -3 * count :].reshape(3, count)
                self.extra = self.extra + (parts[0] + parts[1] + parts[2])
        self.v = total
        self.names = [name for name in self.names if name not in bits]

    def finish(self):
        while self.stages:
            self.take(self.send())


def on_chip(pair, more=None):
    v = pair[0] + swap(pair[1], "c").astype(f32)
    return v if more is None else v + more


def contract(a, b, dims):
    return lax.dot_general(a, b, (dims, ((), ())), preferred_element_type=f32)


def whole(shape):
    return pl.BlockSpec(shape, lambda *i: (0,) * len(shape))


def fixed(shape):
    return pl.BlockSpec(shape, lambda *i: (0,) * len(shape), pipeline_mode=pl.Buffered(1))


def shapes(*pairs):
    return [jax.ShapeDtypeStruct(shape, kind) for shape, kind in pairs]


def params(mib):
    return pltpu.CompilerParams(vmem_limit_bytes=mib * 2**20)


def cost(flops, moved, exps=0):
    return pl.CostEstimate(flops=flops, transcendentals=exps, bytes_accessed=moved)


def sigmoid(a):
    return 0.5 * jnp.tanh(0.5 * a) + 0.5


def ffn_body(branches, first, last, names, *refs):
    r = dict(zip(names, refs))
    win_ref, wout_ref, h_ref, p_ref = r["w_in"], r["w_out"], r["hidden"], r["pre"]
    units = wout_ref.shape[1]
    wide = len(branches) * units
    tile = h_ref.shape[0]
    step = pl.program_id(0)
    half = pl.num_programs(0) // 2
    own = step < half
    here = pl.ds(lax.rem(step, half) * tile, tile)
    x = jnp.where(own, r["xa"][here], r["xb"][here])
    g = jnp.where(own, r["ga"][here], r["gb"][here])
    lane = lax.broadcasted_iota(jnp.int32, (tile, LANES), 1)
    if first:
        r["xs"][...] = x
        r["gs"][...] = g[:, :D]
        route = g[:, D:].astype(f32).astype(jnp.int32)
        logits = contract(x, win_ref[:, 2 * wide :], ((1,), (0,)))
        one, two = lane == route[:, 0:1], lane == route[:, 1:2]
        up = jnp.sum(jnp.where(one, logits, 0.0), axis=1, keepdims=True)
        down = jnp.sum(jnp.where(two, logits, 0.0), axis=1, keepdims=True)
        top = jnp.maximum(up, down)
        up, down = jnp.exp(up - top), jnp.exp(down - top)
        total = up + down
        gates = jnp.where(one, up / total, 0.0) + jnp.where(two, down / total, 0.0)
        grad_gates = jnp.zeros_like(gates)
    else:
        gates, grad_gates = r["gates"][...], r["sums"][...]
    g = g[:, :D]
    for i, e in enumerate(branches):
        at = i * 2 * units
        pre = contract(x, win_ref[:, at : at + 2 * units], ((1,), (0,)))
        a, b = pre[:, :units], pre[:, units:]
        back = contract(g, wout_ref[i], ((1,), (1,)))
        s = sigmoid(a)
        silu = a * s
        hidden = (silu * b).astype(bf16)
        if e < EXPERTS:
            gate = gates[:, e : e + 1]
            hidden = hidden.astype(f32)
            this = jnp.sum(hidden * back, axis=1, keepdims=True)
            grad_gates = jnp.where(lane == e, this, grad_gates)
            hidden = (gate * hidden).astype(bf16)
            back = gate * back
        h_ref[:, i * units : (i + 1) * units] = hidden
        p_ref[:, at : at + units] = (back * b * (s + silu * (1.0 - s))).astype(bf16)
        p_ref[:, at + units : at + 2 * units] = (back * silu).astype(bf16)
        if last and e == EXPERTS - 1:
            inner = jnp.sum(gates * grad_gates, axis=1, keepdims=True)
            p_ref[:, 2 * wide :] = (gates * (grad_gates - inner)).astype(bf16)
    if not last:
        r["gates_out"][...] = gates
        r["sums_out"][...] = grad_gates
    tile_ref = r["tile"]
    deep = p_ref.shape[1]
    out = contract(h_ref[...], wout_ref[...].reshape(wide, D), ((1,), (0,)))
    tile_ref[:, D:] = out
    for at in range(0, D, GROUP):
        cols = slice(at, at + GROUP)
        tile_ref[:, cols] = contract(p_ref[...], win_ref[cols, :deep], ((1,), (1,)))

    @pl.when(own)
    def _():
        r["own"][here] = tile_ref[...]

    @pl.when(jnp.logical_not(own))
    def _():
        r["other"][here] = tile_ref[...].astype(bf16)


def ffn(part, parts, branches, x, g, w_in, w_out, kept, gating=None):
    first, last = gating is None, branches[-1] == BRANCHES - 1
    rows = x[0].shape[0]
    tile = min(256, rows)
    steps = rows // tile
    wide = w_in.shape[1] - LANES
    total = parts * 2 * rows
    here = lambda width: pl.BlockSpec((tile, width), lambda i: (i, 0))
    there = lambda width: pl.BlockSpec((tile, width), lambda i: (2 * part * steps + i, 0))
    ins = list(zip(("xa", "xb", "ga", "gb", "w_in", "w_out"), (*x, *g, w_in, w_out)))
    specs = [fixed(v.shape) for _, v in ins]
    if not first:
        ins += list(zip(("gates", "sums"), gating))
        specs += [here(LANES)] * 2
    outs = [("own", (rows, 2 * D), f32, whole((rows, 2 * D)))]
    outs += [("other", (rows, 2 * D), bf16, whole((rows, 2 * D)))]
    if not last:
        outs += [(n, (2 * rows, LANES), f32, here(LANES)) for n in ("gates_out", "sums_out")]
    at = len(outs)
    widths = [("hidden", wide // 2), ("pre", wide + last * LANES)]
    if first:
        widths += [("xs", D), ("gs", D)]
    outs += [(n, (total, width), bf16, there(width)) for n, width in widths]
    names = [n for n, _ in ins] + ["old"] * len(kept) + [n for n, *_ in outs] + ["tile"]
    results = pl.pallas_call(
        functools.partial(ffn_body, branches, first, last, names),
        grid=(2 * steps,),
        in_specs=specs + [pl.BlockSpec(memory_space=pl.ANY)] * len(kept),
        out_specs=[spec for *_, spec in outs],
        out_shape=shapes(*((shape, kind) for _, shape, kind, _ in outs)),
        scratch_shapes=[pltpu.VMEM((tile, 2 * D), f32)],
        input_output_aliases={len(ins) + i: at + i for i in range(len(kept))},
        compiler_params=params(40),
        cost_estimate=cost(
            12 * rows * D * wide, 3 * w_in.size + rows * (20 * D + 6 * wide), rows * wide
        ),
        name="ffn",
    )(*(v for _, v in ins), *kept)
    return results[:2], results[2:at], results[at:]


def half_turn(v):
    lane = lax.broadcasted_iota(jnp.int32, v.shape, 1)
    low = lane % HEAD_DIM < HEAD_DIM // 2
    return jnp.where(low, pltpu.roll(v, 128 - HEAD_DIM // 2, 1), pltpu.roll(v, HEAD_DIM // 2, 1))


def rope(v, cosine, sine):
    parts = [v[:, at : at + LANES] for at in range(0, v.shape[1], LANES)]
    return jnp.concatenate([p * cosine + half_turn(p) * sine for p in parts], axis=1)


def one_head(v, j):
    lane = lax.broadcasted_iota(jnp.int32, v.shape, 1)
    return jnp.where(lane // HEAD_DIM == j, v, jnp.zeros_like(v))


def normal(rows_in):
    return rows_in * lax.rsqrt(jnp.mean(rows_in * rows_in, axis=-1, keepdims=True) + epsilon)


def row_of(column):
    return jnp.broadcast_to(column, (column.shape[0], LANES)).T[:8]


def attend_body(
    seq_ref, prev_ref, tok_ref, gains_ref, wq_ref, wk_ref, wv_ref, wo_ref, cos_ref, sin_ref,
    normed_ref, q_ref, k_ref, v_ref, mixed_ref, lse_ref, middle_ref, two_ref, sums_ref, acc_ref,
):
    step = pl.program_id(0)
    rows = tok_ref.shape[0]

    @pl.when(step == 0)
    def _():
        for at, ref in ((0, prev_ref), (rows, tok_ref)):
            hat = normal(ref[...].astype(f32))
            normed_ref[at : at + rows] = (hat * gains_ref[0:1]).astype(bf16)

    x = normed_ref[...]
    cosine, sine = cos_ref[...], sin_ref[...]
    own_cos, own_sin = cosine[rows:], sine[rows:]
    q = contract(x[rows:], wq_ref[...], ((1,), (0,)))
    q_ref[...] = (rope(q, own_cos, own_sin) * 0.125).astype(bf16)
    k_ref[...] = rope(contract(x, wk_ref[...], ((1,), (0,))), cosine, sine).astype(bf16)
    v_ref[...] = contract(x, wv_ref[...], ((1,), (0,))).astype(bf16)
    skip = jnp.where(seq_ref[0] > 0, 0.0, 1e30)
    for at in range(0, GROUP, LANES):
        cols = slice(at, at + LANES)
        for top in range(0, rows, BLOCK):
            mixed = jnp.zeros((BLOCK, LANES), f32)
            ends = rows + top + BLOCK
            for j in range(LANES // HEAD_DIM):
                query = one_head(q_ref[top : top + BLOCK, cols], j)
                far = contract(query, k_ref[:rows, cols], ((1,), (1,)))
                near = contract(query, k_ref[rows:ends, cols], ((1,), (1,)))
                peak = jnp.maximum(
                    jnp.max(far, axis=1, keepdims=True) - skip, jnp.max(near, axis=1, keepdims=True)
                )
                far, near = jnp.exp(far - (peak + skip)), jnp.exp(near - peak)
                total = jnp.sum(far, axis=1, keepdims=True) + jnp.sum(near, axis=1, keepdims=True)
                both = contract(far.astype(bf16), one_head(v_ref[:rows, cols], j), ((1,), (0,)))
                both += contract(near.astype(bf16), one_head(v_ref[rows:ends, cols], j), ((1,), (0,)))
                mixed += both / total
                head = (at // HEAD_DIM + j) * 8
                lse_ref[head : head + 8, top : top + BLOCK] = row_of(peak + jnp.log(total))
            mixed_ref[top : top + BLOCK, cols] = mixed.astype(bf16)
    piece = contract(mixed_ref[...], wo_ref[...], ((1,), (0,)))

    @pl.when(step == 0)
    def _():
        acc_ref[...] = piece

    @pl.when(step > 0)
    def _():
        acc_ref[...] += piece

    @pl.when(step == GROUPS - 1)
    def _():
        attn = acc_ref[...]
        tok = tok_ref[...].astype(f32)
        middle = tok + attn
        middle_ref[...] = middle
        two_ref[...] = (normal(middle) * gains_ref[1:2]).astype(bf16)
        for i, v in enumerate((tok, attn, middle)):
            sums_ref[i : i + 1] = jnp.sum(v * v, axis=0, keepdims=True)


def attend(seq, prev, tok, gains, weights, cosine, sine):
    rows = tok.shape[0]
    heads = D // HEAD_DIM
    across = lambda n: pl.BlockSpec((n, GROUP), lambda i: (0, i))
    weight = lambda first: pl.BlockSpec((D, GROUP), lambda i: (0, first + i))
    return pl.pallas_call(
        attend_body,
        grid=(GROUPS,),
        in_specs=[
            pl.BlockSpec(memory_space=pltpu.SMEM),
            whole(prev.shape),
            whole(tok.shape),
            whole(gains.shape),
            weight(0),
            weight(GROUPS),
            weight(2 * GROUPS),
            pl.BlockSpec((GROUP, D), lambda i: (i, 3)),
            whole(cosine.shape),
            whole(sine.shape),
        ],
        out_specs=[
            whole((2 * rows, D)),
            across(rows),
            across(2 * rows),
            across(2 * rows),
            across(rows),
            pl.BlockSpec((8 * heads // GROUPS, rows), lambda i: (i, 0)),
            whole((rows, D)),
            whole((rows, D)),
            whole((8, D)),
        ],
        out_shape=shapes(
            ((2 * rows, D), bf16),
            ((rows, D), bf16),
            ((2 * rows, D), bf16),
            ((2 * rows, D), bf16),
            ((rows, D), bf16),
            ((8 * heads, rows), f32),
            ((rows, D), f32),
            ((rows, D), bf16),
            ((8, D), f32),
        ),
        scratch_shapes=[pltpu.VMEM((rows, D), f32)],
        compiler_params=params(56),
        cost_estimate=cost(
            2 * rows * D * D * 6 + 8 * rows * rows * D, 8 * D * D + 20 * rows * D, heads * 2 * rows * rows
        ),
        name="attend",
    )(seq, prev, tok, gains, *[weights] * 4, cosine, sine)


def attend_back_body(
    seq_ref, grad_ref, wo_ref, wq_ref, wk_ref, wv_ref, q_ref, k_ref, v_ref, mixed_ref, lse_ref,
    normed_ref, cos_ref, sin_ref, *refs,
):
    one_ref, d_ref, gq_ref, gk_ref, gv_ref, dqt_ref, dk_ref, dv_ref = refs[-8:]
    rows = grad_ref.shape[0]
    cosine, sine = cos_ref[...], sin_ref[...]
    skip = jnp.where(seq_ref[0] > 0, 0.0, 1e30)
    grad_mixed = contract(grad_ref[...], wo_ref[...], ((1,), (1,))).astype(bf16)
    for at in range(0, GROUP, LANES):
        cols = slice(at, at + LANES)
        key, value = k_ref[:, cols], v_ref[:, cols]
        key_t = key.T
        products = grad_mixed[:, cols].astype(f32) * mixed_ref[:, cols].astype(f32)
        for j in range(LANES // HEAD_DIM):
            head = (at // HEAD_DIM + j) * 8
            keep = lax.broadcasted_iota(jnp.int32, key_t.shape, 0) // HEAD_DIM == j
            key_j = jnp.where(keep, key_t, jnp.zeros_like(key_t))
            for top in range(0, rows, BLOCK):
                block = slice(top, top + BLOCK)
                query = one_head(q_ref[block, cols], j)
                grad = one_head(grad_mixed[block, cols], j)
                delta = row_of(
                    jnp.sum(one_head(products[block], j), axis=1, keepdims=True)
                )[0:1]
                lse = lse_ref[head : head + 1, block]
                for begin, end, less in ((0, rows, lse + skip), (rows, rows + top + BLOCK, lse)):
                    probs = jnp.exp(contract(key[begin:end], query, ((1,), (1,))) - less)
                    back = contract(value[begin:end], grad, ((1,), (1,))) - delta
                    scores = (probs * back).astype(bf16)
                    grad_v = contract(probs.astype(bf16), grad, ((1,), (0,)))
                    grad_k = contract(scores, query, ((1,), (0,)))
                    grad_q = contract(key_j[:, begin:end], scores, ((1,), (0,)))
                    if j == 0 and top == 0 and begin == 0:
                        dv_ref[begin:end], dk_ref[begin:end] = grad_v, grad_k
                    elif j == 0 and top == 0:
                        dv_ref[begin:end], dk_ref[begin:end] = grad_v, grad_k
                        if end < 2 * rows:
                            rest = jnp.zeros((2 * rows - end, LANES), f32)
                            dv_ref[end:], dk_ref[end:] = rest, rest
                    else:
                        dv_ref[begin:end] += grad_v
                        dk_ref[begin:end] += grad_k
                    if j == 0 and begin == 0:
                        dqt_ref[:, block] = grad_q
                    else:
                        dqt_ref[:, block] += grad_q
        own_cos, own_sin = cosine[rows:], sine[rows:]
        gq_ref[:, cols] = (rope(dqt_ref[...].T, own_cos, -own_sin) * 0.125).astype(bf16)
        gk_ref[:, cols] = rope(dk_ref[...], cosine, -sine).astype(bf16)
        gv_ref[:, cols] = dv_ref[...].astype(bf16)
    gq, gk, gv = gq_ref[...], gk_ref[...], gv_ref[...]
    one = contract(gk, wk_ref[...], ((1,), (1,))) + contract(gv, wv_ref[...], ((1,), (1,)))
    if len(refs) > 8:
        one += refs[0][...]
    one_ref[:rows] = one[:rows]
    one_ref[rows:] = one[rows:] + contract(gq, wq_ref[...], ((1,), (1,)))
    normed = normed_ref[...]
    d_ref[:, :GROUP] = contract(normed[:, rows:], gq, ((1,), (0,))).astype(bf16)
    d_ref[:, GROUP : 2 * GROUP] = contract(normed, gk, ((1,), (0,))).astype(bf16)
    d_ref[:, 2 * GROUP :] = contract(normed, gv, ((1,), (0,))).astype(bf16)


def attend_back(i, seq, grad, weights, q, k, v, mixed, lse, normed_t, cosine, sine, held):
    rows = grad.shape[0]
    heads = D // HEAD_DIM // GROUPS
    across = lambda n: pl.BlockSpec((n, GROUP), lambda _: (0, i))
    weight = lambda first: pl.BlockSpec((D, GROUP), lambda _: (0, first + i))
    return pl.pallas_call(
        attend_back_body,
        grid=(1,),
        in_specs=[
            pl.BlockSpec(memory_space=pltpu.SMEM),
            whole(grad.shape),
            pl.BlockSpec((GROUP, D), lambda _: (i, 3)),
            weight(0),
            weight(GROUPS),
            weight(2 * GROUPS),
            across(rows),
            across(2 * rows),
            across(2 * rows),
            across(rows),
            pl.BlockSpec((8 * heads, rows), lambda _: (i, 0)),
            whole(normed_t.shape),
            whole(cosine.shape),
            whole(sine.shape),
        ]
        + [whole((2 * rows, D))] * len(held),
        out_specs=[whole((2 * rows, D)), whole((D, 3 * GROUP))],
        out_shape=shapes(((2 * rows, D), f32), ((D, 3 * GROUP), bf16)),
        scratch_shapes=[
            pltpu.VMEM((rows, GROUP), bf16),
            pltpu.VMEM((2 * rows, GROUP), bf16),
            pltpu.VMEM((2 * rows, GROUP), bf16),
            pltpu.VMEM((LANES, rows), f32),
            pltpu.VMEM((2 * rows, LANES), f32),
            pltpu.VMEM((2 * rows, LANES), f32),
        ],
        compiler_params=params(56),
        cost_estimate=cost(
            2 * rows * D * GROUP * 11 + 20 * rows * rows * GROUP, 40 * rows * D, heads * 2 * rows * rows
        ),
        name="attend_back",
    )(seq, grad, *[weights] * 4, q, k, v, mixed, lse, normed_t, cosine, sine, *held)


def gather_columns_body(first_ref, second_ref, third_ref, qkv_ref, out_ref, tail_ref):
    for i, ref in enumerate((first_ref, second_ref, third_ref)):
        for part in range(3):
            to = part * D + i * GROUP
            qkv_ref[:, to : to + GROUP] = ref[:, part * GROUP : (part + 1) * GROUP]
    out_ref[...] = first_ref[:, 3 * GROUP :]
    tail_ref[...] = third_ref[:, 3 * GROUP :]


def gather_columns(first, second, third):
    rows = first.shape[0]
    return pl.pallas_call(
        gather_columns_body,
        in_specs=[whole(v.shape) for v in (first, second, third)],
        out_specs=[whole((rows, n)) for n in (3 * D, D, LANES)],
        out_shape=shapes(*(((rows, n), f32) for n in (3 * D, D, LANES))),
        grid=(1,),
        name="gather_columns",
    )(first, second, third)


def rope_tables(positions):
    halfdim = HEAD_DIM // 2
    inverse = 10000.0 ** (-2.0 * jnp.arange(halfdim, dtype=f32) / HEAD_DIM)
    angles = positions.astype(f32)[:, None] * inverse[None, :]
    cosine, sine = jnp.cos(angles), jnp.sin(angles)
    times = LANES // HEAD_DIM
    return (
        jnp.tile(jnp.concatenate([cosine, cosine], axis=1), (1, times)),
        jnp.tile(jnp.concatenate([-sine, sine], axis=1), (1, times)),
    )


SPLIT = (range(0, BRANCHES),)


def columns_out(w_ffn_in):
    depth = lax.axis_size("z")
    rows, count = w_ffn_in.shape[:2]
    pair = 2 * (FF // lax.axis_size(ALL))
    cut = w_ffn_in.reshape(rows, count, 2, 2, 2, depth // 2, 2, pair)
    return cut.transpose(3, 6, 4, 0, 1, 2, 5, 7).reshape(8, rows, -1)


def columns_back(v, count):
    depth = lax.axis_size("z")
    rows = v.shape[1]
    pair = 2 * (FF // lax.axis_size(ALL))
    v = v.reshape(2, 2, 2, rows, count, 2, depth // 2, pair).astype(f32)
    return v.transpose(3, 4, 5, 0, 2, 6, 1, 7).reshape(rows, count, 2 * FF)


def exchange(cut):
    return lax.all_to_all(cut, PLANE, split_axis=0, concat_axis=0, tiled=True)


def columns_in(cut):
    wide = cut.shape[-1]
    cut = cut.reshape(2, -1, wide)
    return lax.all_gather(cut, "z", axis=1, tiled=True).reshape(D, wide)


def units_in(part):
    depth = lax.axis_size("z")
    count, own = part.shape[0], part.shape[1] // depth
    part = part.reshape(count, 2, depth // 2, own, D)
    core = own_bit("c")
    kept = lax.dynamic_index_in_dim(part, core, 1, keepdims=False)
    sent = lax.dynamic_index_in_dim(part, 1 - core, 1, keepdims=False)
    other = swap(sent, "c")
    both = jnp.where(core == 0, jnp.stack([kept, other], 2), jnp.stack([other, kept], 2))
    return both.reshape(count, depth * own, D)


def units_out(d_hid, count):
    depth = lax.axis_size("z")
    own = d_hid.shape[0] // count // depth
    d_hid = d_hid.reshape(count, depth // 2, 2, own, D)
    core = own_bit("c")
    kept = lax.dynamic_index_in_dim(d_hid, core, 2, keepdims=False)
    other = swap(lax.dynamic_index_in_dim(d_hid, 1 - core, 2, keepdims=False), "c")
    both = jnp.where(core == 0, jnp.stack([kept, other], 1), jnp.stack([other, kept], 1))
    both = both.reshape(count, depth * own, D)
    return lax.psum_scatter(both, "z", scatter_dimension=1, tiled=True).transpose(1, 0, 2)


def on_device(
    tokens, cotangent, routes, gain_one, w_qkv, w_attn_out, gain_two, router, w_ffn_in, w_ffn_out
):
    rows = tokens.shape[1]
    own_rows = w_qkv.shape[0]
    low_tokens = tokens.reshape(rows, D)
    low_grad = cotangent.reshape(rows, D)

    cut = exchange(columns_out(w_ffn_in))
    starts = [2 * FF // 8 * branches[0] for branches in SPLIT] + [cut.shape[-1]]
    w_out = lax.all_gather(w_ffn_out.transpose(1, 0, 2), "z", axis=1, tiled=True)
    w_in = [columns_in(cut[:, :, a:b]) for a, b in zip(starts, starts[1:])]
    before = lax.ppermute(low_tokens, "x", [(i, i + 1) for i in range(lax.axis_size("x") - 1)])
    seq_index = lax.axis_index("x")
    positions = (seq_index - 1) * rows + jnp.arange(2 * rows, dtype=jnp.int32)
    cosine, sine = rope_tables(positions)
    seq = seq_index.astype(jnp.int32).reshape(1)
    route = jnp.pad(routes.reshape(rows, TOP), ((0, 0), (0, LANES - TOP))).astype(bf16)
    grad_ext = jnp.concatenate([low_grad, route], axis=1)
    small = jnp.concatenate([gain_one[:, None], gain_two[:, None], router], axis=1)
    small = jnp.pad(small, ((0, 0), (0, LANES - small.shape[1])))
    weights = gather_rows(
        jnp.concatenate([w_qkv, w_attn_out, small], axis=1), (cut, before), (cosine, sine, grad_ext)
    )
    gains = weights[:, 4 * D : 4 * D + 2].astype(f32).T
    router_full = jnp.pad(
        weights[:, 4 * D + 2 : 4 * D + 2 + EXPERTS], ((0, 0), (0, LANES - EXPERTS))
    )
    grad_ext = after(grad_ext, weights)
    grad_x, grad_y = swap(grad_ext, "x"), swap(grad_ext, "y")

    results = attend(seq, before, low_tokens, gains, weights, cosine, sine)
    results = after(results, grad_x, grad_y)
    normed_one, q, k, v, mixed, lse, middle, normed_two, sums = results

    half = rows // 2

    def corner(across_x, across_y):
        return swap(across_x[:half], "y"), swap(across_y[half:], "x")

    def both_cores(u):
        return (u, swap(u, "c"))

    across_x, across_y = swap(normed_two, "x"), swap(normed_two, "y")
    grad_far = corner(grad_x, grad_y)
    normed_t = normed_one.T
    w_out = units_in(after(w_out, normed_two))
    x, g = {0: both_cores(normed_two)}, {0: both_cores(grad_ext)}
    x[0] = after(x[0], normed_t)
    below, gating, d_in, d_hid = {}, {}, [], []
    for branches, columns in zip(SPLIT, w_in):
        first, last = branches[0] == 0, branches[-1] == BRANCHES - 1
        columns = jnp.concatenate([columns, router_full], axis=1)
        units = w_out[branches[0] : branches[-1] + 1]
        if not first:
            columns = after(columns, d_in, d_hid)
        kept, top = (), {}

        def run(which, kept, *moves):
            part, gate, kept = ffn(
                which, 4, branches, x[which], g[which], columns, units, kept, gating.get(which)
            )
            part, moves = after((part, moves), part[0], moves) if moves else (part, ())
            gating[which] = gate or None
            return part, kept, moves

        if first:
            part, kept, moves = run(0, kept, across_x, across_y, *grad_far)
            top[0], (across_x, across_y, *grad_far) = part, moves
            far = corner(across_x, across_y)
            x[1], g[1] = both_cores(across_x), both_cores(grad_x)
            top[1], kept, far = run(1, kept, *far)
            x[3], g[3] = both_cores(jnp.concatenate(far)), both_cores(jnp.concatenate(grad_far))
            x[2], g[2] = both_cores(across_y), both_cores(grad_y)
        else:
            top[0], kept, _ = run(0, kept)
            top[1], kept, _ = run(1, kept)
        top[3], kept, _ = run(3, kept)
        if last:
            v3 = on_chip(top[3], below.get(3))
            moves = swap(v3[:half].astype(bf16), "x"), swap(v3[half:].astype(bf16), "y")
            top[2], kept, (upper, lower) = run(2, kept, *moves)
        else:
            top[2], kept, _ = run(2, kept)
        if first:
            x_all, g_all = kept[2:]
        rows_in_all = x_all
        if last:
            v1 = on_chip(top[1], below.get(1))
            v2 = on_chip(top[2], below.get(2))
            for_x = jnp.concatenate([v1[:half], v1[half:] + lower.astype(f32)]).astype(bf16)
            for_y = jnp.concatenate([v2[:half] + upper.astype(f32), v2[half:]]).astype(bf16)
            from_x, from_y = swap(for_x[:, :D], "x"), swap(for_y[:, :D], "y")
            rows_in_all = after(x_all, for_x, for_y)
        full = contract(rows_in_all, kept[1], ((0,), (0,)))
        wide = columns.shape[1] - LANES
        if last:
            d_router_part = full[:, wide : wide + EXPERTS]
            full, from_x, from_y = after((full, from_x, from_y), full, from_x, from_y)
        full = full[:, :wide].astype(bf16)
        d_in.append(full)
        d_hid.append(contract(after(kept[0], full), g_all, ((0,), (0,))).astype(bf16))
        if not last:
            below = {which: on_chip(part, below.get(which)) for which, part in top.items()}
    total = on_chip(top[0], below.get(0))
    grad_rows = total[:, :D] + from_x.astype(f32) + from_y.astype(f32)
    hat_two = normal(middle)
    d_gain_two_part = jnp.sum(grad_rows * hat_two, axis=0)
    _, norm_two_back = jax.vjp(normal, middle)
    grad_middle = low_grad.astype(f32) + norm_two_back(grad_rows * gains[1:2])[0]
    grad_attn = after(grad_middle.astype(bf16), d_hid)
    d_attn_out = contract(mixed, grad_attn, ((0,), (0,))).astype(bf16)
    d_cols = [
        lax.psum_scatter(u.reshape(2, D // 2, -1), "z", scatter_dimension=1, tiled=True)
        for u in d_in
    ]
    d_w_out = [units_out(u, len(branches)) for u, branches in zip(d_hid, SPLIT)]

    def back(i, grad, held, *moves):
        one, part = attend_back(
            i, seq, grad, weights, q, k, v, mixed, lse, normed_t, cosine, sine, held
        )
        return after((one, part, moves), one, moves)

    for_x, for_y = after((for_x, for_y), grad_attn)
    moves = swap(for_x[:, D:], "x"), swap(for_y[:, D:], "y")
    one, part, (from_x, from_y) = back(0, grad_attn, (), *moves)
    ffn_out = total[:, D:] + from_x.astype(f32) + from_y.astype(f32)
    output = middle + ffn_out
    partial_sums = jnp.concatenate(
        [jnp.sum(sums[:3], axis=1), jnp.stack([jnp.sum(u * u) for u in (ffn_out, output)])]
    )
    first = Scatter(jnp.concatenate([part, d_attn_out], axis=1), own_rows)
    first.take(first.send())
    moves = first.send()
    d_cols = [u.reshape(8, own_rows, -1) for u in d_cols]
    early = exchange(after(d_cols[0], one)) if len(d_cols) > 1 else ()
    one, part, (moves, early) = back(1, after(grad_attn, one, partial_sums), (one,), moves, early)
    first.take(moves)
    second = Scatter(part, own_rows)
    second.take(second.send())
    late = exchange(after(d_cols[-1], one))
    moves = first.send(), second.send(), late
    one, part, moves = back(2, after(grad_attn, one), (one,), *moves)
    first.take(moves[0])
    second.take(moves[1])
    returned = lax.ppermute(
        one[:rows].astype(bf16), "x", [(i + 1, i) for i in range(lax.axis_size("x") - 1)]
    )
    rows_in = low_tokens.astype(f32)
    hat_one = normal(rows_in)
    d_gain_one_part = jnp.sum(one[rows:] * hat_one, axis=0) + jnp.sum(
        one[:rows] * normal(before.astype(f32)), axis=0
    )
    tail = jnp.concatenate(
        [d_gain_one_part[:, None], d_gain_two_part[:, None], d_router_part], axis=1
    )
    tail = jnp.pad(tail, ((0, 0), (0, LANES - tail.shape[1]))).astype(bf16)
    third = Scatter(jnp.concatenate([part, tail], axis=1), own_rows, partial_sums)
    third.take(third.send())
    third.take(third.send())
    second.finish()
    third.finish()
    first.finish()
    returned = after(returned, third.v)
    d_cols = [moves[2]] if len(d_cols) == 1 else [early, moves[2]]
    d_w_qkv, d_w_attn_out, tail = gather_columns(first.v, second.v, third.v)
    stats = jnp.sqrt(third.extra / (rows * lax.axis_size(ALL) * D))
    _, norm_one_back = jax.vjp(normal, rows_in)
    grad_one = (one[rows:] + returned.astype(f32)) * gains[0:1]
    grad_tokens = grad_middle + norm_one_back(grad_one)[0]
    return (
        output.reshape(tokens.shape).astype(bf16),
        grad_tokens.reshape(tokens.shape).astype(bf16),
        tail[:, 0],
        d_w_qkv,
        d_w_attn_out,
        tail[:, 1],
        tail[:, 2 : 2 + EXPERTS],
        jnp.concatenate([columns_back(u, len(b)) for u, b in zip(d_cols, SPLIT)], axis=1),
        jnp.concatenate([u.astype(f32) for u in d_w_out], axis=1),
        stats,
    )


def solution(mesh):
    seq, fsdp = mesh.shape["seq"], mesh.shape["fsdp"]
    inner = Mesh(mesh.devices.reshape(seq, fsdp // 4, 2, 2), ALL)
    data = P(("z", "y", "c"), "x", None)
    weights = tuple(P(ALL, *(None,) * k) for k in (0, 1, 1, 0, 1, 2, 2))
    return jax.shard_map(
        on_device,
        mesh=inner,
        in_specs=(data, data, data) + weights,
        out_specs=(data, data) + weights + (P(),),
        check_vma=False,
    )
```

```python
import functools
import itertools
import math

import jax
import jax.numpy as jnp
from jax import lax
from jax.experimental import pallas as pl
from jax.experimental.pallas import tpu as pltpu
from jax.sharding import Mesh, PartitionSpec as P

D = 768
HEAD_DIM = 64
FF = 2048
EXPERTS = 4
BRANCHES = EXPERTS + 1
TOP = 2
BLOCK = 256
LANES = 128
GROUP = 256
GROUPS = D // GROUP

epsilon = 1e-05
f32 = jnp.float32
bf16 = jnp.bfloat16
ALL = ("x", "z", "y", "c")
PLANE = ("x", "y", "c")


def shuffle(v, axes, by):
    sizes = [lax.axis_size(axis) for axis in axes]
    pairs = []
    for at in range(math.prod(sizes)):
        rest, to, scale = at, 0, 1
        for size, flip in reversed(list(zip(sizes, by))):
            to += (rest % size ^ flip) * scale
            rest, scale = rest // size, scale * size
        pairs.append((at, to))
    return lax.ppermute(v, axes, pairs)


def swap(v, axis):
    return shuffle(v, (axis,), (1,))


def own_bit(axis, bit=0):
    return (lax.axis_index(axis) >> bit) & 1


def after(v, *deps):
    return lax.optimization_barrier((v, deps))[0]


def ordered(low, mine, other):
    return jnp.where(low, jnp.stack([mine, other]), jnp.stack([other, mine]))


def gather_axes(v, bits):
    axes = tuple(dict.fromkeys(axis for axis, _ in bits))

    def part(flips):
        by = [0] * len(axes)
        for (axis, bit), flip in zip(bits, flips):
            by[axes.index(axis)] |= flip << bit
        return shuffle(v, axes, by) if any(flips) else v

    def level(flips):
        if len(flips) == len(bits):
            return part(flips)
        low = own_bit(*bits[len(flips)]) == 0
        return ordered(low, level(flips + (0,)), level(flips + (1,)))

    return level(())


def z_bits():
    return [("z", bit) for bit in reversed(range(lax.axis_size("z").bit_length() - 1))]


def z_stages():
    bits = z_bits()
    return [bits] if len(bits) <= 2 else [[name] for name in bits]


def all_bits():
    return [("x", 0)] + z_bits() + [("y", 0), ("c", 0)]


def gather_rows(v, deps, more):
    held = []
    for bits in z_stages()[::-1] + [[("x", 0), ("y", 0)], [("c", 0)]]:
        if ("x", 0) in bits:
            v = after(v, deps)
        if ("c", 0) in bits:
            v = after(v, more)
        v = gather_axes(v, bits)
        held = bits + held
    lead = [held.index(name) for name in all_bits()]
    v = v.transpose(lead + list(range(len(lead), v.ndim)))
    return v.reshape(-1, v.shape[-1])


class Scatter:
    def __init__(self, v, rows, extra=None):
        self.names = all_bits()
        self.v = v.reshape((2,) * len(self.names) + (rows, v.shape[1]))
        self.extra = extra
        self.stages = [[("c", 0)], [("x", 0), ("y", 0)]] + z_stages()

    def block(self, flips, bits):
        v = self.v
        at = {self.names.index(name): own_bit(*name) ^ flip for name, flip in zip(bits, flips)}
        starts = [at.get(i, 0) for i in range(v.ndim)]
        sizes = [1 if i in at else v.shape[i] for i in range(v.ndim)]
        piece = lax.dynamic_slice(v, starts, sizes)
        return piece.reshape([n for i, n in enumerate(v.shape) if i not in at])

    def send(self):
        bits = self.stages[0]
        axes = tuple(dict.fromkeys(axis for axis, _ in bits))
        width = self.v.shape[-1]
        if self.extra is not None:
            count = self.extra.shape[0]
            coded, rest = [], self.extra
            for _ in range(3):
                coded.append(lax.reduce_precision(rest, 8, 7))
                rest = rest - coded[-1]
            spread = jnp.pad(jnp.concatenate(coded).astype(bf16), (width - 3 * count, 0))
            lane = jnp.arange(width) >= width - 3 * count
        moves = []
        for flips in itertools.product((0, 1), repeat=len(bits)):
            if not any(flips):
                continue
            by = [0] * len(axes)
            for (axis, bit), flip in zip(bits, flips):
                by[axes.index(axis)] |= flip << bit
            sent = self.block(flips, bits).astype(bf16)
            if self.extra is not None:
                sent = jnp.where(lane, spread, sent)
            moves.append(shuffle(sent, axes, by))
        return moves

    def take(self, moves):
        bits, self.stages = self.stages[0], self.stages[1:]
        total = self.block((0,) * len(bits), bits).astype(f32)
        for got in moves:
            got = got.astype(f32)
            total += got
            if self.extra is not None:
                count = self.extra.shape[0]
                parts = got.reshape(-1, got.shape[-1])[0, -3 * count :].reshape(3, count)
                self.extra = self.extra + (parts[0] + parts[1] + parts[2])
        self.v = total
        self.names = [name for name in self.names if name not in bits]

    def finish(self):
        while self.stages:
            self.take(self.send())


def on_chip(pair, more=None):
    v = pair[0] + swap(pair[1], "c").astype(f32)
    return v if more is None else v + more


def contract(a, b, dims):
    return lax.dot_general(a, b, (dims, ((), ())), preferred_element_type=f32)


def whole(shape):
    return pl.BlockSpec(shape, lambda *i: (0,) * len(shape))


def fixed(shape):
    return pl.BlockSpec(shape, lambda *i: (0,) * len(shape), pipeline_mode=pl.Buffered(1))


def shapes(*pairs):
    return [jax.ShapeDtypeStruct(shape, kind) for shape, kind in pairs]


def params(mib):
    return pltpu.CompilerParams(vmem_limit_bytes=mib * 2**20)


def cost(flops, moved, exps=0):
    return pl.CostEstimate(flops=flops, transcendentals=exps, bytes_accessed=moved)


def sigmoid(a):
    return 0.5 * jnp.tanh(0.5 * a) + 0.5


def ffn_body(branches, first, last, names, *refs):
    r = dict(zip(names, refs))
    win_ref, wout_ref, h_ref, p_ref = r["w_in"], r["w_out"], r["hidden"], r["pre"]
    units = wout_ref.shape[1]
    wide = len(branches) * units
    tile = h_ref.shape[0]
    step = pl.program_id(0)
    half = pl.num_programs(0) // 2
    own = step < half
    here = pl.ds(lax.rem(step, half) * tile, tile)
    x = jnp.where(own, r["xa"][here], r["xb"][here])
    g = jnp.where(own, r["ga"][here], r["gb"][here])
    lane = lax.broadcasted_iota(jnp.int32, (tile, LANES), 1)
    if first:
        r["xs"][...] = x
        r["gs"][...] = g[:, :D]
        route = g[:, D:].astype(f32).astype(jnp.int32)
        logits = contract(x, win_ref[:, 2 * wide :], ((1,), (0,)))
        one, two = lane == route[:, 0:1], lane == route[:, 1:2]
        up = jnp.sum(jnp.where(one, logits, 0.0), axis=1, keepdims=True)
        down = jnp.sum(jnp.where(two, logits, 0.0), axis=1, keepdims=True)
        top = jnp.maximum(up, down)
        up, down = jnp.exp(up - top), jnp.exp(down - top)
        total = up + down
        gates = jnp.where(one, up / total, 0.0) + jnp.where(two, down / total, 0.0)
        grad_gates = jnp.zeros_like(gates)
    else:
        gates, grad_gates = r["gates"][...], r["sums"][...]
    g = g[:, :D]
    for i, e in enumerate(branches):
        at = i * 2 * units
        pre = contract(x, win_ref[:, at : at + 2 * units], ((1,), (0,)))
        a, b = pre[:, :units], pre[:, units:]
        back = contract(g, wout_ref[i], ((1,), (1,)))
        s = sigmoid(a)
        silu = a * s
        hidden = (silu * b).astype(bf16)
        if e < EXPERTS:
            gate = gates[:, e : e + 1]
            hidden = hidden.astype(f32)
            this = jnp.sum(hidden * back, axis=1, keepdims=True)
            grad_gates = jnp.where(lane == e, this, grad_gates)
            hidden = (gate * hidden).astype(bf16)
            back = gate * back
        h_ref[:, i * units : (i + 1) * units] = hidden
        p_ref[:, at : at + units] = (back * b * (s + silu * (1.0 - s))).astype(bf16)
        p_ref[:, at + units : at + 2 * units] = (back * silu).astype(bf16)
        if last and e == EXPERTS - 1:
            inner = jnp.sum(gates * grad_gates, axis=1, keepdims=True)
            p_ref[:, 2 * wide :] = (gates * (grad_gates - inner)).astype(bf16)
    if not last:
        r["gates_out"][...] = gates
        r["sums_out"][...] = grad_gates
    tile_ref = r["tile"]
    deep = p_ref.shape[1]
    out = contract(h_ref[...], wout_ref[...].reshape(wide, D), ((1,), (0,)))
    tile_ref[:, D:] = out
    for at in range(0, D, GROUP):
        cols = slice(at, at + GROUP)
        tile_ref[:, cols] = contract(p_ref[...], win_ref[cols, :deep], ((1,), (1,)))

    @pl.when(own)
    def _():
        r["own"][here] = tile_ref[...]

    @pl.when(jnp.logical_not(own))
    def _():
        r["other"][here] = tile_ref[...].astype(bf16)


def ffn(part, parts, branches, x, g, w_in, w_out, kept, gating=None):
    first, last = gating is None, branches[-1] == BRANCHES - 1
    rows = x[0].shape[0]
    tile = min(256, rows)
    steps = rows // tile
    wide = w_in.shape[1] - LANES
    total = parts * 2 * rows
    here = lambda width: pl.BlockSpec((tile, width), lambda i: (i, 0))
    there = lambda width: pl.BlockSpec((tile, width), lambda i: (2 * part * steps + i, 0))
    ins = list(zip(("xa", "xb", "ga", "gb", "w_in", "w_out"), (*x, *g, w_in, w_out)))
    specs = [fixed(v.shape) for _, v in ins]
    if not first:
        ins += list(zip(("gates", "sums"), gating))
        specs += [here(LANES)] * 2
    outs = [("own", (rows, 2 * D), f32, whole((rows, 2 * D)))]
    outs += [("other", (rows, 2 * D), bf16, whole((rows, 2 * D)))]
    if not last:
        outs += [(n, (2 * rows, LANES), f32, here(LANES)) for n in ("gates_out", "sums_out")]
    at = len(outs)
    widths = [("hidden", wide // 2), ("pre", wide + last * LANES)]
    if first:
        widths += [("xs", D), ("gs", D)]
    outs += [(n, (total, width), bf16, there(width)) for n, width in widths]
    names = [n for n, _ in ins] + ["old"] * len(kept) + [n for n, *_ in outs] + ["tile"]
    results = pl.pallas_call(
        functools.partial(ffn_body, branches, first, last, names),
        grid=(2 * steps,),
        in_specs=specs + [pl.BlockSpec(memory_space=pl.ANY)] * len(kept),
        out_specs=[spec for *_, spec in outs],
        out_shape=shapes(*((shape, kind) for _, shape, kind, _ in outs)),
        scratch_shapes=[pltpu.VMEM((tile, 2 * D), f32)],
        input_output_aliases={len(ins) + i: at + i for i in range(len(kept))},
        compiler_params=params(40),
        cost_estimate=cost(
            12 * rows * D * wide, 3 * w_in.size + rows * (20 * D + 6 * wide), rows * wide
        ),
        name="ffn",
    )(*(v for _, v in ins), *kept)
    return results[:2], results[2:at], results[at:]


def half_turn(v):
    lane = lax.broadcasted_iota(jnp.int32, v.shape, 1)
    low = lane % HEAD_DIM < HEAD_DIM // 2
    return jnp.where(low, pltpu.roll(v, 128 - HEAD_DIM // 2, 1), pltpu.roll(v, HEAD_DIM // 2, 1))


def rope(v, cosine, sine):
    parts = [v[:, at : at + LANES] for at in range(0, v.shape[1], LANES)]
    return jnp.concatenate([p * cosine + half_turn(p) * sine for p in parts], axis=1)


def one_head(v, j):
    lane = lax.broadcasted_iota(jnp.int32, v.shape, 1)
    return jnp.where(lane // HEAD_DIM == j, v, jnp.zeros_like(v))


def normal(rows_in):
    return rows_in * lax.rsqrt(jnp.mean(rows_in * rows_in, axis=-1, keepdims=True) + epsilon)


def row_of(column):
    return jnp.broadcast_to(column, (column.shape[0], LANES)).T[:8]


def attend_body(
    seq_ref, prev_ref, tok_ref, gains_ref, wq_ref, wk_ref, wv_ref, wo_ref, cos_ref, sin_ref,
    normed_ref, q_ref, k_ref, v_ref, mixed_ref, lse_ref, middle_ref, two_ref, sums_ref, acc_ref,
):
    step = pl.program_id(0)
    rows = tok_ref.shape[0]

    @pl.when(step == 0)
    def _():
        for at, ref in ((0, prev_ref), (rows, tok_ref)):
            hat = normal(ref[...].astype(f32))
            normed_ref[at : at + rows] = (hat * gains_ref[0:1]).astype(bf16)

    x = normed_ref[...]
    cosine, sine = cos_ref[...], sin_ref[...]
    own_cos, own_sin = cosine[rows:], sine[rows:]
    q = contract(x[rows:], wq_ref[...], ((1,), (0,)))
    q_ref[...] = (rope(q, own_cos, own_sin) * 0.125).astype(bf16)
    k_ref[...] = rope(contract(x, wk_ref[...], ((1,), (0,))), cosine, sine).astype(bf16)
    v_ref[...] = contract(x, wv_ref[...], ((1,), (0,))).astype(bf16)
    skip = jnp.where(seq_ref[0] > 0, 0.0, 1e30)
    for at in range(0, GROUP, LANES):
        cols = slice(at, at + LANES)
        for top in range(0, rows, BLOCK):
            mixed = jnp.zeros((BLOCK, LANES), f32)
            ends = rows + top + BLOCK
            for j in range(LANES // HEAD_DIM):
                query = one_head(q_ref[top : top + BLOCK, cols], j)
                far = contract(query, k_ref[:rows, cols], ((1,), (1,)))
                near = contract(query, k_ref[rows:ends, cols], ((1,), (1,)))
                peak = jnp.maximum(
                    jnp.max(far, axis=1, keepdims=True) - skip, jnp.max(near, axis=1, keepdims=True)
                )
                far, near = jnp.exp(far - (peak + skip)), jnp.exp(near - peak)
                total = jnp.sum(far, axis=1, keepdims=True) + jnp.sum(near, axis=1, keepdims=True)
                both = contract(far.astype(bf16), one_head(v_ref[:rows, cols], j), ((1,), (0,)))
                both += contract(near.astype(bf16), one_head(v_ref[rows:ends, cols], j), ((1,), (0,)))
                mixed += both / total
                head = (at // HEAD_DIM + j) * 8
                lse_ref[head : head + 8, top : top + BLOCK] = row_of(peak + jnp.log(total))
            mixed_ref[top : top + BLOCK, cols] = mixed.astype(bf16)
    piece = contract(mixed_ref[...], wo_ref[...], ((1,), (0,)))

    @pl.when(step == 0)
    def _():
        acc_ref[...] = piece

    @pl.when(step > 0)
    def _():
        acc_ref[...] += piece

    @pl.when(step == GROUPS - 1)
    def _():
        attn = acc_ref[...]
        tok = tok_ref[...].astype(f32)
        middle = tok + attn
        middle_ref[...] = middle
        two_ref[...] = (normal(middle) * gains_ref[1:2]).astype(bf16)
        for i, v in enumerate((tok, attn, middle)):
            sums_ref[i : i + 1] = jnp.sum(v * v, axis=0, keepdims=True)


def attend(seq, prev, tok, gains, weights, cosine, sine):
    rows = tok.shape[0]
    heads = D // HEAD_DIM
    across = lambda n: pl.BlockSpec((n, GROUP), lambda i: (0, i))
    weight = lambda first: pl.BlockSpec((D, GROUP), lambda i: (0, first + i))
    return pl.pallas_call(
        attend_body,
        grid=(GROUPS,),
        in_specs=[
            pl.BlockSpec(memory_space=pltpu.SMEM),
            whole(prev.shape),
            whole(tok.shape),
            whole(gains.shape),
            weight(0),
            weight(GROUPS),
            weight(2 * GROUPS),
            pl.BlockSpec((GROUP, D), lambda i: (i, 3)),
            whole(cosine.shape),
            whole(sine.shape),
        ],
        out_specs=[
            whole((2 * rows, D)),
            across(rows),
            across(2 * rows),
            across(2 * rows),
            across(rows),
            pl.BlockSpec((8 * heads // GROUPS, rows), lambda i: (i, 0)),
            whole((rows, D)),
            whole((rows, D)),
            whole((8, D)),
        ],
        out_shape=shapes(
            ((2 * rows, D), bf16),
            ((rows, D), bf16),
            ((2 * rows, D), bf16),
            ((2 * rows, D), bf16),
            ((rows, D), bf16),
            ((8 * heads, rows), f32),
            ((rows, D), f32),
            ((rows, D), bf16),
            ((8, D), f32),
        ),
        scratch_shapes=[pltpu.VMEM((rows, D), f32)],
        compiler_params=params(36),
        cost_estimate=cost(
            2 * rows * D * D * 6 + 8 * rows * rows * D, 8 * D * D + 20 * rows * D, heads * 2 * rows * rows
        ),
        name="attend",
    )(seq, prev, tok, gains, *[weights] * 4, cosine, sine)


def heads_back(
    skip, grad, wo_ref, q_ref, k_ref, v_ref, mixed_ref, lse_ref, cos_ref, sin_ref, gq_ref, gk_ref,
    gv_ref, dqt_ref, dk_ref, dv_ref,
):
    rows = grad.shape[0]
    cosine, sine = cos_ref[...], sin_ref[...]
    grad_mixed = contract(grad, wo_ref[...], ((1,), (1,))).astype(bf16)
    for at in range(0, GROUP, LANES):
        cols = slice(at, at + LANES)
        key, value = k_ref[:, cols], v_ref[:, cols]
        key_t = key.T
        products = grad_mixed[:, cols].astype(f32) * mixed_ref[:, cols].astype(f32)
        for j in range(LANES // HEAD_DIM):
            head = (at // HEAD_DIM + j) * 8
            keep = lax.broadcasted_iota(jnp.int32, key_t.shape, 0) // HEAD_DIM == j
            key_j = jnp.where(keep, key_t, jnp.zeros_like(key_t))
            for top in range(0, rows, BLOCK):
                block = slice(top, top + BLOCK)
                query = one_head(q_ref[block, cols], j)
                back = one_head(grad_mixed[block, cols], j)
                delta = row_of(
                    jnp.sum(one_head(products[block], j), axis=1, keepdims=True)
                )[0:1]
                lse = lse_ref[head : head + 1, block]
                for begin, end, less in ((0, rows, lse + skip), (rows, rows + top + BLOCK, lse)):
                    probs = jnp.exp(contract(key[begin:end], query, ((1,), (1,))) - less)
                    above = contract(value[begin:end], back, ((1,), (1,))) - delta
                    scores = (probs * above).astype(bf16)
                    grad_v = contract(probs.astype(bf16), back, ((1,), (0,)))
                    grad_k = contract(scores, query, ((1,), (0,)))
                    grad_q = contract(key_j[:, begin:end], scores, ((1,), (0,)))
                    if j == 0 and top == 0:
                        dv_ref[begin:end], dk_ref[begin:end] = grad_v, grad_k
                        if rows < end < 2 * rows:
                            rest = jnp.zeros((2 * rows - end, LANES), f32)
                            dv_ref[end:], dk_ref[end:] = rest, rest
                    else:
                        dv_ref[begin:end] += grad_v
                        dk_ref[begin:end] += grad_k
                    if j == 0 and begin == 0:
                        dqt_ref[:, block] = grad_q
                    else:
                        dqt_ref[:, block] += grad_q
        own_cos, own_sin = cosine[rows:], sine[rows:]
        gq_ref[:, cols] = (rope(dqt_ref[...].T, own_cos, -own_sin) * 0.125).astype(bf16)
        gk_ref[:, cols] = rope(dk_ref[...], cosine, -sine).astype(bf16)
        gv_ref[:, cols] = dv_ref[...].astype(bf16)


def group_sums(normed, gq, gk, gv, wq_ref, wk_ref, wv_ref):
    rows = gq.shape[0]
    one = contract(gk, wk_ref[...], ((1,), (1,))) + contract(gv, wv_ref[...], ((1,), (1,)))
    own = one[rows:] + contract(gq, wq_ref[...], ((1,), (1,)))
    parts = ((normed[:, rows:], gq), (normed, gk), (normed, gv))
    return one[:rows], own, [contract(a, b, ((1,), (0,))).astype(bf16) for a, b in parts]


def attend_back_body(
    seq_ref, grad_ref, wo_ref, wq_ref, wk_ref, wv_ref, q_ref, k_ref, v_ref, mixed_ref, lse_ref,
    normed_ref, all_ref, cos_ref, sin_ref, one_ref, d_ref, *scratch,
):
    step = pl.program_id(0)
    rows = grad_ref.shape[0]

    @pl.when(step < GROUPS - 1)
    def _():
        skip = jnp.where(seq_ref[0] > 0, 0.0, 1e30)
        heads_back(
            skip, grad_ref[...], wo_ref, q_ref, k_ref, v_ref, mixed_ref, lse_ref, cos_ref, sin_ref,
            *scratch,
        )
        gq, gk, gv = (ref[...] for ref in scratch[:3])
        early, own, parts = group_sums(normed_ref[...], gq, gk, gv, wq_ref, wk_ref, wv_ref)
        for i, part in enumerate(parts):
            d_ref[:, i * GROUP : (i + 1) * GROUP] = part

        @pl.when(step == 0)
        def _():
            one_ref[:rows], one_ref[rows:] = early, own

        @pl.when(step > 0)
        def _():
            one_ref[:rows] += early
            one_ref[rows:] += own

    @pl.when(step == GROUPS - 1)
    def _():
        d_ref[...] = contract(all_ref[...], grad_ref[...], ((0,), (0,))).astype(bf16)


def attend_back_last_body(
    seq_ref, grad_ref, wo_ref, wq_ref, wk_ref, wv_ref, q_ref, k_ref, v_ref, mixed_ref, lse_ref,
    normed_ref, prev_ref, tok_ref, two_ref, one_ref, cos_ref, sin_ref, early_ref,
    own_ref, d_ref, *scratch,
):
    rows = grad_ref.shape[0]
    skip = jnp.where(seq_ref[0] > 0, 0.0, 1e30)
    heads_back(
        skip, grad_ref[...], wo_ref, q_ref, k_ref, v_ref, mixed_ref, lse_ref, cos_ref, sin_ref,
        *scratch,
    )
    gq, gk, gv = (ref[...] for ref in scratch[:3])
    early, own, parts = group_sums(normed_ref[...], gq, gk, gv, wq_ref, wk_ref, wv_ref)
    for i, part in enumerate(parts):
        d_ref[:, i * GROUP : (i + 1) * GROUP] = part
    early, own = early + one_ref[:rows], own + one_ref[rows:]
    early_ref[...] = early.astype(bf16)
    own_ref[...] = own
    gain = jnp.sum(early * normal(prev_ref[...].astype(f32)), axis=0, keepdims=True)
    gain += jnp.sum(own * normal(tok_ref[...].astype(f32)), axis=0, keepdims=True)
    gain = jnp.broadcast_to(gain, (LANES, D)).T
    two = jnp.broadcast_to(two_ref[0:1], (LANES, D)).T
    lane = lax.broadcasted_iota(jnp.int32, (D, LANES), 1)
    small = jnp.where(lane == 0, gain, jnp.where(lane == 1, two, 0.0))
    d_ref[:, 3 * GROUP :] = small.astype(bf16)


def back_specs(rows, at):
    heads = D // HEAD_DIM // GROUPS
    across = lambda n: pl.BlockSpec((n, GROUP), lambda i: (0, at(i)))
    weight = lambda first: pl.BlockSpec((D, GROUP), lambda i: (0, first + at(i)))
    return [
        pl.BlockSpec(memory_space=pltpu.SMEM),
        whole((rows, D)),
        pl.BlockSpec((GROUP, D), lambda i: (at(i), 3)),
        weight(0),
        weight(GROUPS),
        weight(2 * GROUPS),
        across(rows),
        across(2 * rows),
        across(2 * rows),
        across(rows),
        pl.BlockSpec((8 * heads, rows), lambda i: (at(i), 0)),
        whole((D, 2 * rows)),
    ]


def back_scratch(rows):
    return [
        pltpu.VMEM((rows, GROUP), bf16),
        pltpu.VMEM((2 * rows, GROUP), bf16),
        pltpu.VMEM((2 * rows, GROUP), bf16),
        pltpu.VMEM((LANES, rows), f32),
        pltpu.VMEM((2 * rows, LANES), f32),
        pltpu.VMEM((2 * rows, LANES), f32),
    ]


def back_cost(rows, count):
    heads = D // HEAD_DIM // GROUPS
    flops = 2 * rows * D * GROUP * 11 + 20 * rows * rows * GROUP
    return cost(count * flops, count * 40 * rows * D, count * heads * 2 * rows * rows)


def attend_back(seq, grad, weights, q, k, v, mixed, lse, normed_t, cosine, sine):
    rows = grad.shape[0]
    return pl.pallas_call(
        attend_back_body,
        grid=(GROUPS,),
        in_specs=back_specs(rows, lambda i: jnp.minimum(i, GROUPS - 2))
        + [whole(v.shape) for v in (mixed, cosine, sine)],
        out_specs=[whole((2 * rows, D)), pl.BlockSpec((D, D), lambda i: (0, i))],
        out_shape=shapes(((2 * rows, D), f32), ((D, GROUPS * D), bf16)),
        scratch_shapes=back_scratch(rows),
        compiler_params=params(36),
        cost_estimate=back_cost(rows, GROUPS - 1),
        name="attend_back",
    )(seq, grad, *[weights] * 4, q, k, v, mixed, lse, normed_t, mixed, cosine, sine)


def attend_back_last(
    seq, grad, weights, q, k, v, mixed, lse, normed_t, prev, tok, two, one, cosine, sine
):
    rows = grad.shape[0]
    extra = (prev, tok, two, one, cosine, sine)
    return pl.pallas_call(
        attend_back_last_body,
        grid=(1,),
        in_specs=back_specs(rows, lambda i: GROUPS - 1) + [whole(v.shape) for v in extra],
        out_specs=[whole((rows, D)), whole((rows, D)), whole((D, 3 * GROUP + LANES))],
        out_shape=shapes(((rows, D), bf16), ((rows, D), f32), ((D, 3 * GROUP + LANES), bf16)),
        scratch_shapes=back_scratch(rows),
        compiler_params=params(36),
        cost_estimate=back_cost(rows, 1),
        name="attend_back_last",
    )(seq, grad, *[weights] * 4, q, k, v, mixed, lse, normed_t, *extra)


def middle_back_body(
    own_ref, other_ref, x_ref, y_ref, middle_ref, grad_ref, gains_ref, mid_ref, low_ref, gain_ref
):
    rows = own_ref[...] + other_ref[...].astype(f32) + x_ref[...].astype(f32)
    rows += y_ref[...].astype(f32)
    middle = middle_ref[...]
    r = lax.rsqrt(jnp.mean(middle * middle, axis=-1, keepdims=True) + epsilon)
    hat = middle * r
    gain = jnp.sum(rows * hat, axis=0, keepdims=True)
    gain_ref[...] = jnp.broadcast_to(gain, gain_ref.shape)
    q = rows * gains_ref[1:2]
    grad = q - hat * jnp.mean(q * hat, axis=-1, keepdims=True)
    grad = grad_ref[...].astype(f32) + r * grad
    mid_ref[...] = grad
    low_ref[...] = grad.astype(bf16)


def middle_back(own, other, from_x, from_y, middle, grad, gains):
    rows = middle.shape[0]
    block = pl.BlockSpec((rows, D), lambda i: (0, 0))
    return pl.pallas_call(
        middle_back_body,
        grid=(1,),
        in_specs=[block] * 6 + [whole(gains.shape)],
        out_specs=[block, block, whole((8, D))],
        out_shape=shapes(((rows, D), f32), ((rows, D), bf16), ((8, D), f32)),
        compiler_params=params(40),
        cost_estimate=cost(20 * rows * D, 22 * rows * D),
        name="middle_back",
    )(own, other, from_x, from_y, middle, grad, gains)


def output_body(own_ref, other_ref, x_ref, y_ref, middle_ref, out_ref, sums_ref):
    ffn = own_ref[...] + other_ref[...].astype(f32) + x_ref[...].astype(f32)
    ffn += y_ref[...].astype(f32)
    out = middle_ref[...] + ffn
    out_ref[...] = out.astype(bf16)
    for i, v in enumerate((ffn, out)):
        sums_ref[i : i + 1] = jnp.sum(v * v, axis=0, keepdims=True)


def output(own, other, from_x, from_y, middle):
    rows = middle.shape[0]
    block = pl.BlockSpec((rows, D), lambda i: (0, 0))
    second = pl.BlockSpec((rows, D), lambda i: (0, 1))
    return pl.pallas_call(
        output_body,
        grid=(1,),
        in_specs=[second, second, block, block, block],
        out_specs=[block, whole((8, D))],
        out_shape=shapes(((rows, D), bf16), ((8, D), f32)),
        compiler_params=params(40),
        cost_estimate=cost(8 * rows * D, 16 * rows * D),
        name="output",
    )(own, other, from_x, from_y, middle)


def tokens_back_body(tok_ref, own_ref, returned_ref, mid_ref, gains_ref, out_ref):
    tok = tok_ref[...].astype(f32)
    r = lax.rsqrt(jnp.mean(tok * tok, axis=-1, keepdims=True) + epsilon)
    hat = tok * r
    q = (own_ref[...] + returned_ref[...].astype(f32)) * gains_ref[0:1]
    grad = q - hat * jnp.mean(q * hat, axis=-1, keepdims=True)
    out_ref[...] = (mid_ref[...] + r * grad).astype(bf16)


def tokens_back(tok, own, returned, mid, gains):
    rows = tok.shape[0]
    block = whole((rows, D))
    return pl.pallas_call(
        tokens_back_body,
        grid=(1,),
        in_specs=[block] * 4 + [whole(gains.shape)],
        out_specs=block,
        out_shape=jax.ShapeDtypeStruct((rows, D), bf16),
        compiler_params=params(40),
        cost_estimate=cost(12 * rows * D, 14 * rows * D),
        name="tokens_back",
    )(tok, own, returned, mid, gains)


def gather_columns_body(sums_ref, qkv_ref, out_ref, tail_ref):
    for i in range(GROUPS):
        at = i * D if i < GROUPS - 1 else GROUPS * D
        for part in range(3):
            to = part * D + i * GROUP
            here = at + part * GROUP
            qkv_ref[:, to : to + GROUP] = sums_ref[:, here : here + GROUP]
    out_ref[...] = sums_ref[:, (GROUPS - 1) * D : GROUPS * D]
    tail_ref[...] = sums_ref[:, (GROUPS + 1) * D :]


def gather_columns(sums):
    rows = sums.shape[0]
    return pl.pallas_call(
        gather_columns_body,
        in_specs=[whole(sums.shape)],
        out_specs=[whole((rows, n)) for n in (3 * D, D, LANES)],
        out_shape=shapes(*(((rows, n), f32) for n in (3 * D, D, LANES))),
        grid=(1,),
        name="gather_columns",
    )(sums)


def columns_back_body(pair, in_ref, out_ref):
    count, _, width = out_ref.shape
    half = width // 2
    deep = half // (8 * pair)
    for e, g, x, c, z, y in itertools.product(
        range(count), range(2), range(2), range(2), range(deep), range(2)
    ):
        to = g * half + (((x * 2 + c) * deep + z) * 2 + y) * pair
        here = ((e * 2 + g) * deep + z) * pair
        piece = in_ref[(x * 2 + y) * 2 + c, :, here : here + pair]
        out_ref[e, :, to : to + pair] = piece.astype(f32)


def rope_tables(positions):
    halfdim = HEAD_DIM // 2
    inverse = 10000.0 ** (-2.0 * jnp.arange(halfdim, dtype=f32) / HEAD_DIM)
    angles = positions.astype(f32)[:, None] * inverse[None, :]
    cosine, sine = jnp.cos(angles), jnp.sin(angles)
    times = LANES // HEAD_DIM
    return (
        jnp.tile(jnp.concatenate([cosine, cosine], axis=1), (1, times)),
        jnp.tile(jnp.concatenate([-sine, sine], axis=1), (1, times)),
    )


SPLIT = (range(0, BRANCHES),)


def columns_out(w_ffn_in):
    depth = lax.axis_size("z")
    rows, count = w_ffn_in.shape[:2]
    pair = 2 * (FF // lax.axis_size(ALL))
    cut = w_ffn_in.reshape(rows, count, 2, 2, 2, depth // 2, 2, pair)
    return cut.transpose(3, 6, 4, 0, 1, 2, 5, 7).reshape(8, rows, -1)


def columns_back(v, count):
    depth = lax.axis_size("z")
    rows = v.shape[1]
    pair = 2 * (FF // lax.axis_size(ALL))
    if pair % LANES == 0:
        out = pl.pallas_call(
            functools.partial(columns_back_body, pair),
            in_specs=[whole(v.shape)],
            out_specs=whole((count, rows, 2 * FF)),
            out_shape=jax.ShapeDtypeStruct((count, rows, 2 * FF), f32),
            grid=(1,),
            name="columns_back",
        )(v)
        return out.transpose(1, 0, 2)
    v = v[:, :, : count * depth * pair].reshape(2, 2, 2, rows, count, 2, depth // 2, pair)
    return v.astype(f32).transpose(3, 4, 5, 0, 2, 6, 1, 7).reshape(rows, count, 2 * FF)


def exchange(cut):
    return lax.all_to_all(cut, PLANE, split_axis=0, concat_axis=0, tiled=True)


def columns_in(cut):
    wide = cut.shape[-1]
    cut = cut.reshape(2, -1, wide)
    return lax.all_gather(cut, "z", axis=1, tiled=True).reshape(D, wide)


def units_in(part):
    depth = lax.axis_size("z")
    count, own = part.shape[0], part.shape[1] // depth
    part = part.reshape(count, 2, depth // 2, own, D)
    core = own_bit("c")
    kept = lax.dynamic_index_in_dim(part, core, 1, keepdims=False)
    sent = lax.dynamic_index_in_dim(part, 1 - core, 1, keepdims=False)
    other = swap(sent, "c")
    both = jnp.where(core == 0, jnp.stack([kept, other], 2), jnp.stack([other, kept], 2))
    return both.reshape(count, depth * own, D)


def units_swap(d_hid, count):
    depth = lax.axis_size("z")
    d_hid = d_hid.reshape(count, depth // 2, 2, -1, D)
    core = own_bit("c")
    kept = lax.dynamic_index_in_dim(d_hid, core, 2, keepdims=False)
    return kept, swap(lax.dynamic_index_in_dim(d_hid, 1 - core, 2, keepdims=False), "c")


def units_out(kept, other):
    count, _, own, _ = kept.shape
    low = own_bit("c") == 0
    both = jnp.where(low, jnp.stack([kept, other], 1), jnp.stack([other, kept], 1))
    return both.reshape(count, -1, D)


def on_device(
    tokens, cotangent, routes, gain_one, w_qkv, w_attn_out, gain_two, router, w_ffn_in, w_ffn_out
):
    rows = tokens.shape[1]
    own_rows = w_qkv.shape[0]
    low_tokens = tokens.reshape(rows, D)
    low_grad = cotangent.reshape(rows, D)

    cut = exchange(columns_out(w_ffn_in))
    starts = [2 * FF // 8 * branches[0] for branches in SPLIT] + [cut.shape[-1]]
    w_out = lax.all_gather(w_ffn_out.transpose(1, 0, 2), "z", axis=1, tiled=True)
    w_in = [columns_in(cut[:, :, a:b]) for a, b in zip(starts, starts[1:])]
    before = lax.ppermute(low_tokens, "x", [(i, i + 1) for i in range(lax.axis_size("x") - 1)])
    seq_index = lax.axis_index("x")
    positions = (seq_index - 1) * rows + jnp.arange(2 * rows, dtype=jnp.int32)
    cosine, sine = rope_tables(positions)
    seq = seq_index.astype(jnp.int32).reshape(1)
    route = jnp.pad(routes.reshape(rows, TOP), ((0, 0), (0, LANES - TOP))).astype(bf16)
    grad_ext = jnp.concatenate([low_grad, route], axis=1)
    small = jnp.concatenate([gain_one[:, None], gain_two[:, None], router], axis=1)
    small = jnp.pad(small, ((0, 0), (0, LANES - small.shape[1])))
    weights = gather_rows(
        jnp.concatenate([w_qkv, w_attn_out, small], axis=1), (before,), (cosine, sine, grad_ext)
    )
    gains = weights[:, 4 * D : 4 * D + 2].astype(f32).T
    router_full = jnp.pad(
        weights[:, 4 * D + 2 : 4 * D + 2 + EXPERTS], ((0, 0), (0, LANES - EXPERTS))
    )
    grad_ext = after(grad_ext, weights)
    grad_x, grad_y = swap(grad_ext, "x"), swap(grad_ext, "y")

    results = attend(seq, before, low_tokens, gains, weights, cosine, sine)
    results = after(results, grad_x, grad_y)
    normed_one, q, k, v, mixed, lse, middle, normed_two, sums = results

    half = rows // 2

    def corner(across_x, across_y):
        return swap(across_x[:half], "y"), swap(across_y[half:], "x")

    def both_cores(u):
        return (u, swap(u, "c"))

    across_x, across_y = swap(normed_two, "x"), swap(normed_two, "y")
    grad_far = corner(grad_x, grad_y)
    normed_t = normed_one.T
    w_out = units_in(after(w_out, normed_two))
    x, g = {0: both_cores(normed_two)}, {0: both_cores(grad_ext)}
    x[0] = after(x[0], normed_t)
    below, gating, d_in, d_hid = {}, {}, [], []
    for branches, columns in zip(SPLIT, w_in):
        first, last = branches[0] == 0, branches[-1] == BRANCHES - 1
        columns = jnp.concatenate([columns, router_full], axis=1)
        units = w_out[branches[0] : branches[-1] + 1]
        if not first:
            columns = after(columns, d_in, d_hid)
        kept, top = (), {}

        def run(which, kept, *moves):
            part, gate, kept = ffn(
                which, 4, branches, x[which], g[which], columns, units, kept, gating.get(which)
            )
            part, moves = after((part, moves), part[0], moves) if moves else (part, ())
            gating[which] = gate or None
            return part, kept, moves

        if first:
            part, kept, moves = run(0, kept, across_x, across_y, *grad_far)
            top[0], (across_x, across_y, *grad_far) = part, moves
            far = corner(across_x, across_y)
            x[1], g[1] = both_cores(across_x), both_cores(grad_x)
            top[1], kept, (*far, other_part) = run(1, kept, *far, swap(top[0][1], "c"))
            x[3], g[3] = both_cores(jnp.concatenate(far)), both_cores(jnp.concatenate(grad_far))
            x[2], g[2] = both_cores(across_y), both_cores(grad_y)
        else:
            top[0], kept, _ = run(0, kept)
            top[1], kept, _ = run(1, kept)
        top[3], kept, _ = run(3, kept)
        if last:
            v3 = on_chip(top[3], below.get(3))
            moves = swap(v3[:half].astype(bf16), "x"), swap(v3[half:].astype(bf16), "y")
            top[2], kept, (upper, lower) = run(2, kept, *moves)
        else:
            top[2], kept, _ = run(2, kept)
        if first:
            x_all, g_all = kept[2:]
        rows_in_all = x_all
        if last:
            v1 = on_chip(top[1], below.get(1))
            v2 = on_chip(top[2], below.get(2))
            for_x = jnp.concatenate([v1[:half], v1[half:] + lower.astype(f32)]).astype(bf16)
            for_y = jnp.concatenate([v2[:half] + upper.astype(f32), v2[half:]]).astype(bf16)
            from_x, from_y = swap(for_x[:, :D], "x"), swap(for_y[:, :D], "y")
            rows_in_all = after(x_all, for_x, for_y)
        full = contract(rows_in_all, kept[1], ((0,), (0,))).astype(bf16)
        wide = columns.shape[1] - LANES
        if last:
            full, from_x, from_y = after((full, from_x, from_y), full, from_x, from_y)
        full = full if last else full[:, :wide]
        d_in.append(full)
        d_hid.append(contract(after(kept[0], full), g_all, ((0,), (0,))).astype(bf16))
        if not last:
            below = {which: on_chip(part, below.get(which)) for which, part in top.items()}
    own_part = top[0][0]
    grad_middle, grad_attn, gain_two_sums = middle_back(
        own_part, other_part, from_x, from_y, middle, low_grad, gains
    )
    grad_attn = after(grad_attn, d_hid)
    d_cols = [
        lax.psum_scatter(u.reshape(2, D // 2, -1), "z", scatter_dimension=1, tiled=True)
        for u in d_in
    ]
    d_hid = [units_swap(u, len(branches)) for u, branches in zip(d_hid, SPLIT)]

    for_x, for_y = after((for_x, for_y), grad_attn)
    moves = swap(for_x[:, D:], "x"), swap(for_y[:, D:], "y")
    one, part = attend_back(
        seq, grad_attn, weights, q, k, v, mixed, lse, normed_t, cosine, sine
    )
    one, part, (from_x, from_y), d_hid = after((one, part, moves, d_hid), one, moves, d_hid)
    first = Scatter(part, own_rows)
    moves = first.send()
    result, squares = output(own_part, other_part, from_x, from_y, middle)
    partial_sums = jnp.concatenate([jnp.sum(sums[:3], axis=1), jnp.sum(squares[:2], axis=1)])
    first.take(moves)
    d_hid = [units_out(*u) for u in after(d_hid, first.v)]
    d_cols = [u.reshape(8, own_rows, -1) for u in d_cols]
    moves = first.send()
    early, own, part = attend_back_last(
        seq, after(grad_attn, one, partial_sums, first.v), weights, q, k, v, mixed, lse, normed_t, before,
        low_tokens, gain_two_sums, one, cosine, sine
    )
    early, own, part, moves, d_cols = after(
        (early, own, part, moves, d_cols), own, moves, d_cols, d_hid
    )
    d_w_out = [lax.psum_scatter(u, "z", scatter_dimension=1, tiled=True) for u in d_hid]
    d_w_out = [u.transpose(1, 0, 2) for u in d_w_out]
    last = Scatter(part, own_rows, partial_sums)
    last_moves = last.send()
    first.take(moves)
    returned = lax.ppermute(early, "x", [(i + 1, i) for i in range(lax.axis_size("x") - 1)])
    d_cols = [exchange(after(u, own)) for u in d_cols]
    last.take(last_moves)
    last_moves = last.send()
    last_moves, d_cols = after((last_moves, d_cols), last_moves, d_cols)
    last.take(last_moves)
    last.v = jnp.concatenate([first.v, last.v], axis=-1)
    last_moves = last.send()
    d_router = jnp.sum(d_cols[-1][:, :, -LANES : EXPERTS - LANES].astype(f32), axis=0)
    d_cols = [columns_back(u, len(b)) for u, b in zip(d_cols, SPLIT)]
    last_moves, d_cols = after((last_moves, d_cols), last_moves, d_cols)
    last.take(last_moves)
    last.finish()
    d_w_qkv, d_w_attn_out, tail = gather_columns(last.v)
    d_w_out = [u.astype(f32) for u in after(d_w_out, last.v)]
    grad_tokens = tokens_back(low_tokens, own, after(returned, last.v), grad_middle, gains)
    stats = jnp.sqrt(last.extra / (rows * lax.axis_size(ALL) * D))
    return (
        result.reshape(tokens.shape),
        grad_tokens.reshape(tokens.shape),
        tail[:, 0],
        d_w_qkv,
        d_w_attn_out,
        tail[:, 1],
        d_router,
        jnp.concatenate(d_cols, axis=1),
        jnp.concatenate(d_w_out, axis=1),
        stats,
    )


def solution(mesh):
    seq, fsdp = mesh.shape["seq"], mesh.shape["fsdp"]
    inner = Mesh(mesh.devices.reshape(seq, fsdp // 4, 2, 2), ALL)
    data = P(("z", "y", "c"), "x", None)
    weights = tuple(P(ALL, *(None,) * k) for k in (0, 1, 1, 0, 1, 2, 2))
    return jax.shard_map(
        on_device,
        mesh=inner,
        in_specs=(data, data, data) + weights,
        out_specs=(data, data) + weights + (P(),),
        check_vma=False,
    )
```

```python
import functools
import itertools
import math

import jax
import jax.numpy as jnp
from jax import lax
from jax.experimental import pallas as pl
from jax.experimental.pallas import tpu as pltpu
from jax.sharding import Mesh, PartitionSpec as P

D = 768
HEAD_DIM = 64
FF = 2048
EXPERTS = 4
BRANCHES = EXPERTS + 1
TOP = 2
BLOCK = 256
LANES = 128
GROUP = 256
GROUPS = D // GROUP

epsilon = 1e-05
f32 = jnp.float32
bf16 = jnp.bfloat16
ALL = ("x", "z", "y", "c")
PLANE = ("x", "y", "c")


def shuffle(v, axes, by):
    sizes = [lax.axis_size(axis) for axis in axes]
    pairs = []
    for at in range(math.prod(sizes)):
        rest, to, scale = at, 0, 1
        for size, flip in reversed(list(zip(sizes, by))):
            to += (rest % size ^ flip) * scale
            rest, scale = rest // size, scale * size
        pairs.append((at, to))
    return lax.ppermute(v, axes, pairs)


def swap(v, axis):
    return shuffle(v, (axis,), (1,))


def own_bit(axis, bit=0):
    return (lax.axis_index(axis) >> bit) & 1


def after(v, *deps):
    return lax.optimization_barrier((v, deps))[0]


def ordered(low, mine, other):
    return jnp.where(low, jnp.stack([mine, other]), jnp.stack([other, mine]))


def gather_axes(v, bits):
    axes = tuple(dict.fromkeys(axis for axis, _ in bits))

    def part(flips):
        by = [0] * len(axes)
        for (axis, bit), flip in zip(bits, flips):
            by[axes.index(axis)] |= flip << bit
        return shuffle(v, axes, by) if any(flips) else v

    def level(flips):
        if len(flips) == len(bits):
            return part(flips)
        low = own_bit(*bits[len(flips)]) == 0
        return ordered(low, level(flips + (0,)), level(flips + (1,)))

    return level(())


def z_bits():
    return [("z", bit) for bit in reversed(range(lax.axis_size("z").bit_length() - 1))]


def z_stages():
    bits = z_bits()
    return [bits] if len(bits) <= 2 else [[name] for name in bits]


def all_bits():
    return [("x", 0)] + z_bits() + [("y", 0), ("c", 0)]


def gather_rows(v, deps, more):
    held = []
    for bits in z_stages()[::-1] + [[("x", 0), ("y", 0)], [("c", 0)]]:
        if ("x", 0) in bits:
            v = after(v, deps)
        if ("c", 0) in bits:
            v = after(v, more)
        v = gather_axes(v, bits)
        held = bits + held
    lead = [held.index(name) for name in all_bits()]
    v = v.transpose(lead + list(range(len(lead), v.ndim)))
    return v.reshape(-1, v.shape[-1])


class Scatter:
    def __init__(self, v, rows, extra=None):
        self.names = all_bits()
        self.v = v.reshape((2,) * len(self.names) + (rows, v.shape[1]))
        self.extra = extra
        self.stages = [[("c", 0)], [("x", 0), ("y", 0)]] + z_stages()

    def block(self, flips, bits):
        v = self.v
        at = {self.names.index(name): own_bit(*name) ^ flip for name, flip in zip(bits, flips)}
        starts = [at.get(i, 0) for i in range(v.ndim)]
        sizes = [1 if i in at else v.shape[i] for i in range(v.ndim)]
        piece = lax.dynamic_slice(v, starts, sizes)
        return piece.reshape([n for i, n in enumerate(v.shape) if i not in at])

    def send(self):
        bits = self.stages[0]
        axes = tuple(dict.fromkeys(axis for axis, _ in bits))
        width = self.v.shape[-1]
        if self.extra is not None:
            count = self.extra.shape[0]
            coded, rest = [], self.extra
            for _ in range(3):
                coded.append(lax.reduce_precision(rest, 8, 7))
                rest = rest - coded[-1]
            spread = jnp.pad(jnp.concatenate(coded).astype(bf16), (width - 3 * count, 0))
            lane = jnp.arange(width) >= width - 3 * count
        moves = []
        for flips in itertools.product((0, 1), repeat=len(bits)):
            if not any(flips):
                continue
            by = [0] * len(axes)
            for (axis, bit), flip in zip(bits, flips):
                by[axes.index(axis)] |= flip << bit
            sent = self.block(flips, bits).astype(bf16)
            if self.extra is not None:
                sent = jnp.where(lane, spread, sent)
            moves.append(shuffle(sent, axes, by))
        return moves

    def take(self, moves):
        bits, self.stages = self.stages[0], self.stages[1:]
        total = self.block((0,) * len(bits), bits).astype(f32)
        for got in moves:
            got = got.astype(f32)
            total += got
            if self.extra is not None:
                count = self.extra.shape[0]
                parts = got.reshape(-1, got.shape[-1])[0, -3 * count :].reshape(3, count)
                self.extra = self.extra + (parts[0] + parts[1] + parts[2])
        self.v = total
        self.names = [name for name in self.names if name not in bits]

    def finish(self):
        while self.stages:
            self.take(self.send())


def on_chip(pair, more=None):
    v = pair[0] + swap(pair[1], "c").astype(f32)
    return v if more is None else v + more


def contract(a, b, dims):
    return lax.dot_general(a, b, (dims, ((), ())), preferred_element_type=f32)


def whole(shape):
    return pl.BlockSpec(shape, lambda *i: (0,) * len(shape))


def fixed(shape):
    return pl.BlockSpec(shape, lambda *i: (0,) * len(shape), pipeline_mode=pl.Buffered(1))


def shapes(*pairs):
    return [jax.ShapeDtypeStruct(shape, kind) for shape, kind in pairs]


def params(mib):
    return pltpu.CompilerParams(vmem_limit_bytes=mib * 2**20)


def cost(flops, moved, exps=0):
    return pl.CostEstimate(flops=flops, transcendentals=exps, bytes_accessed=moved)


def sigmoid(a):
    return 0.5 * jnp.tanh(0.5 * a) + 0.5


def ffn_body(branches, first, last, names, *refs):
    r = dict(zip(names, refs))
    win_ref, wout_ref, h_ref, p_ref = r["w_in"], r["w_out"], r["hidden"], r["pre"]
    units = wout_ref.shape[1]
    wide = len(branches) * units
    tile = h_ref.shape[0]
    step = pl.program_id(0)
    half = pl.num_programs(0) // 2
    own = step < half
    here = pl.ds(lax.rem(step, half) * tile, tile)
    x = jnp.where(own, r["xa"][here], r["xb"][here])
    g = jnp.where(own, r["ga"][here], r["gb"][here])
    lane = lax.broadcasted_iota(jnp.int32, (tile, LANES), 1)
    if first:
        r["xs"][...] = x
        r["gs"][...] = g[:, :D]
        route = g[:, D:].astype(f32).astype(jnp.int32)
        logits = contract(x, win_ref[:, 2 * wide :], ((1,), (0,)))
        one, two = lane == route[:, 0:1], lane == route[:, 1:2]
        up = jnp.sum(jnp.where(one, logits, 0.0), axis=1, keepdims=True)
        down = jnp.sum(jnp.where(two, logits, 0.0), axis=1, keepdims=True)
        top = jnp.maximum(up, down)
        up, down = jnp.exp(up - top), jnp.exp(down - top)
        total = up + down
        gates = jnp.where(one, up / total, 0.0) + jnp.where(two, down / total, 0.0)
        grad_gates = jnp.zeros_like(gates)
    else:
        gates, grad_gates = r["gates"][...], r["sums"][...]
    g = g[:, :D]
    for i, e in enumerate(branches):
        at = i * 2 * units
        pre = contract(x, win_ref[:, at : at + 2 * units], ((1,), (0,)))
        a, b = pre[:, :units], pre[:, units:]
        back = contract(g, wout_ref[i], ((1,), (1,)))
        s = sigmoid(a)
        silu = a * s
        hidden = (silu * b).astype(bf16)
        if e < EXPERTS:
            gate = gates[:, e : e + 1]
            hidden = hidden.astype(f32)
            this = jnp.sum(hidden * back, axis=1, keepdims=True)
            grad_gates = jnp.where(lane == e, this, grad_gates)
            hidden = (gate * hidden).astype(bf16)
            back = gate * back
        h_ref[:, i * units : (i + 1) * units] = hidden
        p_ref[:, at : at + units] = (back * b * (s + silu * (1.0 - s))).astype(bf16)
        p_ref[:, at + units : at + 2 * units] = (back * silu).astype(bf16)
        if last and e == EXPERTS - 1:
            inner = jnp.sum(gates * grad_gates, axis=1, keepdims=True)
            p_ref[:, 2 * wide :] = (gates * (grad_gates - inner)).astype(bf16)
    if not last:
        r["gates_out"][...] = gates
        r["sums_out"][...] = grad_gates
    tile_ref = r["tile"]
    deep = p_ref.shape[1]
    out = contract(h_ref[...], wout_ref[...].reshape(wide, D), ((1,), (0,)))
    tile_ref[:, D:] = out
    for at in range(0, D, GROUP):
        cols = slice(at, at + GROUP)
        tile_ref[:, cols] = contract(p_ref[...], win_ref[cols, :deep], ((1,), (1,)))

    @pl.when(own)
    def _():
        r["own"][here] = tile_ref[...]

    @pl.when(jnp.logical_not(own))
    def _():
        r["other"][here] = tile_ref[...].astype(bf16)


def ffn(part, parts, branches, x, g, w_in, w_out, kept, gating=None):
    first, last = gating is None, branches[-1] == BRANCHES - 1
    rows = x[0].shape[0]
    tile = min(256, rows)
    steps = rows // tile
    wide = w_in.shape[1] - LANES
    total = parts * 2 * rows
    here = lambda width: pl.BlockSpec((tile, width), lambda i: (i, 0))
    there = lambda width: pl.BlockSpec((tile, width), lambda i: (2 * part * steps + i, 0))
    ins = list(zip(("xa", "xb", "ga", "gb", "w_in", "w_out"), (*x, *g, w_in, w_out)))
    specs = [fixed(v.shape) for _, v in ins]
    if not first:
        ins += list(zip(("gates", "sums"), gating))
        specs += [here(LANES)] * 2
    outs = [("own", (rows, 2 * D), f32, whole((rows, 2 * D)))]
    outs += [("other", (rows, 2 * D), bf16, whole((rows, 2 * D)))]
    if not last:
        outs += [(n, (2 * rows, LANES), f32, here(LANES)) for n in ("gates_out", "sums_out")]
    at = len(outs)
    widths = [("hidden", wide // 2), ("pre", wide + last * LANES)]
    if first:
        widths += [("xs", D), ("gs", D)]
    outs += [(n, (total, width), bf16, there(width)) for n, width in widths]
    names = [n for n, _ in ins] + ["old"] * len(kept) + [n for n, *_ in outs] + ["tile"]
    results = pl.pallas_call(
        functools.partial(ffn_body, branches, first, last, names),
        grid=(2 * steps,),
        in_specs=specs + [pl.BlockSpec(memory_space=pl.ANY)] * len(kept),
        out_specs=[spec for *_, spec in outs],
        out_shape=shapes(*((shape, kind) for _, shape, kind, _ in outs)),
        scratch_shapes=[pltpu.VMEM((tile, 2 * D), f32)],
        input_output_aliases={len(ins) + i: at + i for i in range(len(kept))},
        compiler_params=params(30),
        cost_estimate=cost(
            12 * rows * D * wide, 3 * w_in.size + rows * (20 * D + 6 * wide), rows * wide
        ),
        name="ffn",
    )(*(v for _, v in ins), *kept)
    return results[:2], results[2:at], results[at:]


def half_turn(v):
    lane = lax.broadcasted_iota(jnp.int32, v.shape, 1)
    low = lane % HEAD_DIM < HEAD_DIM // 2
    return jnp.where(low, pltpu.roll(v, 128 - HEAD_DIM // 2, 1), pltpu.roll(v, HEAD_DIM // 2, 1))


def rope(v, cosine, sine):
    parts = [v[:, at : at + LANES] for at in range(0, v.shape[1], LANES)]
    return jnp.concatenate([p * cosine + half_turn(p) * sine for p in parts], axis=1)


def one_head(v, j):
    lane = lax.broadcasted_iota(jnp.int32, v.shape, 1)
    return jnp.where(lane // HEAD_DIM == j, v, jnp.zeros_like(v))


def normal(rows_in):
    return rows_in * lax.rsqrt(jnp.mean(rows_in * rows_in, axis=-1, keepdims=True) + epsilon)


def row_of(column):
    return jnp.broadcast_to(column, (column.shape[0], LANES)).T[:8]


def attend_body(
    seq_ref, prev_ref, tok_ref, gains_ref, wq_ref, wk_ref, wv_ref, wo_ref, cos_ref, sin_ref,
    normed_ref, q_ref, k_ref, v_ref, mixed_ref, lse_ref, middle_ref, two_ref, sums_ref, acc_ref,
):
    step = pl.program_id(0)
    rows = tok_ref.shape[0]

    @pl.when(step == 0)
    def _():
        for at, ref in ((0, prev_ref), (rows, tok_ref)):
            hat = normal(ref[...].astype(f32))
            normed_ref[at : at + rows] = (hat * gains_ref[0:1]).astype(bf16)

    x = normed_ref[...]
    cosine, sine = cos_ref[...], sin_ref[...]
    own_cos, own_sin = cosine[rows:], sine[rows:]
    q = contract(x[rows:], wq_ref[...], ((1,), (0,)))
    q_ref[...] = (rope(q, own_cos, own_sin) * 0.125).astype(bf16)
    k_ref[...] = rope(contract(x, wk_ref[...], ((1,), (0,))), cosine, sine).astype(bf16)
    v_ref[...] = contract(x, wv_ref[...], ((1,), (0,))).astype(bf16)
    skip = jnp.where(seq_ref[0] > 0, 0.0, 1e30)
    for at in range(0, GROUP, LANES):
        cols = slice(at, at + LANES)
        for top in range(0, rows, BLOCK):
            mixed = jnp.zeros((BLOCK, LANES), f32)
            ends = rows + top + BLOCK
            for j in range(LANES // HEAD_DIM):
                query = one_head(q_ref[top : top + BLOCK, cols], j)
                far = contract(query, k_ref[:rows, cols], ((1,), (1,)))
                near = contract(query, k_ref[rows:ends, cols], ((1,), (1,)))
                peak = jnp.maximum(
                    jnp.max(far, axis=1, keepdims=True) - skip, jnp.max(near, axis=1, keepdims=True)
                )
                far, near = jnp.exp(far - (peak + skip)), jnp.exp(near - peak)
                total = jnp.sum(far, axis=1, keepdims=True) + jnp.sum(near, axis=1, keepdims=True)
                both = contract(far.astype(bf16), one_head(v_ref[:rows, cols], j), ((1,), (0,)))
                both += contract(near.astype(bf16), one_head(v_ref[rows:ends, cols], j), ((1,), (0,)))
                mixed += both / total
                head = (at // HEAD_DIM + j) * 8
                lse_ref[head : head + 8, top : top + BLOCK] = row_of(peak + jnp.log(total))
            mixed_ref[top : top + BLOCK, cols] = mixed.astype(bf16)
    piece = contract(mixed_ref[...], wo_ref[...], ((1,), (0,)))

    @pl.when(step == 0)
    def _():
        acc_ref[...] = piece

    @pl.when(step > 0)
    def _():
        acc_ref[...] += piece

    @pl.when(step == GROUPS - 1)
    def _():
        attn = acc_ref[...]
        tok = tok_ref[...].astype(f32)
        middle = tok + attn
        middle_ref[...] = middle
        two_ref[...] = (normal(middle) * gains_ref[1:2]).astype(bf16)
        for i, v in enumerate((tok, attn, middle)):
            sums_ref[i : i + 1] = jnp.sum(v * v, axis=0, keepdims=True)


def attend(seq, prev, tok, gains, weights, cosine, sine):
    rows = tok.shape[0]
    heads = D // HEAD_DIM
    across = lambda n: pl.BlockSpec((n, GROUP), lambda i: (0, i))
    weight = lambda first: pl.BlockSpec((D, GROUP), lambda i: (0, first + i))
    return pl.pallas_call(
        attend_body,
        grid=(GROUPS,),
        in_specs=[
            pl.BlockSpec(memory_space=pltpu.SMEM),
            whole(prev.shape),
            whole(tok.shape),
            whole(gains.shape),
            weight(0),
            weight(GROUPS),
            weight(2 * GROUPS),
            pl.BlockSpec((GROUP, D), lambda i: (i, 3)),
            whole(cosine.shape),
            whole(sine.shape),
        ],
        out_specs=[
            whole((2 * rows, D)),
            across(rows),
            across(2 * rows),
            across(2 * rows),
            across(rows),
            pl.BlockSpec((8 * heads // GROUPS, rows), lambda i: (i, 0)),
            whole((rows, D)),
            whole((rows, D)),
            whole((8, D)),
        ],
        out_shape=shapes(
            ((2 * rows, D), bf16),
            ((rows, D), bf16),
            ((2 * rows, D), bf16),
            ((2 * rows, D), bf16),
            ((rows, D), bf16),
            ((8 * heads, rows), f32),
            ((rows, D), f32),
            ((rows, D), bf16),
            ((8, D), f32),
        ),
        scratch_shapes=[pltpu.VMEM((rows, D), f32)],
        compiler_params=params(36),
        cost_estimate=cost(
            2 * rows * D * D * 6 + 8 * rows * rows * D, 8 * D * D + 20 * rows * D, heads * 2 * rows * rows
        ),
        name="attend",
    )(seq, prev, tok, gains, *[weights] * 4, cosine, sine)


def heads_back(
    skip, grad, wo_ref, q_ref, k_ref, v_ref, mixed_ref, lse_ref, cos_ref, sin_ref, gq_ref, gk_ref,
    gv_ref, dqt_ref, dk_ref, dv_ref,
):
    rows = grad.shape[0]
    cosine, sine = cos_ref[...], sin_ref[...]
    grad_mixed = contract(grad, wo_ref[...], ((1,), (1,))).astype(bf16)
    for at in range(0, GROUP, LANES):
        cols = slice(at, at + LANES)
        key, value = k_ref[:, cols], v_ref[:, cols]
        key_t = key.T
        products = grad_mixed[:, cols].astype(f32) * mixed_ref[:, cols].astype(f32)
        for j in range(LANES // HEAD_DIM):
            head = (at // HEAD_DIM + j) * 8
            keep = lax.broadcasted_iota(jnp.int32, key_t.shape, 0) // HEAD_DIM == j
            key_j = jnp.where(keep, key_t, jnp.zeros_like(key_t))
            for top in range(0, rows, BLOCK):
                block = slice(top, top + BLOCK)
                query = one_head(q_ref[block, cols], j)
                back = one_head(grad_mixed[block, cols], j)
                delta = row_of(
                    jnp.sum(one_head(products[block], j), axis=1, keepdims=True)
                )[0:1]
                lse = lse_ref[head : head + 1, block]
                for begin, end, less in ((0, rows, lse + skip), (rows, rows + top + BLOCK, lse)):
                    probs = jnp.exp(contract(key[begin:end], query, ((1,), (1,))) - less)
                    above = contract(value[begin:end], back, ((1,), (1,))) - delta
                    scores = (probs * above).astype(bf16)
                    grad_v = contract(probs.astype(bf16), back, ((1,), (0,)))
                    grad_k = contract(scores, query, ((1,), (0,)))
                    grad_q = contract(key_j[:, begin:end], scores, ((1,), (0,)))
                    if j == 0 and top == 0:
                        dv_ref[begin:end], dk_ref[begin:end] = grad_v, grad_k
                        if rows < end < 2 * rows:
                            rest = jnp.zeros((2 * rows - end, LANES), f32)
                            dv_ref[end:], dk_ref[end:] = rest, rest
                    else:
                        dv_ref[begin:end] += grad_v
                        dk_ref[begin:end] += grad_k
                    if j == 0 and begin == 0:
                        dqt_ref[:, block] = grad_q
                    else:
                        dqt_ref[:, block] += grad_q
        own_cos, own_sin = cosine[rows:], sine[rows:]
        gq_ref[:, cols] = (rope(dqt_ref[...].T, own_cos, -own_sin) * 0.125).astype(bf16)
        gk_ref[:, cols] = rope(dk_ref[...], cosine, -sine).astype(bf16)
        gv_ref[:, cols] = dv_ref[...].astype(bf16)


def group_sums(normed, gq, gk, gv, wq_ref, wk_ref, wv_ref):
    rows = gq.shape[0]
    one = contract(gk, wk_ref[...], ((1,), (1,))) + contract(gv, wv_ref[...], ((1,), (1,)))
    own = one[rows:] + contract(gq, wq_ref[...], ((1,), (1,)))
    parts = ((normed[:, rows:], gq), (normed, gk), (normed, gv))
    return one[:rows], own, [contract(a, b, ((1,), (0,))).astype(bf16) for a, b in parts]


def attend_back_body(
    seq_ref, grad_ref, wo_ref, wq_ref, wk_ref, wv_ref, q_ref, k_ref, v_ref, mixed_ref, lse_ref,
    normed_ref, all_ref, cos_ref, sin_ref, one_ref, d_ref, *scratch,
):
    step = pl.program_id(0)
    rows = grad_ref.shape[0]

    @pl.when(step < GROUPS - 1)
    def _():
        skip = jnp.where(seq_ref[0] > 0, 0.0, 1e30)
        heads_back(
            skip, grad_ref[...], wo_ref, q_ref, k_ref, v_ref, mixed_ref, lse_ref, cos_ref, sin_ref,
            *scratch,
        )
        gq, gk, gv = (ref[...] for ref in scratch[:3])
        early, own, parts = group_sums(normed_ref[...], gq, gk, gv, wq_ref, wk_ref, wv_ref)
        for i, part in enumerate(parts):
            d_ref[:, i * GROUP : (i + 1) * GROUP] = part

        @pl.when(step == 0)
        def _():
            one_ref[:rows], one_ref[rows:] = early, own

        @pl.when(step > 0)
        def _():
            one_ref[:rows] += early
            one_ref[rows:] += own

    @pl.when(step == GROUPS - 1)
    def _():
        d_ref[...] = contract(all_ref[...], grad_ref[...], ((0,), (0,))).astype(bf16)


def attend_back_last_body(
    seq_ref, grad_ref, wo_ref, wq_ref, wk_ref, wv_ref, q_ref, k_ref, v_ref, mixed_ref, lse_ref,
    normed_ref, prev_ref, tok_ref, two_ref, one_ref, cos_ref, sin_ref, early_ref,
    own_ref, d_ref, *scratch,
):
    rows = grad_ref.shape[0]
    skip = jnp.where(seq_ref[0] > 0, 0.0, 1e30)
    heads_back(
        skip, grad_ref[...], wo_ref, q_ref, k_ref, v_ref, mixed_ref, lse_ref, cos_ref, sin_ref,
        *scratch,
    )
    gq, gk, gv = (ref[...] for ref in scratch[:3])
    early, own, parts = group_sums(normed_ref[...], gq, gk, gv, wq_ref, wk_ref, wv_ref)
    for i, part in enumerate(parts):
        d_ref[:, i * GROUP : (i + 1) * GROUP] = part
    early, own = early + one_ref[:rows], own + one_ref[rows:]
    early_ref[...] = early.astype(bf16)
    own_ref[...] = own
    gain = jnp.sum(early * normal(prev_ref[...].astype(f32)), axis=0, keepdims=True)
    gain += jnp.sum(own * normal(tok_ref[...].astype(f32)), axis=0, keepdims=True)
    gain = jnp.broadcast_to(gain, (LANES, D)).T
    two = jnp.broadcast_to(two_ref[0:1], (LANES, D)).T
    lane = lax.broadcasted_iota(jnp.int32, (D, LANES), 1)
    small = jnp.where(lane == 0, gain, jnp.where(lane == 1, two, 0.0))
    d_ref[:, 3 * GROUP :] = small.astype(bf16)


def back_specs(rows, at):
    heads = D // HEAD_DIM // GROUPS
    across = lambda n: pl.BlockSpec((n, GROUP), lambda i: (0, at(i)))
    weight = lambda first: pl.BlockSpec((D, GROUP), lambda i: (0, first + at(i)))
    return [
        pl.BlockSpec(memory_space=pltpu.SMEM),
        whole((rows, D)),
        pl.BlockSpec((GROUP, D), lambda i: (at(i), 3)),
        weight(0),
        weight(GROUPS),
        weight(2 * GROUPS),
        across(rows),
        across(2 * rows),
        across(2 * rows),
        across(rows),
        pl.BlockSpec((8 * heads, rows), lambda i: (at(i), 0)),
        whole((D, 2 * rows)),
    ]


def back_scratch(rows):
    return [
        pltpu.VMEM((rows, GROUP), bf16),
        pltpu.VMEM((2 * rows, GROUP), bf16),
        pltpu.VMEM((2 * rows, GROUP), bf16),
        pltpu.VMEM((LANES, rows), f32),
        pltpu.VMEM((2 * rows, LANES), f32),
        pltpu.VMEM((2 * rows, LANES), f32),
    ]


def back_cost(rows, count):
    heads = D // HEAD_DIM // GROUPS
    flops = 2 * rows * D * GROUP * 11 + 20 * rows * rows * GROUP
    return cost(count * flops, count * 40 * rows * D, count * heads * 2 * rows * rows)


def attend_back(seq, grad, weights, q, k, v, mixed, lse, normed_t, cosine, sine):
    rows = grad.shape[0]
    return pl.pallas_call(
        attend_back_body,
        grid=(GROUPS,),
        in_specs=back_specs(rows, lambda i: jnp.minimum(i, GROUPS - 2))
        + [whole(v.shape) for v in (mixed, cosine, sine)],
        out_specs=[whole((2 * rows, D)), pl.BlockSpec((D, D), lambda i: (0, i))],
        out_shape=shapes(((2 * rows, D), f32), ((D, GROUPS * D), bf16)),
        scratch_shapes=back_scratch(rows),
        compiler_params=params(36),
        cost_estimate=back_cost(rows, GROUPS - 1),
        name="attend_back",
    )(seq, grad, *[weights] * 4, q, k, v, mixed, lse, normed_t, mixed, cosine, sine)


def attend_back_last(
    seq, grad, weights, q, k, v, mixed, lse, normed_t, prev, tok, two, one, cosine, sine
):
    rows = grad.shape[0]
    extra = (prev, tok, two, one, cosine, sine)
    return pl.pallas_call(
        attend_back_last_body,
        grid=(1,),
        in_specs=back_specs(rows, lambda i: GROUPS - 1) + [whole(v.shape) for v in extra],
        out_specs=[whole((rows, D)), whole((rows, D)), whole((D, 3 * GROUP + LANES))],
        out_shape=shapes(((rows, D), bf16), ((rows, D), f32), ((D, 3 * GROUP + LANES), bf16)),
        scratch_shapes=back_scratch(rows),
        compiler_params=params(36),
        cost_estimate=back_cost(rows, 1),
        name="attend_back_last",
    )(seq, grad, *[weights] * 4, q, k, v, mixed, lse, normed_t, *extra)


def middle_back_body(
    own_ref, other_ref, x_ref, y_ref, middle_ref, grad_ref, gains_ref, mid_ref, low_ref, gain_ref
):
    rows = own_ref[...] + other_ref[...].astype(f32) + x_ref[...].astype(f32)
    rows += y_ref[...].astype(f32)
    middle = middle_ref[...]
    r = lax.rsqrt(jnp.mean(middle * middle, axis=-1, keepdims=True) + epsilon)
    hat = middle * r
    gain = jnp.sum(rows * hat, axis=0, keepdims=True)
    gain_ref[...] = jnp.broadcast_to(gain, gain_ref.shape)
    q = rows * gains_ref[1:2]
    grad = q - hat * jnp.mean(q * hat, axis=-1, keepdims=True)
    grad = grad_ref[...].astype(f32) + r * grad
    mid_ref[...] = grad
    low_ref[...] = grad.astype(bf16)


def middle_back(own, other, from_x, from_y, middle, grad, gains):
    rows = middle.shape[0]
    block = pl.BlockSpec((rows, D), lambda i: (0, 0))
    return pl.pallas_call(
        middle_back_body,
        grid=(1,),
        in_specs=[block] * 6 + [whole(gains.shape)],
        out_specs=[block, block, whole((8, D))],
        out_shape=shapes(((rows, D), f32), ((rows, D), bf16), ((8, D), f32)),
        compiler_params=params(40),
        cost_estimate=cost(20 * rows * D, 22 * rows * D),
        name="middle_back",
    )(own, other, from_x, from_y, middle, grad, gains)


def output_body(own_ref, other_ref, x_ref, y_ref, middle_ref, out_ref, sums_ref):
    ffn = own_ref[...] + other_ref[...].astype(f32) + x_ref[...].astype(f32)
    ffn += y_ref[...].astype(f32)
    out = middle_ref[...] + ffn
    out_ref[...] = out.astype(bf16)
    for i, v in enumerate((ffn, out)):
        sums_ref[i : i + 1] = jnp.sum(v * v, axis=0, keepdims=True)


def output(own, other, from_x, from_y, middle):
    rows = middle.shape[0]
    block = pl.BlockSpec((rows, D), lambda i: (0, 0))
    second = pl.BlockSpec((rows, D), lambda i: (0, 1))
    return pl.pallas_call(
        output_body,
        grid=(1,),
        in_specs=[second, second, block, block, block],
        out_specs=[block, whole((8, D))],
        out_shape=shapes(((rows, D), bf16), ((8, D), f32)),
        compiler_params=params(40),
        cost_estimate=cost(8 * rows * D, 16 * rows * D),
        name="output",
    )(own, other, from_x, from_y, middle)


def tokens_back_body(tok_ref, own_ref, returned_ref, mid_ref, gains_ref, out_ref):
    tok = tok_ref[...].astype(f32)
    r = lax.rsqrt(jnp.mean(tok * tok, axis=-1, keepdims=True) + epsilon)
    hat = tok * r
    q = (own_ref[...] + returned_ref[...].astype(f32)) * gains_ref[0:1]
    grad = q - hat * jnp.mean(q * hat, axis=-1, keepdims=True)
    out_ref[...] = (mid_ref[...] + r * grad).astype(bf16)


def tokens_back(tok, own, returned, mid, gains):
    rows = tok.shape[0]
    block = whole((rows, D))
    return pl.pallas_call(
        tokens_back_body,
        grid=(1,),
        in_specs=[block] * 4 + [whole(gains.shape)],
        out_specs=block,
        out_shape=jax.ShapeDtypeStruct((rows, D), bf16),
        compiler_params=params(40),
        cost_estimate=cost(12 * rows * D, 14 * rows * D),
        name="tokens_back",
    )(tok, own, returned, mid, gains)


def gather_columns_body(sums_ref, qkv_ref, out_ref, tail_ref):
    for i in range(GROUPS):
        at = i * D if i < GROUPS - 1 else GROUPS * D
        for part in range(3):
            to = part * D + i * GROUP
            here = at + part * GROUP
            qkv_ref[:, to : to + GROUP] = sums_ref[:, here : here + GROUP]
    out_ref[...] = sums_ref[:, (GROUPS - 1) * D : GROUPS * D]
    tail_ref[...] = sums_ref[:, (GROUPS + 1) * D :]


def gather_columns(sums):
    rows = sums.shape[0]
    return pl.pallas_call(
        gather_columns_body,
        in_specs=[whole(sums.shape)],
        out_specs=[whole((rows, n)) for n in (3 * D, D, LANES)],
        out_shape=shapes(*(((rows, n), f32) for n in (3 * D, D, LANES))),
        grid=(1,),
        name="gather_columns",
    )(sums)


def columns_back_body(pair, in_ref, out_ref):
    count, _, width = out_ref.shape
    half = width // 2
    deep = half // (8 * pair)
    for e, g, x, c, z, y in itertools.product(
        range(count), range(2), range(2), range(2), range(deep), range(2)
    ):
        to = g * half + (((x * 2 + c) * deep + z) * 2 + y) * pair
        here = ((e * 2 + g) * deep + z) * pair
        piece = in_ref[(x * 2 + y) * 2 + c, :, here : here + pair]
        out_ref[e, :, to : to + pair] = piece.astype(f32)


def rope_tables(positions):
    halfdim = HEAD_DIM // 2
    inverse = 10000.0 ** (-2.0 * jnp.arange(halfdim, dtype=f32) / HEAD_DIM)
    angles = positions.astype(f32)[:, None] * inverse[None, :]
    cosine, sine = jnp.cos(angles), jnp.sin(angles)
    times = LANES // HEAD_DIM
    return (
        jnp.tile(jnp.concatenate([cosine, cosine], axis=1), (1, times)),
        jnp.tile(jnp.concatenate([-sine, sine], axis=1), (1, times)),
    )


SPLIT = (range(0, BRANCHES),)


def columns_out(w_ffn_in):
    depth = lax.axis_size("z")
    rows, count = w_ffn_in.shape[:2]
    pair = 2 * (FF // lax.axis_size(ALL))
    cut = w_ffn_in.reshape(rows, count, 2, 2, 2, depth // 2, 2, pair)
    return cut.transpose(3, 6, 4, 0, 1, 2, 5, 7).reshape(8, rows, -1)


def columns_back(v, count):
    depth = lax.axis_size("z")
    rows = v.shape[1]
    pair = 2 * (FF // lax.axis_size(ALL))
    if pair % LANES == 0:
        out = pl.pallas_call(
            functools.partial(columns_back_body, pair),
            in_specs=[whole(v.shape)],
            out_specs=whole((count, rows, 2 * FF)),
            out_shape=jax.ShapeDtypeStruct((count, rows, 2 * FF), f32),
            grid=(1,),
            name="columns_back",
        )(v)
        return out.transpose(1, 0, 2)
    v = v[:, :, : count * depth * pair].reshape(2, 2, 2, rows, count, 2, depth // 2, pair)
    return v.astype(f32).transpose(3, 4, 5, 0, 2, 6, 1, 7).reshape(rows, count, 2 * FF)


def exchange(cut):
    return lax.all_to_all(cut, PLANE, split_axis=0, concat_axis=0, tiled=True)


def columns_in(cut):
    wide = cut.shape[-1]
    cut = cut.reshape(2, -1, wide)
    return lax.all_gather(cut, "z", axis=1, tiled=True).reshape(D, wide)


def units_in(part):
    depth = lax.axis_size("z")
    count, own = part.shape[0], part.shape[1] // depth
    part = part.reshape(count, 2, depth // 2, own, D)
    core = own_bit("c")
    kept = lax.dynamic_index_in_dim(part, core, 1, keepdims=False)
    sent = lax.dynamic_index_in_dim(part, 1 - core, 1, keepdims=False)
    other = swap(sent, "c")
    both = jnp.where(core == 0, jnp.stack([kept, other], 2), jnp.stack([other, kept], 2))
    return both.reshape(count, depth * own, D)


def units_swap(d_hid, count):
    depth = lax.axis_size("z")
    d_hid = d_hid.reshape(count, depth // 2, 2, -1, D)
    core = own_bit("c")
    kept = lax.dynamic_index_in_dim(d_hid, core, 2, keepdims=False)
    return kept, swap(lax.dynamic_index_in_dim(d_hid, 1 - core, 2, keepdims=False), "c")


def units_out(kept, other):
    count, _, own, _ = kept.shape
    low = own_bit("c") == 0
    both = jnp.where(low, jnp.stack([kept, other], 1), jnp.stack([other, kept], 1))
    return both.reshape(count, -1, D)


def on_device(
    tokens, cotangent, routes, gain_one, w_qkv, w_attn_out, gain_two, router, w_ffn_in, w_ffn_out
):
    rows = tokens.shape[1]
    own_rows = w_qkv.shape[0]
    low_tokens = tokens.reshape(rows, D)
    low_grad = cotangent.reshape(rows, D)

    cut = exchange(columns_out(w_ffn_in))
    starts = [2 * FF // 8 * branches[0] for branches in SPLIT] + [cut.shape[-1]]
    w_out = lax.all_gather(w_ffn_out.transpose(1, 0, 2), "z", axis=1, tiled=True)
    w_in = [columns_in(cut[:, :, a:b]) for a, b in zip(starts, starts[1:])]
    before = lax.ppermute(low_tokens, "x", [(i, i + 1) for i in range(lax.axis_size("x") - 1)])
    seq_index = lax.axis_index("x")
    positions = (seq_index - 1) * rows + jnp.arange(2 * rows, dtype=jnp.int32)
    cosine, sine = rope_tables(positions)
    seq = seq_index.astype(jnp.int32).reshape(1)
    route = jnp.pad(routes.reshape(rows, TOP), ((0, 0), (0, LANES - TOP))).astype(bf16)
    grad_ext = jnp.concatenate([low_grad, route], axis=1)
    small = jnp.concatenate([gain_one[:, None], gain_two[:, None], router], axis=1)
    small = jnp.pad(small, ((0, 0), (0, LANES - small.shape[1])))
    weights = gather_rows(
        jnp.concatenate([w_qkv, w_attn_out, small], axis=1), (before,), (cosine, sine, grad_ext)
    )
    gains = weights[:, 4 * D : 4 * D + 2].astype(f32).T
    router_full = jnp.pad(
        weights[:, 4 * D + 2 : 4 * D + 2 + EXPERTS], ((0, 0), (0, LANES - EXPERTS))
    )
    grad_ext = after(grad_ext, weights)
    grad_x, grad_y = swap(grad_ext, "x"), swap(grad_ext, "y")

    results = attend(seq, before, low_tokens, gains, weights, cosine, sine)
    results = after(results, grad_x, grad_y)
    normed_one, q, k, v, mixed, lse, middle, normed_two, sums = results

    half = rows // 2

    def corner(across_x, across_y):
        return swap(across_x[:half], "y"), swap(across_y[half:], "x")

    def both_cores(u):
        return (u, swap(u, "c"))

    across_x, across_y = swap(normed_two, "x"), swap(normed_two, "y")
    grad_far = corner(grad_x, grad_y)
    normed_t = normed_one.T
    w_out = units_in(after(w_out, normed_two))
    x, g = {0: both_cores(normed_two)}, {0: both_cores(grad_ext)}
    x[0] = after(x[0], normed_t)
    below, gating, d_in, d_hid = {}, {}, [], []
    for branches, columns in zip(SPLIT, w_in):
        first, last = branches[0] == 0, branches[-1] == BRANCHES - 1
        columns = jnp.concatenate([columns, router_full], axis=1)
        units = w_out[branches[0] : branches[-1] + 1]
        if not first:
            columns = after(columns, d_in, d_hid)
        kept, top = (), {}

        def run(which, kept, *moves):
            part, gate, kept = ffn(
                which, 4, branches, x[which], g[which], columns, units, kept, gating.get(which)
            )
            part, moves = after((part, moves), part[0], moves) if moves else (part, ())
            gating[which] = gate or None
            return part, kept, moves

        if first:
            part, kept, moves = run(0, kept, across_x, across_y, *grad_far)
            top[0], (across_x, across_y, *grad_far) = part, moves
            far = corner(across_x, across_y)
            x[1], g[1] = both_cores(across_x), both_cores(grad_x)
            top[1], kept, (*far, other_part) = run(1, kept, *far, swap(top[0][1], "c"))
            x[3], g[3] = both_cores(jnp.concatenate(far)), both_cores(jnp.concatenate(grad_far))
            x[2], g[2] = both_cores(across_y), both_cores(grad_y)
        else:
            top[0], kept, _ = run(0, kept)
            top[1], kept, _ = run(1, kept)
        top[3], kept, _ = run(3, kept)
        if last:
            v3 = on_chip(top[3], below.get(3))
            moves = swap(v3[:half].astype(bf16), "x"), swap(v3[half:].astype(bf16), "y")
            top[2], kept, (upper, lower) = run(2, kept, *moves)
        else:
            top[2], kept, _ = run(2, kept)
        if first:
            x_all, g_all = kept[2:]
        rows_in_all = x_all
        if last:
            v1 = on_chip(top[1], below.get(1))
            v2 = on_chip(top[2], below.get(2))
            for_x = jnp.concatenate([v1[:half], v1[half:] + lower.astype(f32)]).astype(bf16)
            for_y = jnp.concatenate([v2[:half] + upper.astype(f32), v2[half:]]).astype(bf16)
            from_x, from_y = swap(for_x[:, :D], "x"), swap(for_y[:, :D], "y")
            rows_in_all = after(x_all, for_x, for_y)
        full = contract(rows_in_all, kept[1], ((0,), (0,))).astype(bf16)
        wide = columns.shape[1] - LANES
        if last:
            full, from_x, from_y = after((full, from_x, from_y), full, from_x, from_y)
        full = full if last else full[:, :wide]
        d_in.append(full)
        d_hid.append(contract(after(kept[0], full), g_all, ((0,), (0,))).astype(bf16))
        if not last:
            below = {which: on_chip(part, below.get(which)) for which, part in top.items()}
    own_part = top[0][0]
    grad_middle, grad_attn, gain_two_sums = middle_back(
        own_part, other_part, from_x, from_y, middle, low_grad, gains
    )
    grad_attn = after(grad_attn, d_hid)
    d_cols = [
        lax.psum_scatter(u.reshape(2, D // 2, -1), "z", scatter_dimension=1, tiled=True)
        for u in d_in
    ]
    d_hid = [units_swap(u, len(branches)) for u, branches in zip(d_hid, SPLIT)]

    for_x, for_y = after((for_x, for_y), grad_attn)
    moves = swap(for_x[:, D:], "x"), swap(for_y[:, D:], "y")
    one, part = attend_back(
        seq, grad_attn, weights, q, k, v, mixed, lse, normed_t, cosine, sine
    )
    one, part, (from_x, from_y), d_hid = after((one, part, moves, d_hid), one, moves, d_hid)
    first = Scatter(part, own_rows)
    moves = first.send()
    result, squares = output(own_part, other_part, from_x, from_y, middle)
    partial_sums = jnp.concatenate([jnp.sum(sums[:3], axis=1), jnp.sum(squares[:2], axis=1)])
    first.take(moves)
    d_hid = [units_out(*u) for u in after(d_hid, first.v)]
    d_cols = [u.reshape(8, own_rows, -1) for u in d_cols]
    moves = first.send()
    early, own, part = attend_back_last(
        seq, after(grad_attn, one, partial_sums, first.v), weights, q, k, v, mixed, lse, normed_t, before,
        low_tokens, gain_two_sums, one, cosine, sine
    )
    early, own, part, moves, d_cols = after(
        (early, own, part, moves, d_cols), own, moves, d_cols, d_hid
    )
    d_w_out = [lax.psum_scatter(u, "z", scatter_dimension=1, tiled=True) for u in d_hid]
    d_w_out = [u.transpose(1, 0, 2) for u in d_w_out]
    last = Scatter(part, own_rows, partial_sums)
    last_moves = last.send()
    first.take(moves)
    returned = lax.ppermute(early, "x", [(i + 1, i) for i in range(lax.axis_size("x") - 1)])
    last.take(last_moves)
    last_moves = last.send()
    last.take(last_moves)
    d_cols = [exchange(after(u, last.v)) for u in d_cols]
    last.v = jnp.concatenate([first.v, last.v], axis=-1)
    last_moves = last.send()
    d_router = jnp.sum(d_cols[-1][:, :, -LANES : EXPERTS - LANES].astype(f32), axis=0)
    d_cols = [columns_back(u, len(b)) for u, b in zip(d_cols, SPLIT)]
    last_moves, d_cols = after((last_moves, d_cols), last_moves, d_cols)
    last.take(last_moves)
    last.finish()
    d_w_qkv, d_w_attn_out, tail = gather_columns(last.v)
    d_w_out = [u.astype(f32) for u in after(d_w_out, last.v)]
    grad_tokens = tokens_back(low_tokens, own, after(returned, last.v), grad_middle, gains)
    stats = jnp.sqrt(last.extra / (rows * lax.axis_size(ALL) * D))
    return (
        result.reshape(tokens.shape),
        grad_tokens.reshape(tokens.shape),
        tail[:, 0],
        d_w_qkv,
        d_w_attn_out,
        tail[:, 1],
        d_router,
        jnp.concatenate(d_cols, axis=1),
        jnp.concatenate(d_w_out, axis=1),
        stats,
    )


def solution(mesh):
    seq, fsdp = mesh.shape["seq"], mesh.shape["fsdp"]
    inner = Mesh(mesh.devices.reshape(seq, fsdp // 4, 2, 2), ALL)
    data = P(("z", "y", "c"), "x", None)
    weights = tuple(P(ALL, *(None,) * k) for k in (0, 1, 1, 0, 1, 2, 2))
    return jax.shard_map(
        on_device,
        mesh=inner,
        in_specs=(data, data, data) + weights,
        out_specs=(data, data) + weights + (P(),),
        check_vma=False,
    )
```

```python
import functools
import itertools
import math

import jax
import jax.numpy as jnp
from jax import lax
from jax.experimental import pallas as pl
from jax.experimental.pallas import tpu as pltpu
from jax.sharding import Mesh, PartitionSpec as P

D = 768
HEAD_DIM = 64
FF = 2048
EXPERTS = 4
BRANCHES = EXPERTS + 1
TOP = 2
BLOCK = 256
LANES = 128
GROUP = 256
GROUPS = D // GROUP

epsilon = 1e-05
f32 = jnp.float32
bf16 = jnp.bfloat16
ALL = ("x", "z", "y", "c")
PLANE = ("x", "y", "c")


def shuffle(v, axes, by):
    sizes = [lax.axis_size(axis) for axis in axes]
    pairs = []
    for at in range(math.prod(sizes)):
        rest, to, scale = at, 0, 1
        for size, flip in reversed(list(zip(sizes, by))):
            to += (rest % size ^ flip) * scale
            rest, scale = rest // size, scale * size
        pairs.append((at, to))
    return lax.ppermute(v, axes, pairs)


def swap(v, axis):
    return shuffle(v, (axis,), (1,))


def own_bit(axis, bit=0):
    return (lax.axis_index(axis) >> bit) & 1


def after(v, *deps):
    return lax.optimization_barrier((v, deps))[0]


def ordered(low, mine, other):
    return jnp.where(low, jnp.stack([mine, other]), jnp.stack([other, mine]))


def gather_axes(v, bits):
    axes = tuple(dict.fromkeys(axis for axis, _ in bits))

    def part(flips):
        by = [0] * len(axes)
        for (axis, bit), flip in zip(bits, flips):
            by[axes.index(axis)] |= flip << bit
        return shuffle(v, axes, by) if any(flips) else v

    def level(flips):
        if len(flips) == len(bits):
            return part(flips)
        low = own_bit(*bits[len(flips)]) == 0
        return ordered(low, level(flips + (0,)), level(flips + (1,)))

    return level(())


def z_bits():
    return [("z", bit) for bit in reversed(range(lax.axis_size("z").bit_length() - 1))]


def z_stages():
    bits = z_bits()
    return [bits] if len(bits) <= 2 else [[name] for name in bits]


def all_bits():
    return [("x", 0)] + z_bits() + [("y", 0), ("c", 0)]


def gather_rows(v, deps, more):
    held = []
    for bits in z_stages()[::-1] + [[("x", 0), ("y", 0)], [("c", 0)]]:
        if ("x", 0) in bits:
            v = after(v, deps)
        if ("c", 0) in bits:
            v = after(v, more)
        v = gather_axes(v, bits)
        held = bits + held
    lead = [held.index(name) for name in all_bits()]
    v = v.transpose(lead + list(range(len(lead), v.ndim)))
    return v.reshape(-1, v.shape[-1])


class Scatter:
    def __init__(self, v, rows, extra=None):
        self.names = all_bits()
        self.v = v.reshape((2,) * len(self.names) + (rows, v.shape[1]))
        self.extra = extra
        self.stages = [[("c", 0)], [("x", 0), ("y", 0)]] + z_stages()

    def block(self, flips, bits):
        v = self.v
        at = {self.names.index(name): own_bit(*name) ^ flip for name, flip in zip(bits, flips)}
        starts = [at.get(i, 0) for i in range(v.ndim)]
        sizes = [1 if i in at else v.shape[i] for i in range(v.ndim)]
        piece = lax.dynamic_slice(v, starts, sizes)
        return piece.reshape([n for i, n in enumerate(v.shape) if i not in at])

    def send(self):
        bits = self.stages[0]
        axes = tuple(dict.fromkeys(axis for axis, _ in bits))
        width = self.v.shape[-1]
        if self.extra is not None:
            count = self.extra.shape[0]
            coded, rest = [], self.extra
            for _ in range(3):
                coded.append(lax.reduce_precision(rest, 8, 7))
                rest = rest - coded[-1]
            spread = jnp.pad(jnp.concatenate(coded).astype(bf16), (width - 3 * count, 0))
            lane = jnp.arange(width) >= width - 3 * count
        moves = []
        for flips in itertools.product((0, 1), repeat=len(bits)):
            if not any(flips):
                continue
            by = [0] * len(axes)
            for (axis, bit), flip in zip(bits, flips):
                by[axes.index(axis)] |= flip << bit
            sent = self.block(flips, bits).astype(bf16)
            if self.extra is not None:
                sent = jnp.where(lane, spread, sent)
            moves.append(shuffle(sent, axes, by))
        return moves

    def take(self, moves):
        bits, self.stages = self.stages[0], self.stages[1:]
        total = self.block((0,) * len(bits), bits).astype(f32)
        for got in moves:
            got = got.astype(f32)
            total += got
            if self.extra is not None:
                count = self.extra.shape[0]
                parts = got.reshape(-1, got.shape[-1])[0, -3 * count :].reshape(3, count)
                self.extra = self.extra + (parts[0] + parts[1] + parts[2])
        self.v = total
        self.names = [name for name in self.names if name not in bits]

    def finish(self):
        while self.stages:
            self.take(self.send())


def on_chip(pair, more=None):
    v = pair[0] + swap(pair[1], "c").astype(f32)
    return v if more is None else v + more


def contract(a, b, dims):
    return lax.dot_general(a, b, (dims, ((), ())), preferred_element_type=f32)


def whole(shape):
    return pl.BlockSpec(shape, lambda *i: (0,) * len(shape))


def fixed(shape):
    return pl.BlockSpec(shape, lambda *i: (0,) * len(shape), pipeline_mode=pl.Buffered(1))


def shapes(*pairs):
    return [jax.ShapeDtypeStruct(shape, kind) for shape, kind in pairs]


def params(mib):
    return pltpu.CompilerParams(vmem_limit_bytes=mib * 2**20)


def cost(flops, moved, exps=0):
    return pl.CostEstimate(flops=flops, transcendentals=exps, bytes_accessed=moved)


def sigmoid(a):
    return 0.5 * jnp.tanh(0.5 * a) + 0.5


def ffn_body(branches, first, last, names, *refs):
    r = dict(zip(names, refs))
    win_ref, wout_ref, h_ref, p_ref = r["w_in"], r["w_out"], r["hidden"], r["pre"]
    units = wout_ref.shape[1]
    wide = len(branches) * units
    tile = h_ref.shape[0]
    step = pl.program_id(0)
    half = pl.num_programs(0) // 2
    own = step < half
    here = pl.ds(lax.rem(step, half) * tile, tile)
    x = jnp.where(own, r["xa"][here], r["xb"][here])
    g = jnp.where(own, r["ga"][here], r["gb"][here])
    lane = lax.broadcasted_iota(jnp.int32, (tile, LANES), 1)
    if first:
        r["xs"][...] = x
        r["gs"][...] = g[:, :D]
        route = g[:, D:].astype(f32).astype(jnp.int32)
        logits = contract(x, win_ref[:, 2 * wide :], ((1,), (0,)))
        one, two = lane == route[:, 0:1], lane == route[:, 1:2]
        up = jnp.sum(jnp.where(one, logits, 0.0), axis=1, keepdims=True)
        down = jnp.sum(jnp.where(two, logits, 0.0), axis=1, keepdims=True)
        top = jnp.maximum(up, down)
        up, down = jnp.exp(up - top), jnp.exp(down - top)
        total = up + down
        gates = jnp.where(one, up / total, 0.0) + jnp.where(two, down / total, 0.0)
        grad_gates = jnp.zeros_like(gates)
    else:
        gates, grad_gates = r["gates"][...], r["sums"][...]
    g = g[:, :D]
    for i, e in enumerate(branches):
        at = i * 2 * units
        pre = contract(x, win_ref[:, at : at + 2 * units], ((1,), (0,)))
        a, b = pre[:, :units], pre[:, units:]
        back = contract(g, wout_ref[i], ((1,), (1,)))
        s = sigmoid(a)
        silu = a * s
        hidden = (silu * b).astype(bf16)
        if e < EXPERTS:
            gate = gates[:, e : e + 1]
            hidden = hidden.astype(f32)
            this = jnp.sum(hidden * back, axis=1, keepdims=True)
            grad_gates = jnp.where(lane == e, this, grad_gates)
            hidden = (gate * hidden).astype(bf16)
            back = gate * back
        h_ref[:, i * units : (i + 1) * units] = hidden
        p_ref[:, at : at + units] = (back * b * (s + silu * (1.0 - s))).astype(bf16)
        p_ref[:, at + units : at + 2 * units] = (back * silu).astype(bf16)
        if last and e == EXPERTS - 1:
            inner = jnp.sum(gates * grad_gates, axis=1, keepdims=True)
            p_ref[:, 2 * wide :] = (gates * (grad_gates - inner)).astype(bf16)
    if not last:
        r["gates_out"][...] = gates
        r["sums_out"][...] = grad_gates
    tile_ref = r["tile"]
    deep = p_ref.shape[1]
    out = contract(h_ref[...], wout_ref[...].reshape(wide, D), ((1,), (0,)))
    tile_ref[:, D:] = out
    for at in range(0, D, GROUP):
        cols = slice(at, at + GROUP)
        tile_ref[:, cols] = contract(p_ref[...], win_ref[cols, :deep], ((1,), (1,)))

    @pl.when(own)
    def _():
        r["own"][here] = tile_ref[...]

    @pl.when(jnp.logical_not(own))
    def _():
        r["other"][here] = tile_ref[...].astype(bf16)


def ffn(part, parts, branches, x, g, w_in, w_out, kept, gating=None):
    first, last = gating is None, branches[-1] == BRANCHES - 1
    rows = x[0].shape[0]
    tile = min(256, rows)
    steps = rows // tile
    wide = w_in.shape[1] - LANES
    total = parts * 2 * rows
    here = lambda width: pl.BlockSpec((tile, width), lambda i: (i, 0))
    there = lambda width: pl.BlockSpec((tile, width), lambda i: (2 * part * steps + i, 0))
    ins = list(zip(("xa", "xb", "ga", "gb", "w_in", "w_out"), (*x, *g, w_in, w_out)))
    specs = [fixed(v.shape) for _, v in ins]
    if not first:
        ins += list(zip(("gates", "sums"), gating))
        specs += [here(LANES)] * 2
    outs = [("own", (rows, 2 * D), f32, whole((rows, 2 * D)))]
    outs += [("other", (rows, 2 * D), bf16, whole((rows, 2 * D)))]
    if not last:
        outs += [(n, (2 * rows, LANES), f32, here(LANES)) for n in ("gates_out", "sums_out")]
    at = len(outs)
    widths = [("hidden", wide // 2), ("pre", wide + last * LANES)]
    if first:
        widths += [("xs", D), ("gs", D)]
    outs += [(n, (total, width), bf16, there(width)) for n, width in widths]
    names = [n for n, _ in ins] + ["old"] * len(kept) + [n for n, *_ in outs] + ["tile"]
    results = pl.pallas_call(
        functools.partial(ffn_body, branches, first, last, names),
        grid=(2 * steps,),
        in_specs=specs + [pl.BlockSpec(memory_space=pl.ANY)] * len(kept),
        out_specs=[spec for *_, spec in outs],
        out_shape=shapes(*((shape, kind) for _, shape, kind, _ in outs)),
        scratch_shapes=[pltpu.VMEM((tile, 2 * D), f32)],
        input_output_aliases={len(ins) + i: at + i for i in range(len(kept))},
        compiler_params=params(30),
        cost_estimate=cost(
            12 * rows * D * wide, 3 * w_in.size + rows * (20 * D + 6 * wide), rows * wide
        ),
        name="ffn",
    )(*(v for _, v in ins), *kept)
    return results[:2], results[2:at], results[at:]


def half_turn(v):
    lane = lax.broadcasted_iota(jnp.int32, v.shape, 1)
    low = lane % HEAD_DIM < HEAD_DIM // 2
    return jnp.where(low, pltpu.roll(v, 128 - HEAD_DIM // 2, 1), pltpu.roll(v, HEAD_DIM // 2, 1))


def rope(v, cosine, sine):
    parts = [v[:, at : at + LANES] for at in range(0, v.shape[1], LANES)]
    return jnp.concatenate([p * cosine + half_turn(p) * sine for p in parts], axis=1)


def one_head(v, j):
    lane = lax.broadcasted_iota(jnp.int32, v.shape, 1)
    return jnp.where(lane // HEAD_DIM == j, v, jnp.zeros_like(v))


def normal(rows_in):
    return rows_in * lax.rsqrt(jnp.mean(rows_in * rows_in, axis=-1, keepdims=True) + epsilon)


def row_of(column):
    return jnp.broadcast_to(column, (column.shape[0], LANES)).T[:8]


def attend_body(
    seq_ref, prev_ref, tok_ref, gains_ref, wq_ref, wk_ref, wv_ref, wo_ref, cos_ref, sin_ref,
    normed_ref, q_ref, k_ref, v_ref, mixed_ref, lse_ref, middle_ref, two_ref, sums_ref, acc_ref,
):
    step = pl.program_id(0)
    rows = tok_ref.shape[0]

    @pl.when(step == 0)
    def _():
        for at, ref in ((0, prev_ref), (rows, tok_ref)):
            hat = normal(ref[...].astype(f32))
            normed_ref[at : at + rows] = (hat * gains_ref[0:1]).astype(bf16)

    x = normed_ref[...]
    cosine, sine = cos_ref[...], sin_ref[...]
    own_cos, own_sin = cosine[rows:], sine[rows:]
    q = contract(x[rows:], wq_ref[...], ((1,), (0,)))
    q_ref[...] = (rope(q, own_cos, own_sin) * 0.125).astype(bf16)
    k_ref[...] = rope(contract(x, wk_ref[...], ((1,), (0,))), cosine, sine).astype(bf16)
    v_ref[...] = contract(x, wv_ref[...], ((1,), (0,))).astype(bf16)
    skip = jnp.where(seq_ref[0] > 0, 0.0, 1e30)
    for at in range(0, GROUP, LANES):
        cols = slice(at, at + LANES)
        for top in range(0, rows, BLOCK):
            mixed = jnp.zeros((BLOCK, LANES), f32)
            ends = rows + top + BLOCK
            for j in range(LANES // HEAD_DIM):
                query = one_head(q_ref[top : top + BLOCK, cols], j)
                far = contract(query, k_ref[:rows, cols], ((1,), (1,)))
                near = contract(query, k_ref[rows:ends, cols], ((1,), (1,)))
                peak = jnp.maximum(
                    jnp.max(far, axis=1, keepdims=True) - skip, jnp.max(near, axis=1, keepdims=True)
                )
                far, near = jnp.exp(far - (peak + skip)), jnp.exp(near - peak)
                total = jnp.sum(far, axis=1, keepdims=True) + jnp.sum(near, axis=1, keepdims=True)
                both = contract(far.astype(bf16), one_head(v_ref[:rows, cols], j), ((1,), (0,)))
                both += contract(near.astype(bf16), one_head(v_ref[rows:ends, cols], j), ((1,), (0,)))
                mixed += both / total
                head = (at // HEAD_DIM + j) * 8
                lse_ref[head : head + 8, top : top + BLOCK] = row_of(peak + jnp.log(total))
            mixed_ref[top : top + BLOCK, cols] = mixed.astype(bf16)
    piece = contract(mixed_ref[...], wo_ref[...], ((1,), (0,)))

    @pl.when(step == 0)
    def _():
        acc_ref[...] = piece

    @pl.when(step > 0)
    def _():
        acc_ref[...] += piece

    @pl.when(step == GROUPS - 1)
    def _():
        attn = acc_ref[...]
        tok = tok_ref[...].astype(f32)
        middle = tok + attn
        middle_ref[...] = middle
        two_ref[...] = (normal(middle) * gains_ref[1:2]).astype(bf16)
        for i, v in enumerate((tok, attn, middle)):
            sums_ref[i : i + 1] = jnp.sum(v * v, axis=0, keepdims=True)


def attend(seq, prev, tok, gains, weights, cosine, sine):
    rows = tok.shape[0]
    heads = D // HEAD_DIM
    across = lambda n: pl.BlockSpec((n, GROUP), lambda i: (0, i))
    weight = lambda first: pl.BlockSpec((D, GROUP), lambda i: (0, first + i))
    return pl.pallas_call(
        attend_body,
        grid=(GROUPS,),
        in_specs=[
            pl.BlockSpec(memory_space=pltpu.SMEM),
            whole(prev.shape),
            whole(tok.shape),
            whole(gains.shape),
            weight(0),
            weight(GROUPS),
            weight(2 * GROUPS),
            pl.BlockSpec((GROUP, D), lambda i: (i, 3)),
            whole(cosine.shape),
            whole(sine.shape),
        ],
        out_specs=[
            whole((2 * rows, D)),
            across(rows),
            across(2 * rows),
            across(2 * rows),
            across(rows),
            pl.BlockSpec((8 * heads // GROUPS, rows), lambda i: (i, 0)),
            whole((rows, D)),
            whole((rows, D)),
            whole((8, D)),
        ],
        out_shape=shapes(
            ((2 * rows, D), bf16),
            ((rows, D), bf16),
            ((2 * rows, D), bf16),
            ((2 * rows, D), bf16),
            ((rows, D), bf16),
            ((8 * heads, rows), f32),
            ((rows, D), f32),
            ((rows, D), bf16),
            ((8, D), f32),
        ),
        scratch_shapes=[pltpu.VMEM((rows, D), f32)],
        compiler_params=params(52),
        cost_estimate=cost(
            2 * rows * D * D * 6 + 8 * rows * rows * D, 8 * D * D + 20 * rows * D, heads * 2 * rows * rows
        ),
        name="attend",
    )(seq, prev, tok, gains, *[weights] * 4, cosine, sine)


def heads_back(
    skip, grad, wo_ref, q_ref, k_ref, v_ref, mixed_ref, lse_ref, cos_ref, sin_ref, gq_ref, gk_ref,
    gv_ref, dqt_ref, dk_ref, dv_ref,
):
    rows = grad.shape[0]
    cosine, sine = cos_ref[...], sin_ref[...]
    grad_mixed = contract(grad, wo_ref[...], ((1,), (1,))).astype(bf16)
    for at in range(0, GROUP, LANES):
        cols = slice(at, at + LANES)
        key, value = k_ref[:, cols], v_ref[:, cols]
        key_t = key.T
        products = grad_mixed[:, cols].astype(f32) * mixed_ref[:, cols].astype(f32)
        for j in range(LANES // HEAD_DIM):
            head = (at // HEAD_DIM + j) * 8
            keep = lax.broadcasted_iota(jnp.int32, key_t.shape, 0) // HEAD_DIM == j
            key_j = jnp.where(keep, key_t, jnp.zeros_like(key_t))
            for top in range(0, rows, BLOCK):
                block = slice(top, top + BLOCK)
                query = one_head(q_ref[block, cols], j)
                back = one_head(grad_mixed[block, cols], j)
                delta = row_of(
                    jnp.sum(one_head(products[block], j), axis=1, keepdims=True)
                )[0:1]
                lse = lse_ref[head : head + 1, block]
                for begin, end, less in ((0, rows, lse + skip), (rows, rows + top + BLOCK, lse)):
                    probs = jnp.exp(contract(key[begin:end], query, ((1,), (1,))) - less)
                    above = contract(value[begin:end], back, ((1,), (1,))) - delta
                    scores = (probs * above).astype(bf16)
                    grad_v = contract(probs.astype(bf16), back, ((1,), (0,)))
                    grad_k = contract(scores, query, ((1,), (0,)))
                    grad_q = contract(key_j[:, begin:end], scores, ((1,), (0,)))
                    if j == 0 and top == 0:
                        dv_ref[begin:end], dk_ref[begin:end] = grad_v, grad_k
                        if rows < end < 2 * rows:
                            rest = jnp.zeros((2 * rows - end, LANES), f32)
                            dv_ref[end:], dk_ref[end:] = rest, rest
                    else:
                        dv_ref[begin:end] += grad_v
                        dk_ref[begin:end] += grad_k
                    if j == 0 and begin == 0:
                        dqt_ref[:, block] = grad_q
                    else:
                        dqt_ref[:, block] += grad_q
        own_cos, own_sin = cosine[rows:], sine[rows:]
        gq_ref[:, cols] = (rope(dqt_ref[...].T, own_cos, -own_sin) * 0.125).astype(bf16)
        gk_ref[:, cols] = rope(dk_ref[...], cosine, -sine).astype(bf16)
        gv_ref[:, cols] = dv_ref[...].astype(bf16)


def group_sums(normed, gq, gk, gv, wq_ref, wk_ref, wv_ref):
    rows = gq.shape[0]
    one = contract(gk, wk_ref[...], ((1,), (1,))) + contract(gv, wv_ref[...], ((1,), (1,)))
    own = one[rows:] + contract(gq, wq_ref[...], ((1,), (1,)))
    parts = ((normed[:, rows:], gq), (normed, gk), (normed, gv))
    return one[:rows], own, [contract(a, b, ((1,), (0,))).astype(bf16) for a, b in parts]


def attend_back_body(
    seq_ref, grad_ref, wo_ref, wq_ref, wk_ref, wv_ref, q_ref, k_ref, v_ref, mixed_ref, lse_ref,
    normed_ref, all_ref, cos_ref, sin_ref, one_ref, d_ref, *scratch,
):
    step = pl.program_id(0)
    rows = grad_ref.shape[0]

    @pl.when(step < GROUPS - 1)
    def _():
        skip = jnp.where(seq_ref[0] > 0, 0.0, 1e30)
        heads_back(
            skip, grad_ref[...], wo_ref, q_ref, k_ref, v_ref, mixed_ref, lse_ref, cos_ref, sin_ref,
            *scratch,
        )
        gq, gk, gv = (ref[...] for ref in scratch[:3])
        early, own, parts = group_sums(normed_ref[...], gq, gk, gv, wq_ref, wk_ref, wv_ref)
        for i, part in enumerate(parts):
            d_ref[:, i * GROUP : (i + 1) * GROUP] = part

        @pl.when(step == 0)
        def _():
            one_ref[:rows], one_ref[rows:] = early, own

        @pl.when(step > 0)
        def _():
            one_ref[:rows] += early
            one_ref[rows:] += own

    @pl.when(step == GROUPS - 1)
    def _():
        d_ref[...] = contract(all_ref[...], grad_ref[...], ((0,), (0,))).astype(bf16)


def attend_back_last_body(
    seq_ref, grad_ref, wo_ref, wq_ref, wk_ref, wv_ref, q_ref, k_ref, v_ref, mixed_ref, lse_ref,
    normed_ref, prev_ref, tok_ref, two_ref, one_ref, cos_ref, sin_ref, early_ref,
    own_ref, d_ref, *scratch,
):
    rows = grad_ref.shape[0]
    skip = jnp.where(seq_ref[0] > 0, 0.0, 1e30)
    heads_back(
        skip, grad_ref[...], wo_ref, q_ref, k_ref, v_ref, mixed_ref, lse_ref, cos_ref, sin_ref,
        *scratch,
    )
    gq, gk, gv = (ref[...] for ref in scratch[:3])
    early, own, parts = group_sums(normed_ref[...], gq, gk, gv, wq_ref, wk_ref, wv_ref)
    for i, part in enumerate(parts):
        d_ref[:, i * GROUP : (i + 1) * GROUP] = part
    early, own = early + one_ref[:rows], own + one_ref[rows:]
    early_ref[...] = early.astype(bf16)
    own_ref[...] = own
    gain = jnp.sum(early * normal(prev_ref[...].astype(f32)), axis=0, keepdims=True)
    gain += jnp.sum(own * normal(tok_ref[...].astype(f32)), axis=0, keepdims=True)
    gain = jnp.broadcast_to(gain, (LANES, D)).T
    two = jnp.broadcast_to(two_ref[0:1], (LANES, D)).T
    lane = lax.broadcasted_iota(jnp.int32, (D, LANES), 1)
    small = jnp.where(lane == 0, gain, jnp.where(lane == 1, two, 0.0))
    d_ref[:, 3 * GROUP :] = small.astype(bf16)


def back_specs(rows, at):
    heads = D // HEAD_DIM // GROUPS
    across = lambda n: pl.BlockSpec((n, GROUP), lambda i: (0, at(i)))
    weight = lambda first: pl.BlockSpec((D, GROUP), lambda i: (0, first + at(i)))
    return [
        pl.BlockSpec(memory_space=pltpu.SMEM),
        whole((rows, D)),
        pl.BlockSpec((GROUP, D), lambda i: (at(i), 3)),
        weight(0),
        weight(GROUPS),
        weight(2 * GROUPS),
        across(rows),
        across(2 * rows),
        across(2 * rows),
        across(rows),
        pl.BlockSpec((8 * heads, rows), lambda i: (at(i), 0)),
        whole((D, 2 * rows)),
    ]


def back_scratch(rows):
    return [
        pltpu.VMEM((rows, GROUP), bf16),
        pltpu.VMEM((2 * rows, GROUP), bf16),
        pltpu.VMEM((2 * rows, GROUP), bf16),
        pltpu.VMEM((LANES, rows), f32),
        pltpu.VMEM((2 * rows, LANES), f32),
        pltpu.VMEM((2 * rows, LANES), f32),
    ]


def back_cost(rows, count):
    heads = D // HEAD_DIM // GROUPS
    flops = 2 * rows * D * GROUP * 11 + 20 * rows * rows * GROUP
    return cost(count * flops, count * 40 * rows * D, count * heads * 2 * rows * rows)


def attend_back(seq, grad, weights, q, k, v, mixed, lse, normed_t, cosine, sine):
    rows = grad.shape[0]
    return pl.pallas_call(
        attend_back_body,
        grid=(GROUPS,),
        in_specs=back_specs(rows, lambda i: jnp.minimum(i, GROUPS - 2))
        + [whole(v.shape) for v in (mixed, cosine, sine)],
        out_specs=[whole((2 * rows, D)), pl.BlockSpec((D, D), lambda i: (0, i))],
        out_shape=shapes(((2 * rows, D), f32), ((D, GROUPS * D), bf16)),
        scratch_shapes=back_scratch(rows),
        compiler_params=params(36),
        cost_estimate=back_cost(rows, GROUPS - 1),
        name="attend_back",
    )(seq, grad, *[weights] * 4, q, k, v, mixed, lse, normed_t, mixed, cosine, sine)


def attend_back_last(
    seq, grad, weights, q, k, v, mixed, lse, normed_t, prev, tok, two, one, cosine, sine
):
    rows = grad.shape[0]
    extra = (prev, tok, two, one, cosine, sine)
    return pl.pallas_call(
        attend_back_last_body,
        grid=(1,),
        in_specs=back_specs(rows, lambda i: GROUPS - 1) + [whole(v.shape) for v in extra],
        out_specs=[whole((rows, D)), whole((rows, D)), whole((D, 3 * GROUP + LANES))],
        out_shape=shapes(((rows, D), bf16), ((rows, D), f32), ((D, 3 * GROUP + LANES), bf16)),
        scratch_shapes=back_scratch(rows),
        compiler_params=params(36),
        cost_estimate=back_cost(rows, 1),
        name="attend_back_last",
    )(seq, grad, *[weights] * 4, q, k, v, mixed, lse, normed_t, *extra)


def middle_back_body(
    own_ref, other_ref, x_ref, y_ref, middle_ref, grad_ref, gains_ref, mid_ref, low_ref, gain_ref
):
    rows = own_ref[...] + other_ref[...].astype(f32) + x_ref[...].astype(f32)
    rows += y_ref[...].astype(f32)
    middle = middle_ref[...]
    r = lax.rsqrt(jnp.mean(middle * middle, axis=-1, keepdims=True) + epsilon)
    hat = middle * r
    gain = jnp.sum(rows * hat, axis=0, keepdims=True)
    gain_ref[...] = jnp.broadcast_to(gain, gain_ref.shape)
    q = rows * gains_ref[1:2]
    grad = q - hat * jnp.mean(q * hat, axis=-1, keepdims=True)
    grad = grad_ref[...].astype(f32) + r * grad
    mid_ref[...] = grad
    low_ref[...] = grad.astype(bf16)


def middle_back(own, other, from_x, from_y, middle, grad, gains):
    rows = middle.shape[0]
    block = pl.BlockSpec((rows, D), lambda i: (0, 0))
    return pl.pallas_call(
        middle_back_body,
        grid=(1,),
        in_specs=[block] * 6 + [whole(gains.shape)],
        out_specs=[block, block, whole((8, D))],
        out_shape=shapes(((rows, D), f32), ((rows, D), bf16), ((8, D), f32)),
        compiler_params=params(40),
        cost_estimate=cost(20 * rows * D, 22 * rows * D),
        name="middle_back",
    )(own, other, from_x, from_y, middle, grad, gains)


def output_body(own_ref, other_ref, x_ref, y_ref, middle_ref, out_ref, sums_ref):
    ffn = own_ref[...] + other_ref[...].astype(f32) + x_ref[...].astype(f32)
    ffn += y_ref[...].astype(f32)
    out = middle_ref[...] + ffn
    out_ref[...] = out.astype(bf16)
    for i, v in enumerate((ffn, out)):
        sums_ref[i : i + 1] = jnp.sum(v * v, axis=0, keepdims=True)


def output(own, other, from_x, from_y, middle):
    rows = middle.shape[0]
    block = pl.BlockSpec((rows, D), lambda i: (0, 0))
    second = pl.BlockSpec((rows, D), lambda i: (0, 1))
    return pl.pallas_call(
        output_body,
        grid=(1,),
        in_specs=[second, second, block, block, block],
        out_specs=[block, whole((8, D))],
        out_shape=shapes(((rows, D), bf16), ((8, D), f32)),
        compiler_params=params(40),
        cost_estimate=cost(8 * rows * D, 16 * rows * D),
        name="output",
    )(own, other, from_x, from_y, middle)


def tokens_back_body(tok_ref, own_ref, returned_ref, mid_ref, gains_ref, out_ref):
    tok = tok_ref[...].astype(f32)
    r = lax.rsqrt(jnp.mean(tok * tok, axis=-1, keepdims=True) + epsilon)
    hat = tok * r
    q = (own_ref[...] + returned_ref[...].astype(f32)) * gains_ref[0:1]
    grad = q - hat * jnp.mean(q * hat, axis=-1, keepdims=True)
    out_ref[...] = (mid_ref[...] + r * grad).astype(bf16)


def tokens_back(tok, own, returned, mid, gains):
    rows = tok.shape[0]
    block = whole((rows, D))
    return pl.pallas_call(
        tokens_back_body,
        grid=(1,),
        in_specs=[block] * 4 + [whole(gains.shape)],
        out_specs=block,
        out_shape=jax.ShapeDtypeStruct((rows, D), bf16),
        compiler_params=params(40),
        cost_estimate=cost(12 * rows * D, 14 * rows * D),
        name="tokens_back",
    )(tok, own, returned, mid, gains)


def gather_columns_body(sums_ref, qkv_ref, out_ref, tail_ref):
    for i in range(GROUPS):
        at = i * D if i < GROUPS - 1 else GROUPS * D
        for part in range(3):
            to = part * D + i * GROUP
            here = at + part * GROUP
            qkv_ref[:, to : to + GROUP] = sums_ref[:, here : here + GROUP]
    out_ref[...] = sums_ref[:, (GROUPS - 1) * D : GROUPS * D]
    tail_ref[...] = sums_ref[:, (GROUPS + 1) * D :]


def gather_columns(sums):
    rows = sums.shape[0]
    return pl.pallas_call(
        gather_columns_body,
        in_specs=[whole(sums.shape)],
        out_specs=[whole((rows, n)) for n in (3 * D, D, LANES)],
        out_shape=shapes(*(((rows, n), f32) for n in (3 * D, D, LANES))),
        grid=(1,),
        name="gather_columns",
    )(sums)


def columns_back_body(pair, in_ref, out_ref):
    count, _, width = out_ref.shape
    half = width // 2
    deep = half // (8 * pair)
    for e, g, x, c, z, y in itertools.product(
        range(count), range(2), range(2), range(2), range(deep), range(2)
    ):
        to = g * half + (((x * 2 + c) * deep + z) * 2 + y) * pair
        here = ((e * 2 + g) * deep + z) * pair
        piece = in_ref[(x * 2 + y) * 2 + c, :, here : here + pair]
        out_ref[e, :, to : to + pair] = piece.astype(f32)


def rope_tables(positions):
    halfdim = HEAD_DIM // 2
    inverse = 10000.0 ** (-2.0 * jnp.arange(halfdim, dtype=f32) / HEAD_DIM)
    angles = positions.astype(f32)[:, None] * inverse[None, :]
    cosine, sine = jnp.cos(angles), jnp.sin(angles)
    times = LANES // HEAD_DIM
    return (
        jnp.tile(jnp.concatenate([cosine, cosine], axis=1), (1, times)),
        jnp.tile(jnp.concatenate([-sine, sine], axis=1), (1, times)),
    )


SPLIT = (range(0, BRANCHES),)


def columns_out(w_ffn_in):
    depth = lax.axis_size("z")
    rows, count = w_ffn_in.shape[:2]
    pair = 2 * (FF // lax.axis_size(ALL))
    cut = w_ffn_in.reshape(rows, count, 2, 2, 2, depth // 2, 2, pair)
    return cut.transpose(3, 6, 4, 0, 1, 2, 5, 7).reshape(8, rows, -1)


def columns_back(v, count):
    depth = lax.axis_size("z")
    rows = v.shape[1]
    pair = 2 * (FF // lax.axis_size(ALL))
    if pair % LANES == 0:
        out = pl.pallas_call(
            functools.partial(columns_back_body, pair),
            in_specs=[whole(v.shape)],
            out_specs=whole((count, rows, 2 * FF)),
            out_shape=jax.ShapeDtypeStruct((count, rows, 2 * FF), f32),
            grid=(1,),
            name="columns_back",
        )(v)
        return out.transpose(1, 0, 2)
    v = v[:, :, : count * depth * pair].reshape(2, 2, 2, rows, count, 2, depth // 2, pair)
    return v.astype(f32).transpose(3, 4, 5, 0, 2, 6, 1, 7).reshape(rows, count, 2 * FF)


def exchange(cut):
    return lax.all_to_all(cut, PLANE, split_axis=0, concat_axis=0, tiled=True)


def columns_in(cut):
    wide = cut.shape[-1]
    cut = cut.reshape(2, -1, wide)
    return lax.all_gather(cut, "z", axis=1, tiled=True).reshape(D, wide)


def units_in(part):
    depth = lax.axis_size("z")
    count, own = part.shape[0], part.shape[1] // depth
    part = part.reshape(count, 2, depth // 2, own, D)
    core = own_bit("c")
    kept = lax.dynamic_index_in_dim(part, core, 1, keepdims=False)
    sent = lax.dynamic_index_in_dim(part, 1 - core, 1, keepdims=False)
    other = swap(sent, "c")
    both = jnp.where(core == 0, jnp.stack([kept, other], 2), jnp.stack([other, kept], 2))
    return both.reshape(count, depth * own, D)


def units_swap(d_hid, count):
    depth = lax.axis_size("z")
    d_hid = d_hid.reshape(count, depth // 2, 2, -1, D)
    core = own_bit("c")
    kept = lax.dynamic_index_in_dim(d_hid, core, 2, keepdims=False)
    return kept, swap(lax.dynamic_index_in_dim(d_hid, 1 - core, 2, keepdims=False), "c")


def units_out(kept, other):
    count, _, own, _ = kept.shape
    low = own_bit("c") == 0
    both = jnp.where(low, jnp.stack([kept, other], 1), jnp.stack([other, kept], 1))
    return both.reshape(count, -1, D)


def on_device(
    tokens, cotangent, routes, gain_one, w_qkv, w_attn_out, gain_two, router, w_ffn_in, w_ffn_out
):
    rows = tokens.shape[1]
    own_rows = w_qkv.shape[0]
    low_tokens = tokens.reshape(rows, D)
    low_grad = cotangent.reshape(rows, D)

    cut = exchange(columns_out(w_ffn_in))
    starts = [2 * FF // 8 * branches[0] for branches in SPLIT] + [cut.shape[-1]]
    w_out = lax.all_gather(w_ffn_out.transpose(1, 0, 2), "z", axis=1, tiled=True)
    w_in = [columns_in(cut[:, :, a:b]) for a, b in zip(starts, starts[1:])]
    before = lax.ppermute(low_tokens, "x", [(i, i + 1) for i in range(lax.axis_size("x") - 1)])
    seq_index = lax.axis_index("x")
    positions = (seq_index - 1) * rows + jnp.arange(2 * rows, dtype=jnp.int32)
    cosine, sine = rope_tables(positions)
    seq = seq_index.astype(jnp.int32).reshape(1)
    route = jnp.pad(routes.reshape(rows, TOP), ((0, 0), (0, LANES - TOP))).astype(bf16)
    grad_ext = jnp.concatenate([low_grad, route], axis=1)
    small = jnp.concatenate([gain_one[:, None], gain_two[:, None], router], axis=1)
    small = jnp.pad(small, ((0, 0), (0, LANES - small.shape[1])))
    weights = gather_rows(
        jnp.concatenate([w_qkv, w_attn_out, small], axis=1), (before,), (cosine, sine, grad_ext)
    )
    gains = weights[:, 4 * D : 4 * D + 2].astype(f32).T
    router_full = jnp.pad(
        weights[:, 4 * D + 2 : 4 * D + 2 + EXPERTS], ((0, 0), (0, LANES - EXPERTS))
    )
    grad_ext = after(grad_ext, weights)
    grad_x, grad_y = swap(grad_ext, "x"), swap(grad_ext, "y")

    results = attend(seq, before, low_tokens, gains, weights, cosine, sine)
    results = after(results, grad_x, grad_y)
    normed_one, q, k, v, mixed, lse, middle, normed_two, sums = results

    half = rows // 2

    def corner(across_x, across_y):
        return swap(across_x[:half], "y"), swap(across_y[half:], "x")

    def both_cores(u):
        return (u, swap(u, "c"))

    across_x, across_y = swap(normed_two, "x"), swap(normed_two, "y")
    grad_far = corner(grad_x, grad_y)
    normed_t = normed_one.T
    w_out = units_in(after(w_out, normed_two))
    x, g = {0: both_cores(normed_two)}, {0: both_cores(grad_ext)}
    x[0] = after(x[0], normed_t)
    below, gating, d_in, d_hid = {}, {}, [], []
    for branches, columns in zip(SPLIT, w_in):
        first, last = branches[0] == 0, branches[-1] == BRANCHES - 1
        columns = jnp.concatenate([columns, router_full], axis=1)
        units = w_out[branches[0] : branches[-1] + 1]
        if not first:
            columns = after(columns, d_in, d_hid)
        kept, top = (), {}

        def run(which, kept, *moves):
            part, gate, kept = ffn(
                which, 4, branches, x[which], g[which], columns, units, kept, gating.get(which)
            )
            part, moves = after((part, moves), part[0], moves) if moves else (part, ())
            gating[which] = gate or None
            return part, kept, moves

        if first:
            part, kept, moves = run(0, kept, across_x, across_y, *grad_far)
            top[0], (across_x, across_y, *grad_far) = part, moves
            far = corner(across_x, across_y)
            x[1], g[1] = both_cores(across_x), both_cores(grad_x)
            top[1], kept, (*far, other_part) = run(1, kept, *far, swap(top[0][1], "c"))
            x[3], g[3] = both_cores(jnp.concatenate(far)), both_cores(jnp.concatenate(grad_far))
            x[2], g[2] = both_cores(across_y), both_cores(grad_y)
        else:
            top[0], kept, _ = run(0, kept)
            top[1], kept, _ = run(1, kept)
        top[3], kept, _ = run(3, kept)
        if last:
            v3 = on_chip(top[3], below.get(3))
            moves = swap(v3[:half].astype(bf16), "x"), swap(v3[half:].astype(bf16), "y")
            top[2], kept, (upper, lower) = run(2, kept, *moves)
        else:
            top[2], kept, _ = run(2, kept)
        if first:
            x_all, g_all = kept[2:]
        rows_in_all = x_all
        if last:
            v1 = on_chip(top[1], below.get(1))
            v2 = on_chip(top[2], below.get(2))
            for_x = jnp.concatenate([v1[:half], v1[half:] + lower.astype(f32)]).astype(bf16)
            for_y = jnp.concatenate([v2[:half] + upper.astype(f32), v2[half:]]).astype(bf16)
            from_x, from_y = swap(for_x[:, :D], "x"), swap(for_y[:, :D], "y")
            rows_in_all = after(x_all, for_x, for_y)
        full = contract(rows_in_all, kept[1], ((0,), (0,))).astype(bf16)
        wide = columns.shape[1] - LANES
        if last:
            full, from_x, from_y = after((full, from_x, from_y), full, from_x, from_y)
        full = full if last else full[:, :wide]
        d_in.append(full)
        d_hid.append(contract(after(kept[0], full), g_all, ((0,), (0,))).astype(bf16))
        if not last:
            below = {which: on_chip(part, below.get(which)) for which, part in top.items()}
    own_part = top[0][0]
    grad_middle, grad_attn, gain_two_sums = middle_back(
        own_part, other_part, from_x, from_y, middle, low_grad, gains
    )
    grad_attn = after(grad_attn, d_hid)
    d_cols = [
        lax.psum_scatter(u.reshape(2, D // 2, -1), "z", scatter_dimension=1, tiled=True)
        for u in d_in
    ]
    d_hid = [units_swap(u, len(branches)) for u, branches in zip(d_hid, SPLIT)]

    for_x, for_y = after((for_x, for_y), grad_attn)
    moves = swap(for_x[:, D:], "x"), swap(for_y[:, D:], "y")
    one, part = attend_back(
        seq, grad_attn, weights, q, k, v, mixed, lse, normed_t, cosine, sine
    )
    one, part, (from_x, from_y), d_hid = after((one, part, moves, d_hid), one, moves, d_hid)
    first = Scatter(part, own_rows)
    moves = first.send()
    result, squares = output(own_part, other_part, from_x, from_y, middle)
    partial_sums = jnp.concatenate([jnp.sum(sums[:3], axis=1), jnp.sum(squares[:2], axis=1)])
    first.take(moves)
    d_hid = [units_out(*u) for u in after(d_hid, first.v)]
    d_cols = [u.reshape(8, own_rows, -1) for u in d_cols]
    moves = first.send()
    early, own, part = attend_back_last(
        seq, after(grad_attn, one, partial_sums, first.v), weights, q, k, v, mixed, lse, normed_t, before,
        low_tokens, gain_two_sums, one, cosine, sine
    )
    early, own, part, moves, d_cols = after(
        (early, own, part, moves, d_cols), own, moves, d_cols, d_hid
    )
    d_w_out = [lax.psum_scatter(u, "z", scatter_dimension=1, tiled=True) for u in d_hid]
    d_w_out = [u.transpose(1, 0, 2) for u in d_w_out]
    last = Scatter(part, own_rows, partial_sums)
    last_moves = last.send()
    first.take(moves)
    returned = lax.ppermute(early, "x", [(i + 1, i) for i in range(lax.axis_size("x") - 1)])
    last.take(last_moves)
    last_moves = last.send()
    last.take(last_moves)
    d_cols = [exchange(after(u, last.v)) for u in d_cols]
    last.v = jnp.concatenate([first.v, last.v], axis=-1)
    last_moves = last.send()
    d_router = jnp.sum(d_cols[-1][:, :, -LANES : EXPERTS - LANES].astype(f32), axis=0)
    d_cols = [columns_back(u, len(b)) for u, b in zip(d_cols, SPLIT)]
    last_moves, d_cols = after((last_moves, d_cols), last_moves, d_cols)
    last.take(last_moves)
    last.finish()
    d_w_qkv, d_w_attn_out, tail = gather_columns(last.v)
    d_w_out = [u.astype(f32) for u in after(d_w_out, last.v)]
    grad_tokens = tokens_back(low_tokens, own, after(returned, last.v), grad_middle, gains)
    stats = jnp.sqrt(last.extra / (rows * lax.axis_size(ALL) * D))
    return (
        result.reshape(tokens.shape),
        grad_tokens.reshape(tokens.shape),
        tail[:, 0],
        d_w_qkv,
        d_w_attn_out,
        tail[:, 1],
        d_router,
        jnp.concatenate(d_cols, axis=1),
        jnp.concatenate(d_w_out, axis=1),
        stats,
    )


def solution(mesh):
    seq, fsdp = mesh.shape["seq"], mesh.shape["fsdp"]
    inner = Mesh(mesh.devices.reshape(seq, fsdp // 4, 2, 2), ALL)
    data = P(("z", "y", "c"), "x", None)
    weights = tuple(P(ALL, *(None,) * k) for k in (0, 1, 1, 0, 1, 2, 2))
    return jax.shard_map(
        on_device,
        mesh=inner,
        in_specs=(data, data, data) + weights,
        out_specs=(data, data) + weights + (P(),),
        check_vma=False,
    )
```

```python
import functools
import itertools
import math

import jax
import jax.numpy as jnp
from jax import lax
from jax.experimental import pallas as pl
from jax.experimental.pallas import tpu as pltpu
from jax.sharding import Mesh, PartitionSpec as P

D = 768
HEAD_DIM = 64
FF = 2048
EXPERTS = 4
BRANCHES = EXPERTS + 1
TOP = 2
BLOCK = 256
LANES = 128
GROUP = 256
GROUPS = D // GROUP

epsilon = 1e-05
f32 = jnp.float32
bf16 = jnp.bfloat16
ALL = ("x", "z", "y", "c")
PLANE = ("x", "y", "c")


def shuffle(v, axes, by):
    sizes = [lax.axis_size(axis) for axis in axes]
    pairs = []
    for at in range(math.prod(sizes)):
        rest, to, scale = at, 0, 1
        for size, flip in reversed(list(zip(sizes, by))):
            to += (rest % size ^ flip) * scale
            rest, scale = rest // size, scale * size
        pairs.append((at, to))
    return lax.ppermute(v, axes, pairs)


def swap(v, axis):
    return shuffle(v, (axis,), (1,))


def own_bit(axis, bit=0):
    return (lax.axis_index(axis) >> bit) & 1


def after(v, *deps):
    return lax.optimization_barrier((v, deps))[0]


def ordered(low, mine, other):
    return jnp.where(low, jnp.stack([mine, other]), jnp.stack([other, mine]))


def gather_axes(v, bits):
    axes = tuple(dict.fromkeys(axis for axis, _ in bits))

    def part(flips):
        by = [0] * len(axes)
        for (axis, bit), flip in zip(bits, flips):
            by[axes.index(axis)] |= flip << bit
        return shuffle(v, axes, by) if any(flips) else v

    def level(flips):
        if len(flips) == len(bits):
            return part(flips)
        low = own_bit(*bits[len(flips)]) == 0
        return ordered(low, level(flips + (0,)), level(flips + (1,)))

    return level(())


def z_bits():
    return [("z", bit) for bit in reversed(range(lax.axis_size("z").bit_length() - 1))]


def z_stages():
    bits = z_bits()
    return [bits] if len(bits) <= 2 else [[name] for name in bits]


def all_bits():
    return [("x", 0)] + z_bits() + [("y", 0), ("c", 0)]


def gather_rows(v, deps, more):
    held = []
    for bits in z_stages()[::-1] + [[("x", 0), ("y", 0)], [("c", 0)]]:
        if ("x", 0) in bits:
            v = after(v, deps)
        if ("c", 0) in bits:
            v = after(v, more)
        v = gather_axes(v, bits)
        held = bits + held
    lead = [held.index(name) for name in all_bits()]
    v = v.transpose(lead + list(range(len(lead), v.ndim)))
    return v.reshape(-1, v.shape[-1])


class Scatter:
    def __init__(self, v, rows, extra=None):
        self.names = all_bits()
        self.v = v.reshape((2,) * len(self.names) + (rows, v.shape[1]))
        self.extra = extra
        self.stages = [[("c", 0)], [("x", 0), ("y", 0)]] + z_stages()

    def block(self, flips, bits):
        v = self.v
        at = {self.names.index(name): own_bit(*name) ^ flip for name, flip in zip(bits, flips)}
        starts = [at.get(i, 0) for i in range(v.ndim)]
        sizes = [1 if i in at else v.shape[i] for i in range(v.ndim)]
        piece = lax.dynamic_slice(v, starts, sizes)
        return piece.reshape([n for i, n in enumerate(v.shape) if i not in at])

    def send(self):
        bits = self.stages[0]
        axes = tuple(dict.fromkeys(axis for axis, _ in bits))
        width = self.v.shape[-1]
        if self.extra is not None:
            count = self.extra.shape[0]
            coded, rest = [], self.extra
            for _ in range(3):
                coded.append(lax.reduce_precision(rest, 8, 7))
                rest = rest - coded[-1]
            spread = jnp.pad(jnp.concatenate(coded).astype(bf16), (width - 3 * count, 0))
            lane = jnp.arange(width) >= width - 3 * count
        moves = []
        for flips in itertools.product((0, 1), repeat=len(bits)):
            if not any(flips):
                continue
            by = [0] * len(axes)
            for (axis, bit), flip in zip(bits, flips):
                by[axes.index(axis)] |= flip << bit
            sent = self.block(flips, bits).astype(bf16)
            if self.extra is not None:
                sent = jnp.where(lane, spread, sent)
            moves.append(shuffle(sent, axes, by))
        return moves

    def take(self, moves):
        bits, self.stages = self.stages[0], self.stages[1:]
        total = self.block((0,) * len(bits), bits).astype(f32)
        for got in moves:
            got = got.astype(f32)
            total += got
            if self.extra is not None:
                count = self.extra.shape[0]
                parts = got.reshape(-1, got.shape[-1])[0, -3 * count :].reshape(3, count)
                self.extra = self.extra + (parts[0] + parts[1] + parts[2])
        self.v = total
        self.names = [name for name in self.names if name not in bits]

    def finish(self):
        while self.stages:
            self.take(self.send())


def on_chip(pair, more=None):
    v = pair[0] + swap(pair[1], "c").astype(f32)
    return v if more is None else v + more


def contract(a, b, dims):
    return lax.dot_general(a, b, (dims, ((), ())), preferred_element_type=f32)


def whole(shape):
    return pl.BlockSpec(shape, lambda *i: (0,) * len(shape))


def fixed(shape):
    return pl.BlockSpec(shape, lambda *i: (0,) * len(shape), pipeline_mode=pl.Buffered(1))


def shapes(*pairs):
    return [jax.ShapeDtypeStruct(shape, kind) for shape, kind in pairs]


def params(mib):
    return pltpu.CompilerParams(vmem_limit_bytes=mib * 2**20)


def cost(flops, moved, exps=0):
    return pl.CostEstimate(flops=flops, transcendentals=exps, bytes_accessed=moved)


def sigmoid(a):
    return 0.5 * jnp.tanh(0.5 * a) + 0.5


def ffn_body(branches, first, last, names, *refs):
    r = dict(zip(names, refs))
    win_ref, wout_ref, h_ref, p_ref = r["w_in"], r["w_out"], r["hidden"], r["pre"]
    units = wout_ref.shape[1]
    wide = len(branches) * units
    tile = h_ref.shape[0]
    step = pl.program_id(0)
    half = pl.num_programs(0) // 2
    own = step < half
    here = pl.ds(lax.rem(step, half) * tile, tile)
    x = jnp.where(own, r["xa"][here], r["xb"][here])
    g = jnp.where(own, r["ga"][here], r["gb"][here])
    lane = lax.broadcasted_iota(jnp.int32, (tile, LANES), 1)
    if first:
        r["xs"][...] = x
        r["gs"][...] = g[:, :D]
        route = g[:, D:].astype(f32).astype(jnp.int32)
        logits = contract(x, win_ref[:, 2 * wide :], ((1,), (0,)))
        one, two = lane == route[:, 0:1], lane == route[:, 1:2]
        up = jnp.sum(jnp.where(one, logits, 0.0), axis=1, keepdims=True)
        down = jnp.sum(jnp.where(two, logits, 0.0), axis=1, keepdims=True)
        top = jnp.maximum(up, down)
        up, down = jnp.exp(up - top), jnp.exp(down - top)
        total = up + down
        gates = jnp.where(one, up / total, 0.0) + jnp.where(two, down / total, 0.0)
        grad_gates = jnp.zeros_like(gates)
    else:
        gates, grad_gates = r["gates"][...], r["sums"][...]
    g = g[:, :D]
    for i, e in enumerate(branches):
        at = i * 2 * units
        pre = contract(x, win_ref[:, at : at + 2 * units], ((1,), (0,)))
        a, b = pre[:, :units], pre[:, units:]
        back = contract(g, wout_ref[i], ((1,), (1,)))
        s = sigmoid(a)
        silu = a * s
        hidden = (silu * b).astype(bf16)
        if e < EXPERTS:
            gate = gates[:, e : e + 1]
            hidden = hidden.astype(f32)
            this = jnp.sum(hidden * back, axis=1, keepdims=True)
            grad_gates = jnp.where(lane == e, this, grad_gates)
            hidden = (gate * hidden).astype(bf16)
            back = gate * back
        h_ref[:, i * units : (i + 1) * units] = hidden
        p_ref[:, at : at + units] = (back * b * (s + silu * (1.0 - s))).astype(bf16)
        p_ref[:, at + units : at + 2 * units] = (back * silu).astype(bf16)
        if last and e == EXPERTS - 1:
            inner = jnp.sum(gates * grad_gates, axis=1, keepdims=True)
            p_ref[:, 2 * wide :] = (gates * (grad_gates - inner)).astype(bf16)
    if not last:
        r["gates_out"][...] = gates
        r["sums_out"][...] = grad_gates
    tile_ref = r["tile"]
    deep = p_ref.shape[1]
    out = contract(h_ref[...], wout_ref[...].reshape(wide, D), ((1,), (0,)))
    tile_ref[:, D:] = out
    for at in range(0, D, GROUP):
        cols = slice(at, at + GROUP)
        tile_ref[:, cols] = contract(p_ref[...], win_ref[cols, :deep], ((1,), (1,)))

    @pl.when(own)
    def _():
        r["own"][here] = tile_ref[...]

    @pl.when(jnp.logical_not(own))
    def _():
        r["other"][here] = tile_ref[...].astype(bf16)


def ffn(part, parts, branches, x, g, w_in, w_out, kept, gating=None):
    first, last = gating is None, branches[-1] == BRANCHES - 1
    rows = x[0].shape[0]
    tile = min(256, rows)
    steps = rows // tile
    wide = w_in.shape[1] - LANES
    total = parts * 2 * rows
    here = lambda width: pl.BlockSpec((tile, width), lambda i: (i, 0))
    there = lambda width: pl.BlockSpec((tile, width), lambda i: (2 * part * steps + i, 0))
    ins = list(zip(("xa", "xb", "ga", "gb", "w_in", "w_out"), (*x, *g, w_in, w_out)))
    specs = [fixed(v.shape) for _, v in ins]
    if not first:
        ins += list(zip(("gates", "sums"), gating))
        specs += [here(LANES)] * 2
    outs = [("own", (rows, 2 * D), f32, whole((rows, 2 * D)))]
    outs += [("other", (rows, 2 * D), bf16, whole((rows, 2 * D)))]
    if not last:
        outs += [(n, (2 * rows, LANES), f32, here(LANES)) for n in ("gates_out", "sums_out")]
    at = len(outs)
    widths = [("hidden", wide // 2), ("pre", wide + last * LANES)]
    if first:
        widths += [("xs", D), ("gs", D)]
    outs += [(n, (total, width), bf16, there(width)) for n, width in widths]
    names = [n for n, _ in ins] + ["old"] * len(kept) + [n for n, *_ in outs] + ["tile"]
    results = pl.pallas_call(
        functools.partial(ffn_body, branches, first, last, names),
        grid=(2 * steps,),
        in_specs=specs + [pl.BlockSpec(memory_space=pl.ANY)] * len(kept),
        out_specs=[spec for *_, spec in outs],
        out_shape=shapes(*((shape, kind) for _, shape, kind, _ in outs)),
        scratch_shapes=[pltpu.VMEM((tile, 2 * D), f32)],
        input_output_aliases={len(ins) + i: at + i for i in range(len(kept))},
        compiler_params=params(30),
        cost_estimate=cost(
            12 * rows * D * wide, 3 * w_in.size + rows * (20 * D + 6 * wide), rows * wide
        ),
        name="ffn",
    )(*(v for _, v in ins), *kept)
    return results[:2], results[2:at], results[at:]


def half_turn(v):
    lane = lax.broadcasted_iota(jnp.int32, v.shape, 1)
    low = lane % HEAD_DIM < HEAD_DIM // 2
    return jnp.where(low, pltpu.roll(v, 128 - HEAD_DIM // 2, 1), pltpu.roll(v, HEAD_DIM // 2, 1))


def rope(v, cosine, sine):
    parts = [v[:, at : at + LANES] for at in range(0, v.shape[1], LANES)]
    return jnp.concatenate([p * cosine + half_turn(p) * sine for p in parts], axis=1)


def one_head(v, j):
    lane = lax.broadcasted_iota(jnp.int32, v.shape, 1)
    return jnp.where(lane // HEAD_DIM == j, v, jnp.zeros_like(v))


def normal(rows_in):
    return rows_in * lax.rsqrt(jnp.mean(rows_in * rows_in, axis=-1, keepdims=True) + epsilon)


def row_of(column):
    return jnp.broadcast_to(column, (column.shape[0], LANES)).T[:8]


def attend_body(
    seq_ref, prev_ref, tok_ref, gains_ref, wq_ref, wk_ref, wv_ref, wo_ref, cos_ref, sin_ref,
    normed_ref, q_ref, k_ref, v_ref, mixed_ref, lse_ref, middle_ref, two_ref, sums_ref, acc_ref,
):
    step = pl.program_id(0)
    rows = tok_ref.shape[0]

    @pl.when(step == 0)
    def _():
        for at, ref in ((0, prev_ref), (rows, tok_ref)):
            hat = normal(ref[...].astype(f32))
            normed_ref[at : at + rows] = (hat * gains_ref[0:1]).astype(bf16)

    x = normed_ref[...]
    cosine, sine = cos_ref[...], sin_ref[...]
    own_cos, own_sin = cosine[rows:], sine[rows:]
    q = contract(x[rows:], wq_ref[...], ((1,), (0,)))
    q_ref[...] = (rope(q, own_cos, own_sin) * 0.125).astype(bf16)
    k_ref[...] = rope(contract(x, wk_ref[...], ((1,), (0,))), cosine, sine).astype(bf16)
    v_ref[...] = contract(x, wv_ref[...], ((1,), (0,))).astype(bf16)
    skip = jnp.where(seq_ref[0] > 0, 0.0, 1e30)
    for at in range(0, GROUP, LANES):
        cols = slice(at, at + LANES)
        for top in range(0, rows, BLOCK):
            mixed = jnp.zeros((BLOCK, LANES), f32)
            ends = rows + top + BLOCK
            for j in range(LANES // HEAD_DIM):
                query = one_head(q_ref[top : top + BLOCK, cols], j)
                far = contract(query, k_ref[:rows, cols], ((1,), (1,)))
                near = contract(query, k_ref[rows:ends, cols], ((1,), (1,)))
                peak = jnp.maximum(
                    jnp.max(far, axis=1, keepdims=True) - skip, jnp.max(near, axis=1, keepdims=True)
                )
                far, near = jnp.exp(far - (peak + skip)), jnp.exp(near - peak)
                total = jnp.sum(far, axis=1, keepdims=True) + jnp.sum(near, axis=1, keepdims=True)
                both = contract(far.astype(bf16), one_head(v_ref[:rows, cols], j), ((1,), (0,)))
                both += contract(near.astype(bf16), one_head(v_ref[rows:ends, cols], j), ((1,), (0,)))
                mixed += both / total
                head = (at // HEAD_DIM + j) * 8
                lse_ref[head : head + 8, top : top + BLOCK] = row_of(peak + jnp.log(total))
            mixed_ref[top : top + BLOCK, cols] = mixed.astype(bf16)
    piece = contract(mixed_ref[...], wo_ref[...], ((1,), (0,)))

    @pl.when(step == 0)
    def _():
        acc_ref[...] = piece

    @pl.when(step > 0)
    def _():
        acc_ref[...] += piece

    @pl.when(step == GROUPS - 1)
    def _():
        attn = acc_ref[...]
        tok = tok_ref[...].astype(f32)
        middle = tok + attn
        middle_ref[...] = middle
        two_ref[...] = (normal(middle) * gains_ref[1:2]).astype(bf16)
        for i, v in enumerate((tok, attn, middle)):
            sums_ref[i : i + 1] = jnp.sum(v * v, axis=0, keepdims=True)


def attend(seq, prev, tok, gains, weights, cosine, sine):
    rows = tok.shape[0]
    heads = D // HEAD_DIM
    across = lambda n: pl.BlockSpec((n, GROUP), lambda i: (0, i))
    weight = lambda first: pl.BlockSpec((D, GROUP), lambda i: (0, first + i))
    return pl.pallas_call(
        attend_body,
        grid=(GROUPS,),
        in_specs=[
            pl.BlockSpec(memory_space=pltpu.SMEM),
            whole(prev.shape),
            whole(tok.shape),
            whole(gains.shape),
            weight(0),
            weight(GROUPS),
            weight(2 * GROUPS),
            pl.BlockSpec((GROUP, D), lambda i: (i, 3)),
            whole(cosine.shape),
            whole(sine.shape),
        ],
        out_specs=[
            whole((2 * rows, D)),
            across(rows),
            across(2 * rows),
            across(2 * rows),
            across(rows),
            pl.BlockSpec((8 * heads // GROUPS, rows), lambda i: (i, 0)),
            whole((rows, D)),
            whole((rows, D)),
            whole((8, D)),
        ],
        out_shape=shapes(
            ((2 * rows, D), bf16),
            ((rows, D), bf16),
            ((2 * rows, D), bf16),
            ((2 * rows, D), bf16),
            ((rows, D), bf16),
            ((8 * heads, rows), f32),
            ((rows, D), f32),
            ((rows, D), bf16),
            ((8, D), f32),
        ),
        scratch_shapes=[pltpu.VMEM((rows, D), f32)],
        compiler_params=params(52),
        cost_estimate=cost(
            2 * rows * D * D * 6 + 8 * rows * rows * D, 8 * D * D + 20 * rows * D, heads * 2 * rows * rows
        ),
        name="attend",
    )(seq, prev, tok, gains, *[weights] * 4, cosine, sine)


def heads_back(
    skip, grad, wo_ref, q_ref, k_ref, v_ref, mixed_ref, lse_ref, cos_ref, sin_ref, gq_ref, gk_ref,
    gv_ref, dqt_ref, dk_ref, dv_ref,
):
    rows = grad.shape[0]
    cosine, sine = cos_ref[...], sin_ref[...]
    grad_mixed = contract(grad, wo_ref[...], ((1,), (1,))).astype(bf16)
    for at in range(0, GROUP, LANES):
        cols = slice(at, at + LANES)
        key, value = k_ref[:, cols], v_ref[:, cols]
        key_t = key.T
        products = grad_mixed[:, cols].astype(f32) * mixed_ref[:, cols].astype(f32)
        for j in range(LANES // HEAD_DIM):
            head = (at // HEAD_DIM + j) * 8
            keep = lax.broadcasted_iota(jnp.int32, key_t.shape, 0) // HEAD_DIM == j
            key_j = jnp.where(keep, key_t, jnp.zeros_like(key_t))
            for top in range(0, rows, BLOCK):
                block = slice(top, top + BLOCK)
                query = one_head(q_ref[block, cols], j)
                back = one_head(grad_mixed[block, cols], j)
                delta = row_of(
                    jnp.sum(one_head(products[block], j), axis=1, keepdims=True)
                )[0:1]
                lse = lse_ref[head : head + 1, block]
                for begin, end, less in ((0, rows, lse + skip), (rows, rows + top + BLOCK, lse)):
                    probs = jnp.exp(contract(key[begin:end], query, ((1,), (1,))) - less)
                    above = contract(value[begin:end], back, ((1,), (1,))) - delta
                    scores = (probs * above).astype(bf16)
                    grad_v = contract(probs.astype(bf16), back, ((1,), (0,)))
                    grad_k = contract(scores, query, ((1,), (0,)))
                    grad_q = contract(key_j[:, begin:end], scores, ((1,), (0,)))
                    if j == 0 and top == 0:
                        dv_ref[begin:end], dk_ref[begin:end] = grad_v, grad_k
                        if rows < end < 2 * rows:
                            rest = jnp.zeros((2 * rows - end, LANES), f32)
                            dv_ref[end:], dk_ref[end:] = rest, rest
                    else:
                        dv_ref[begin:end] += grad_v
                        dk_ref[begin:end] += grad_k
                    if j == 0 and begin == 0:
                        dqt_ref[:, block] = grad_q
                    else:
                        dqt_ref[:, block] += grad_q
        own_cos, own_sin = cosine[rows:], sine[rows:]
        gq_ref[:, cols] = (rope(dqt_ref[...].T, own_cos, -own_sin) * 0.125).astype(bf16)
        gk_ref[:, cols] = rope(dk_ref[...], cosine, -sine).astype(bf16)
        gv_ref[:, cols] = dv_ref[...].astype(bf16)


def group_sums(normed, gq, gk, gv, wq_ref, wk_ref, wv_ref):
    rows = gq.shape[0]
    one = contract(gk, wk_ref[...], ((1,), (1,))) + contract(gv, wv_ref[...], ((1,), (1,)))
    own = one[rows:] + contract(gq, wq_ref[...], ((1,), (1,)))
    parts = ((normed[:, rows:], gq), (normed, gk), (normed, gv))
    return one[:rows], own, [contract(a, b, ((1,), (0,))).astype(bf16) for a, b in parts]


def attend_back_body(
    seq_ref, grad_ref, wo_ref, wq_ref, wk_ref, wv_ref, q_ref, k_ref, v_ref, mixed_ref, lse_ref,
    normed_ref, all_ref, cos_ref, sin_ref, one_ref, d_ref, *scratch,
):
    step = pl.program_id(0)
    rows = grad_ref.shape[0]

    @pl.when(step < GROUPS - 1)
    def _():
        skip = jnp.where(seq_ref[0] > 0, 0.0, 1e30)
        heads_back(
            skip, grad_ref[...], wo_ref, q_ref, k_ref, v_ref, mixed_ref, lse_ref, cos_ref, sin_ref,
            *scratch,
        )
        gq, gk, gv = (ref[...] for ref in scratch[:3])
        early, own, parts = group_sums(normed_ref[...], gq, gk, gv, wq_ref, wk_ref, wv_ref)
        for i, part in enumerate(parts):
            d_ref[:, i * GROUP : (i + 1) * GROUP] = part

        @pl.when(step == 0)
        def _():
            one_ref[:rows], one_ref[rows:] = early, own

        @pl.when(step > 0)
        def _():
            one_ref[:rows] += early
            one_ref[rows:] += own

    @pl.when(step == GROUPS - 1)
    def _():
        d_ref[...] = contract(all_ref[...], grad_ref[...], ((0,), (0,))).astype(bf16)


def attend_back_last_body(
    seq_ref, grad_ref, wo_ref, wq_ref, wk_ref, wv_ref, q_ref, k_ref, v_ref, mixed_ref, lse_ref,
    normed_ref, prev_ref, tok_ref, two_ref, one_ref, cos_ref, sin_ref, early_ref,
    own_ref, d_ref, *scratch,
):
    rows = grad_ref.shape[0]
    skip = jnp.where(seq_ref[0] > 0, 0.0, 1e30)
    heads_back(
        skip, grad_ref[...], wo_ref, q_ref, k_ref, v_ref, mixed_ref, lse_ref, cos_ref, sin_ref,
        *scratch,
    )
    gq, gk, gv = (ref[...] for ref in scratch[:3])
    early, own, parts = group_sums(normed_ref[...], gq, gk, gv, wq_ref, wk_ref, wv_ref)
    for i, part in enumerate(parts):
        d_ref[:, i * GROUP : (i + 1) * GROUP] = part
    early, own = early + one_ref[:rows], own + one_ref[rows:]
    early_ref[...] = early.astype(bf16)
    own_ref[...] = own
    gain = jnp.sum(early * normal(prev_ref[...].astype(f32)), axis=0, keepdims=True)
    gain += jnp.sum(own * normal(tok_ref[...].astype(f32)), axis=0, keepdims=True)
    gain = jnp.broadcast_to(gain, (LANES, D)).T
    two = jnp.broadcast_to(two_ref[0:1], (LANES, D)).T
    lane = lax.broadcasted_iota(jnp.int32, (D, LANES), 1)
    small = jnp.where(lane == 0, gain, jnp.where(lane == 1, two, 0.0))
    d_ref[:, 3 * GROUP :] = small.astype(bf16)


def back_specs(rows, at):
    heads = D // HEAD_DIM // GROUPS
    across = lambda n: pl.BlockSpec((n, GROUP), lambda i: (0, at(i)))
    weight = lambda first: pl.BlockSpec((D, GROUP), lambda i: (0, first + at(i)))
    return [
        pl.BlockSpec(memory_space=pltpu.SMEM),
        whole((rows, D)),
        pl.BlockSpec((GROUP, D), lambda i: (at(i), 3)),
        weight(0),
        weight(GROUPS),
        weight(2 * GROUPS),
        across(rows),
        across(2 * rows),
        across(2 * rows),
        across(rows),
        pl.BlockSpec((8 * heads, rows), lambda i: (at(i), 0)),
        whole((D, 2 * rows)),
    ]


def back_scratch(rows):
    return [
        pltpu.VMEM((rows, GROUP), bf16),
        pltpu.VMEM((2 * rows, GROUP), bf16),
        pltpu.VMEM((2 * rows, GROUP), bf16),
        pltpu.VMEM((LANES, rows), f32),
        pltpu.VMEM((2 * rows, LANES), f32),
        pltpu.VMEM((2 * rows, LANES), f32),
    ]


def back_cost(rows, count):
    heads = D // HEAD_DIM // GROUPS
    flops = 2 * rows * D * GROUP * 11 + 20 * rows * rows * GROUP
    return cost(count * flops, count * 40 * rows * D, count * heads * 2 * rows * rows)


def attend_back(seq, grad, weights, q, k, v, mixed, lse, normed_t, cosine, sine):
    rows = grad.shape[0]
    return pl.pallas_call(
        attend_back_body,
        grid=(GROUPS,),
        in_specs=back_specs(rows, lambda i: jnp.minimum(i, GROUPS - 2))
        + [whole(v.shape) for v in (mixed, cosine, sine)],
        out_specs=[whole((2 * rows, D)), pl.BlockSpec((D, D), lambda i: (0, i))],
        out_shape=shapes(((2 * rows, D), f32), ((D, GROUPS * D), bf16)),
        scratch_shapes=back_scratch(rows),
        compiler_params=params(36),
        cost_estimate=back_cost(rows, GROUPS - 1),
        name="attend_back",
    )(seq, grad, *[weights] * 4, q, k, v, mixed, lse, normed_t, mixed, cosine, sine)


def attend_back_last(
    seq, grad, weights, q, k, v, mixed, lse, normed_t, prev, tok, two, one, cosine, sine
):
    rows = grad.shape[0]
    extra = (prev, tok, two, one, cosine, sine)
    return pl.pallas_call(
        attend_back_last_body,
        grid=(1,),
        in_specs=back_specs(rows, lambda i: GROUPS - 1) + [whole(v.shape) for v in extra],
        out_specs=[whole((rows, D)), whole((rows, D)), whole((D, 3 * GROUP + LANES))],
        out_shape=shapes(((rows, D), bf16), ((rows, D), f32), ((D, 3 * GROUP + LANES), bf16)),
        scratch_shapes=back_scratch(rows),
        compiler_params=params(36),
        cost_estimate=back_cost(rows, 1),
        name="attend_back_last",
    )(seq, grad, *[weights] * 4, q, k, v, mixed, lse, normed_t, *extra)


def middle_back_body(
    own_ref, other_ref, x_ref, y_ref, middle_ref, grad_ref, gains_ref, mid_ref, low_ref, gain_ref
):
    rows = own_ref[...] + other_ref[...].astype(f32) + x_ref[...].astype(f32)
    rows += y_ref[...].astype(f32)
    middle = middle_ref[...]
    r = lax.rsqrt(jnp.mean(middle * middle, axis=-1, keepdims=True) + epsilon)
    hat = middle * r
    gain = jnp.sum(rows * hat, axis=0, keepdims=True)
    gain_ref[...] = jnp.broadcast_to(gain, gain_ref.shape)
    q = rows * gains_ref[1:2]
    grad = q - hat * jnp.mean(q * hat, axis=-1, keepdims=True)
    grad = grad_ref[...].astype(f32) + r * grad
    mid_ref[...] = grad
    low_ref[...] = grad.astype(bf16)


def middle_back(own, other, from_x, from_y, middle, grad, gains):
    rows = middle.shape[0]
    block = pl.BlockSpec((rows, D), lambda i: (0, 0))
    return pl.pallas_call(
        middle_back_body,
        grid=(1,),
        in_specs=[block] * 6 + [whole(gains.shape)],
        out_specs=[block, block, whole((8, D))],
        out_shape=shapes(((rows, D), f32), ((rows, D), bf16), ((8, D), f32)),
        compiler_params=params(40),
        cost_estimate=cost(20 * rows * D, 22 * rows * D),
        name="middle_back",
    )(own, other, from_x, from_y, middle, grad, gains)


def output_body(own_ref, other_ref, x_ref, y_ref, middle_ref, out_ref, sums_ref):
    ffn = own_ref[...] + other_ref[...].astype(f32) + x_ref[...].astype(f32)
    ffn += y_ref[...].astype(f32)
    out = middle_ref[...] + ffn
    out_ref[...] = out.astype(bf16)
    for i, v in enumerate((ffn, out)):
        sums_ref[i : i + 1] = jnp.sum(v * v, axis=0, keepdims=True)


def output(own, other, from_x, from_y, middle):
    rows = middle.shape[0]
    block = pl.BlockSpec((rows, D), lambda i: (0, 0))
    second = pl.BlockSpec((rows, D), lambda i: (0, 1))
    return pl.pallas_call(
        output_body,
        grid=(1,),
        in_specs=[second, second, block, block, block],
        out_specs=[block, whole((8, D))],
        out_shape=shapes(((rows, D), bf16), ((8, D), f32)),
        compiler_params=params(40),
        cost_estimate=cost(8 * rows * D, 16 * rows * D),
        name="output",
    )(own, other, from_x, from_y, middle)


def tokens_back_body(tok_ref, own_ref, returned_ref, mid_ref, gains_ref, out_ref):
    tok = tok_ref[...].astype(f32)
    r = lax.rsqrt(jnp.mean(tok * tok, axis=-1, keepdims=True) + epsilon)
    hat = tok * r
    q = (own_ref[...] + returned_ref[...].astype(f32)) * gains_ref[0:1]
    grad = q - hat * jnp.mean(q * hat, axis=-1, keepdims=True)
    out_ref[...] = (mid_ref[...] + r * grad).astype(bf16)


def tokens_back(tok, own, returned, mid, gains):
    rows = tok.shape[0]
    block = whole((rows, D))
    return pl.pallas_call(
        tokens_back_body,
        grid=(1,),
        in_specs=[block] * 4 + [whole(gains.shape)],
        out_specs=block,
        out_shape=jax.ShapeDtypeStruct((rows, D), bf16),
        compiler_params=params(40),
        cost_estimate=cost(12 * rows * D, 14 * rows * D),
        name="tokens_back",
    )(tok, own, returned, mid, gains)


def gather_columns_body(sums_ref, qkv_ref, out_ref, tail_ref):
    for i in range(GROUPS):
        at = i * D if i < GROUPS - 1 else GROUPS * D
        for part in range(3):
            to = part * D + i * GROUP
            here = at + part * GROUP
            qkv_ref[:, to : to + GROUP] = sums_ref[:, here : here + GROUP]
    out_ref[...] = sums_ref[:, (GROUPS - 1) * D : GROUPS * D]
    tail_ref[...] = sums_ref[:, (GROUPS + 1) * D :]


def gather_columns(sums):
    rows = sums.shape[0]
    return pl.pallas_call(
        gather_columns_body,
        in_specs=[whole(sums.shape)],
        out_specs=[whole((rows, n)) for n in (3 * D, D, LANES)],
        out_shape=shapes(*(((rows, n), f32) for n in (3 * D, D, LANES))),
        grid=(1,),
        name="gather_columns",
    )(sums)


def columns_back_body(pair, in_ref, out_ref):
    count, _, width = out_ref.shape
    half = width // 2
    deep = half // (8 * pair)
    for e, g, x, c, z, y in itertools.product(
        range(count), range(2), range(2), range(2), range(deep), range(2)
    ):
        to = g * half + (((x * 2 + c) * deep + z) * 2 + y) * pair
        here = ((e * 2 + g) * deep + z) * pair
        piece = in_ref[(x * 2 + y) * 2 + c, :, here : here + pair]
        out_ref[e, :, to : to + pair] = piece.astype(f32)


def rope_tables(positions):
    halfdim = HEAD_DIM // 2
    inverse = 10000.0 ** (-2.0 * jnp.arange(halfdim, dtype=f32) / HEAD_DIM)
    angles = positions.astype(f32)[:, None] * inverse[None, :]
    cosine, sine = jnp.cos(angles), jnp.sin(angles)
    times = LANES // HEAD_DIM
    return (
        jnp.tile(jnp.concatenate([cosine, cosine], axis=1), (1, times)),
        jnp.tile(jnp.concatenate([-sine, sine], axis=1), (1, times)),
    )


SPLIT = (range(0, BRANCHES),)


def columns_out(w_ffn_in):
    depth = lax.axis_size("z")
    rows, count = w_ffn_in.shape[:2]
    pair = 2 * (FF // lax.axis_size(ALL))
    cut = w_ffn_in.reshape(rows, count, 2, 2, 2, depth // 2, 2, pair)
    return cut.transpose(3, 6, 4, 0, 1, 2, 5, 7).reshape(8, rows, -1)


def columns_back(v, count):
    depth = lax.axis_size("z")
    rows = v.shape[1]
    pair = 2 * (FF // lax.axis_size(ALL))
    if pair % LANES == 0:
        out = pl.pallas_call(
            functools.partial(columns_back_body, pair),
            in_specs=[whole(v.shape)],
            out_specs=whole((count, rows, 2 * FF)),
            out_shape=jax.ShapeDtypeStruct((count, rows, 2 * FF), f32),
            grid=(1,),
            name="columns_back",
        )(v)
        return out.transpose(1, 0, 2)
    v = v[:, :, : count * depth * pair].reshape(2, 2, 2, rows, count, 2, depth // 2, pair)
    return v.astype(f32).transpose(3, 4, 5, 0, 2, 6, 1, 7).reshape(rows, count, 2 * FF)


def exchange(cut):
    return lax.all_to_all(cut, PLANE, split_axis=0, concat_axis=0, tiled=True)


def columns_in(cut):
    wide = cut.shape[-1]
    cut = cut.reshape(2, -1, wide)
    return lax.all_gather(cut, "z", axis=1, tiled=True).reshape(D, wide)


def units_in(part):
    depth = lax.axis_size("z")
    count, own = part.shape[0], part.shape[1] // depth
    part = part.reshape(count, 2, depth // 2, own, D)
    core = own_bit("c")
    kept = lax.dynamic_index_in_dim(part, core, 1, keepdims=False)
    sent = lax.dynamic_index_in_dim(part, 1 - core, 1, keepdims=False)
    other = swap(sent, "c")
    both = jnp.where(core == 0, jnp.stack([kept, other], 2), jnp.stack([other, kept], 2))
    return both.reshape(count, depth * own, D)


def units_swap(d_hid, count):
    depth = lax.axis_size("z")
    d_hid = d_hid.reshape(count, depth // 2, 2, -1, D)
    core = own_bit("c")
    kept = lax.dynamic_index_in_dim(d_hid, core, 2, keepdims=False)
    return kept, swap(lax.dynamic_index_in_dim(d_hid, 1 - core, 2, keepdims=False), "c")


def units_out(kept, other):
    count, _, own, _ = kept.shape
    low = own_bit("c") == 0
    both = jnp.where(low, jnp.stack([kept, other], 1), jnp.stack([other, kept], 1))
    return both.reshape(count, -1, D)


def on_device(
    tokens, cotangent, routes, gain_one, w_qkv, w_attn_out, gain_two, router, w_ffn_in, w_ffn_out
):
    rows = tokens.shape[1]
    own_rows = w_qkv.shape[0]
    low_tokens = tokens.reshape(rows, D)
    low_grad = cotangent.reshape(rows, D)

    cut = exchange(columns_out(w_ffn_in))
    starts = [2 * FF // 8 * branches[0] for branches in SPLIT] + [cut.shape[-1]]
    w_out = lax.all_gather(w_ffn_out.transpose(1, 0, 2), "z", axis=1, tiled=True)
    w_in = [columns_in(cut[:, :, a:b]) for a, b in zip(starts, starts[1:])]
    before = lax.ppermute(low_tokens, "x", [(i, i + 1) for i in range(lax.axis_size("x") - 1)])
    seq_index = lax.axis_index("x")
    positions = (seq_index - 1) * rows + jnp.arange(2 * rows, dtype=jnp.int32)
    cosine, sine = rope_tables(positions)
    seq = seq_index.astype(jnp.int32).reshape(1)
    route = jnp.pad(routes.reshape(rows, TOP), ((0, 0), (0, LANES - TOP))).astype(bf16)
    grad_ext = jnp.concatenate([low_grad, route], axis=1)
    small = jnp.concatenate([gain_one[:, None], gain_two[:, None], router], axis=1)
    small = jnp.pad(small, ((0, 0), (0, LANES - small.shape[1])))
    weights = gather_rows(
        jnp.concatenate([w_qkv, w_attn_out, small], axis=1), (before,), (cosine, sine, grad_ext)
    )
    gains = weights[:, 4 * D : 4 * D + 2].astype(f32).T
    router_full = jnp.pad(
        weights[:, 4 * D + 2 : 4 * D + 2 + EXPERTS], ((0, 0), (0, LANES - EXPERTS))
    )
    grad_ext = after(grad_ext, weights)
    grad_x, grad_y = swap(grad_ext, "x"), swap(grad_ext, "y")

    results = attend(seq, before, low_tokens, gains, weights, cosine, sine)
    results = after(results, grad_x, grad_y)
    normed_one, q, k, v, mixed, lse, middle, normed_two, sums = results

    half = rows // 2

    def corner(across_x, across_y):
        return swap(across_x[:half], "y"), swap(across_y[half:], "x")

    def both_cores(u):
        return (u, swap(u, "c"))

    across_x, across_y = swap(normed_two, "x"), swap(normed_two, "y")
    grad_far = corner(grad_x, grad_y)
    normed_t = normed_one.T
    w_out = units_in(after(w_out, normed_two))
    x, g = {0: both_cores(normed_two)}, {0: both_cores(grad_ext)}
    x[0] = after(x[0], normed_t)
    below, gating, d_in, d_hid = {}, {}, [], []
    for branches, columns in zip(SPLIT, w_in):
        first, last = branches[0] == 0, branches[-1] == BRANCHES - 1
        columns = jnp.concatenate([columns, router_full], axis=1)
        units = w_out[branches[0] : branches[-1] + 1]
        if not first:
            columns = after(columns, d_in, d_hid)
        kept, top = (), {}

        def run(which, kept, *moves):
            part, gate, kept = ffn(
                which, 4, branches, x[which], g[which], columns, units, kept, gating.get(which)
            )
            part, moves = after((part, moves), part[0], moves) if moves else (part, ())
            gating[which] = gate or None
            return part, kept, moves

        if first:
            part, kept, moves = run(0, kept, across_x, across_y, *grad_far)
            top[0], (across_x, across_y, *grad_far) = part, moves
            far = corner(across_x, across_y)
            x[1], g[1] = both_cores(across_x), both_cores(grad_x)
            top[1], kept, (*far, other_part) = run(1, kept, *far, swap(top[0][1], "c"))
            x[3], g[3] = both_cores(jnp.concatenate(far)), both_cores(jnp.concatenate(grad_far))
            x[2], g[2] = both_cores(across_y), both_cores(grad_y)
        else:
            top[0], kept, _ = run(0, kept)
            top[1], kept, _ = run(1, kept)
        top[3], kept, _ = run(3, kept)
        if last:
            v3 = on_chip(top[3], below.get(3))
            moves = swap(v3[:half].astype(bf16), "x"), swap(v3[half:].astype(bf16), "y")
            top[2], kept, (upper, lower) = run(2, kept, *moves)
        else:
            top[2], kept, _ = run(2, kept)
        if first:
            x_all, g_all = kept[2:]
        rows_in_all = x_all
        if last:
            v1 = on_chip(top[1], below.get(1))
            v2 = on_chip(top[2], below.get(2))
            for_x = jnp.concatenate([v1[:half], v1[half:] + lower.astype(f32)]).astype(bf16)
            for_y = jnp.concatenate([v2[:half] + upper.astype(f32), v2[half:]]).astype(bf16)
            from_x, from_y = swap(for_x[:, :D], "x"), swap(for_y[:, :D], "y")
            rows_in_all = after(x_all, for_x, for_y)
        full = contract(rows_in_all, kept[1], ((0,), (0,))).astype(bf16)
        wide = columns.shape[1] - LANES
        if last:
            full, from_x, from_y = after((full, from_x, from_y), full, from_x, from_y)
        full = full if last else full[:, :wide]
        d_in.append(full)
        d_hid.append(contract(after(kept[0], full), g_all, ((0,), (0,))).astype(bf16))
        if not last:
            below = {which: on_chip(part, below.get(which)) for which, part in top.items()}
    own_part = top[0][0]
    grad_middle, grad_attn, gain_two_sums = middle_back(
        own_part, other_part, from_x, from_y, middle, low_grad, gains
    )
    grad_attn = after(grad_attn, d_hid)
    d_cols = [
        lax.psum_scatter(u.reshape(2, D // 2, -1), "z", scatter_dimension=1, tiled=True)
        for u in d_in
    ]
    d_hid = [units_swap(u, len(branches)) for u, branches in zip(d_hid, SPLIT)]

    for_x, for_y = after((for_x, for_y), grad_attn)
    moves = swap(for_x[:, D:], "x"), swap(for_y[:, D:], "y")
    one, part = attend_back(
        seq, grad_attn, weights, q, k, v, mixed, lse, normed_t, cosine, sine
    )
    one, part, (from_x, from_y), d_hid = after((one, part, moves, d_hid), one, moves, d_hid)
    first = Scatter(part, own_rows)
    moves = first.send()
    result, squares = output(own_part, other_part, from_x, from_y, middle)
    partial_sums = jnp.concatenate([jnp.sum(sums[:3], axis=1), jnp.sum(squares[:2], axis=1)])
    first.take(moves)
    d_hid = [units_out(*u) for u in after(d_hid, first.v)]
    d_cols = [u.reshape(8, own_rows, -1) for u in d_cols]
    moves = first.send()
    early, own, part = attend_back_last(
        seq, after(grad_attn, one, partial_sums, first.v), weights, q, k, v, mixed, lse, normed_t, before,
        low_tokens, gain_two_sums, one, cosine, sine
    )
    early, own, part, moves, d_cols = after(
        (early, own, part, moves, d_cols), own, moves, d_cols, d_hid
    )
    d_w_out = [lax.psum_scatter(u, "z", scatter_dimension=1, tiled=True) for u in d_hid]
    d_w_out = [u.transpose(1, 0, 2) for u in d_w_out]
    last = Scatter(part, own_rows, partial_sums)
    last_moves = last.send()
    first.take(moves)
    returned = lax.ppermute(early, "x", [(i + 1, i) for i in range(lax.axis_size("x") - 1)])
    last.take(last_moves)
    last_moves = last.send()
    last.take(last_moves)
    d_cols = [exchange(after(u, last.v)) for u in d_cols]
    last.v = jnp.concatenate([first.v, last.v], axis=-1)
    last_moves = last.send()
    d_router = jnp.sum(d_cols[-1][:, :, -LANES : EXPERTS - LANES].astype(f32), axis=0)
    d_cols = [columns_back(u, len(b)) for u, b in zip(d_cols, SPLIT)]
    last_moves, d_cols, d_router = after((last_moves, d_cols, d_router), last_moves)
    last.take(last_moves)
    last.finish()
    d_w_qkv, d_w_attn_out, tail = gather_columns(last.v)
    d_w_out = [u.astype(f32) for u in after(d_w_out, last.v)]
    grad_tokens = tokens_back(low_tokens, own, after(returned, last.v), grad_middle, gains)
    stats = jnp.sqrt(last.extra / (rows * lax.axis_size(ALL) * D))
    return (
        result.reshape(tokens.shape),
        grad_tokens.reshape(tokens.shape),
        tail[:, 0],
        d_w_qkv,
        d_w_attn_out,
        tail[:, 1],
        d_router,
        jnp.concatenate(d_cols, axis=1),
        jnp.concatenate(d_w_out, axis=1),
        stats,
    )


def solution(mesh):
    seq, fsdp = mesh.shape["seq"], mesh.shape["fsdp"]
    inner = Mesh(mesh.devices.reshape(seq, fsdp // 4, 2, 2), ALL)
    data = P(("z", "y", "c"), "x", None)
    weights = tuple(P(ALL, *(None,) * k) for k in (0, 1, 1, 0, 1, 2, 2))
    return jax.shard_map(
        on_device,
        mesh=inner,
        in_specs=(data, data, data) + weights,
        out_specs=(data, data) + weights + (P(),),
        check_vma=False,
    )
```
